32 devices in a mesh: seq: 8 (over z, x), tp: 4 (over y, core).
Axes of the slice: x: 2, y: 2, z: 4, core: 2. Of those that a mesh axis runs over, the one named last changes fastest.
Arguments:
- hidden_states: bfloat16 [2048, 3584], P('seq', 'tp'), may hold values from -6 to 6
- queries: bfloat16 [2048, 3584], P('seq', 'tp'), may hold values from -6 to 6
- key_weight: bfloat16 [3584, 512], P(None, 'tp'), may hold values from -0.09375 to 0.09375
- value_weight: bfloat16 [3584, 512], P(None, 'tp'), may hold values from -0.09375 to 0.09375
- output_weight: bfloat16 [3584, 3584], P('tp'), may hold values from -1.5 to 1.5
- prefix_keys: bfloat16 [2048, 512], P('seq', 'tp'), may hold values from -64 to 64
- prefix_values: bfloat16 [2048, 512], P('seq', 'tp'), may hold values from -6 to 6
- reads: int32 [8, 16], replicated, may hold values from 0 to 31, as said below
- out_grad: bfloat16 [2048, 3584], P('seq', 'tp'), may hold values from -6 to 6
Outputs:
- layer_output: bfloat16 [2048, 3584], P('seq', 'tp')
- prefix_key_grad: float32 [2048, 512], P('seq', 'tp')
- prefix_value_grad: float32 [2048, 512], P('seq', 'tp')
The draws below stay inside these ranges and needn't reach their ends.
Inputs may be any that keep to these rules, and one draw needn't show every extreme that they name: Entry l of a row is the row's node at depth l of a prefix tree, one of the blocks l * (2) to (l + 1) * 2 - 1; two rows that share a node share all its ancestors, and all rows share the root. Block b is held by index b // 4 of seq; every row names exactly 2 blocks of each index that it reads from.
All inputs are finite; a program needn't handle non-finite values.
Results may differ from the reference program's by a relative error of at most 0.0095.
Values may be sent and summed in bfloat16 or wider, within the bound.
No kernel may reach another device: no remote copies, remote signals or barrier semaphores. Data moves between devices by JAX's collectives and lax.ppermute only.
A program may use at most 128 MiB of HBM per device.

```python
import jax
import jax.numpy as jnp
from jax import lax

D = 3584
QH = 28
KVH = 4
HD = 128
TOK_DEV = 256
PBLK = 64
READS = 16
NBLK = 32
TOKENS = 2048
N_SEQ = 8
N_TP = 4


def draw_reads(key, part):
    per_level = NBLK // READS
    log_width = per_level.bit_length() - 1
    order = jax.random.permutation(jax.random.fold_in(key, 11), N_SEQ).astype(jnp.int32)
    levels = jnp.arange(READS, dtype=jnp.int32)
    branch = (2 ** jnp.minimum(levels, log_width)).astype(jnp.int32)
    node = order[:, None] * branch[None, :] // N_SEQ
    slot_noise = jax.random.randint(jax.random.fold_in(key, 23), (READS, per_level), 0, 1024) * per_level + jnp.arange(per_level, dtype=jnp.int32)[None, :]
    slot_order = jnp.argsort(slot_noise, axis=1).astype(jnp.int32)
    chosen = slot_order[levels[None, :], node]
    return (levels[None, :] * per_level + chosen).astype(jnp.int32)


def draw_prefix_keys(key, part):
    row_total = NBLK * PBLK
    col_total = KVH * HD
    base_values = jax.random.normal(jax.random.fold_in(key, 3), (row_total, col_total), jnp.float32)
    return jnp.clip(base_values, -6.0, 6.0).astype(jnp.bfloat16)


def block_levels(rng, dims, shards, least, high):
    loudness, own = 1.0, jax.random.fold_in(rng, 6)
    for dim, shards_of in shards:
        steps = jnp.exp(jax.random.uniform(jax.random.fold_in(own, dim), (shards_of,), jnp.float32, least / len(shards), high / len(shards)))
        loudness = loudness * jnp.repeat(steps, dims[dim] // shards_of).reshape([-1 if axis == dim else 1 for axis in range(len(dims))])
    return loudness


def normal_values(stream_key, dims, spread, limit, cuts=(), kind=jnp.bfloat16):
    entries = spread * jax.random.normal(stream_key, dims, jnp.float32)
    if cuts:
        entries = entries * block_levels(stream_key, dims, cuts, -0.22, 0.18)
    return jnp.clip(entries, -limit, limit).astype(kind)


def setup_inputs(seed: int = 0) -> dict:
    key_list = jax.random.split(jax.random.key(seed), 10)
    return {
        "hidden_states": normal_values(key_list[0], (TOKENS, D), 1.0, 6.0, ((0, 8), (1, 4))),
        "queries": normal_values(key_list[1], (TOKENS, QH * HD), 1.0, 6.0, ((0, 8), (1, 4))),
        "key_weight": normal_values(key_list[2], (D, KVH * HD), D ** -0.5, 0.09375, ((1, 4),)),
        "value_weight": normal_values(key_list[3], (D, KVH * HD), D ** -0.5, 0.09375, ((1, 4),)),
        "output_weight": normal_values(key_list[4], (QH * HD, D), (max(1, QH * HD // 256)) ** -0.5, 1.5, ((0, 4),)),
        "prefix_keys": draw_prefix_keys(jax.random.fold_in(key_list[9], 71), 0),
        "prefix_values": normal_values(key_list[6], (NBLK * PBLK, KVH * HD), 1.0, 6.0, ((0, 8), (1, 4))),
        "reads": draw_reads(jax.random.fold_in(key_list[9], 71), 0),
        "out_grad": normal_values(key_list[8], (TOKENS, D), 1.0, 6.0, ((0, 8), (1, 4))),
    }


def attend_block(queries, keys_prefix, values_prefix, keys_own, values_own, head_grads, scaling):
    length = queries.shape[0]
    scores_prefix = jnp.einsum('tkgd,pkd->kgtp', queries, keys_prefix) * scaling
    scores_own = jnp.einsum('tkgd,ukd->kgtu', queries, keys_own) * scaling
    causal = jnp.arange(length)[None, :] <= jnp.arange(length)[:, None]
    masked_own = jnp.where(causal[None, None], scores_own, -jnp.inf)
    peak_score = jnp.maximum(jnp.max(scores_prefix, axis=-1), jnp.max(masked_own, axis=-1))[..., None]
    exps_prefix = jnp.exp(scores_prefix - peak_score)
    exps_own = jnp.exp(masked_own - peak_score)
    denominator = (jnp.sum(exps_prefix, axis=-1) + jnp.sum(exps_own, axis=-1))[..., None]
    softmax_prefix = exps_prefix / denominator
    softmax_own = exps_own / denominator
    weights_prefix = lax.optimization_barrier(softmax_prefix.astype(jnp.bfloat16)).astype(jnp.float32)
    weights_own = lax.optimization_barrier(softmax_own.astype(jnp.bfloat16)).astype(jnp.float32)
    context = jnp.einsum('kgtp,pkd->tkgd', weights_prefix, values_prefix)
    context = context + jnp.einsum('kgtu,ukd->tkgd', weights_own, values_own)
    context = context.astype(jnp.bfloat16)
    slope_prefix = jnp.einsum('tkgd,pkd->kgtp', head_grads, values_prefix)
    slope_own = jnp.einsum('tkgd,ukd->kgtu', head_grads, values_own)
    row_delta = jnp.sum(softmax_prefix * slope_prefix, axis=-1) + jnp.sum(softmax_own * slope_own, axis=-1)
    score_grad = (softmax_prefix * (slope_prefix - row_delta[..., None])).astype(jnp.bfloat16)
    score_grad = lax.optimization_barrier(score_grad).astype(jnp.float32)
    value_grad = jnp.einsum('kgtp,tkgd->pkd', weights_prefix, head_grads)
    key_grad = jnp.einsum('kgtp,tkgd->pkd', score_grad, queries) * scaling
    return context, key_grad, value_grad


def reference(hidden_states, queries, key_weight, value_weight, output_weight, prefix_keys, prefix_values, reads, out_grad):
    scaling = HD ** -0.5
    groups = QH // KVH
    new_keys = jnp.dot(hidden_states, key_weight, preferred_element_type=jnp.float32).astype(jnp.bfloat16)
    new_values = jnp.dot(hidden_states, value_weight, preferred_element_type=jnp.float32).astype(jnp.bfloat16)
    context_grad = jnp.dot(out_grad, output_weight.T, preferred_element_type=jnp.float32).astype(jnp.bfloat16)
    cache_keys = prefix_keys.reshape(NBLK, PBLK, KVH, HD)
    cache_values = prefix_values.reshape(NBLK, PBLK, KVH, HD)

    def block_step(totals, inputs):
        key_total, value_total = totals
        block_queries, block_keys, block_values, block_grads, block_reads = inputs
        keys_prefix = cache_keys[block_reads].reshape(READS * PBLK, KVH, HD).astype(jnp.float32)
        values_prefix = cache_values[block_reads].reshape(READS * PBLK, KVH, HD).astype(jnp.float32)
        context, key_grad, value_grad = attend_block(
            block_queries.astype(jnp.float32), keys_prefix, values_prefix,
            block_keys.astype(jnp.float32), block_values.astype(jnp.float32),
            block_grads.astype(jnp.float32), scaling)
        key_total = key_total.at[block_reads].add(key_grad.reshape(READS, PBLK, KVH, HD))
        value_total = value_total.at[block_reads].add(value_grad.reshape(READS, PBLK, KVH, HD))
        return (key_total, value_total), context.reshape(TOK_DEV, QH * HD)

    inputs = (queries.reshape(N_SEQ, TOK_DEV, KVH, groups, HD),
              new_keys.reshape(N_SEQ, TOK_DEV, KVH, HD),
              new_values.reshape(N_SEQ, TOK_DEV, KVH, HD),
              context_grad.reshape(N_SEQ, TOK_DEV, KVH, groups, HD),
              reads)
    zeros_grad = jnp.zeros((NBLK, PBLK, KVH, HD), jnp.float32)
    (key_total, value_total), context_all = lax.scan(block_step, (zeros_grad, zeros_grad), inputs)
    context_all = context_all.reshape(TOKENS, QH * HD)
    head_share = QH * HD // N_TP
    layer_output = jnp.zeros((TOKENS, D), jnp.float32)
    for share_index in range(N_TP):
        share_out = jnp.dot(context_all[:, share_index * head_share:(share_index + 1) * head_share],
                            output_weight[share_index * head_share:(share_index + 1) * head_share],
                            preferred_element_type=jnp.float32).astype(jnp.bfloat16)
        layer_output = layer_output + lax.optimization_barrier(share_out).astype(jnp.float32)
    return (layer_output.astype(jnp.bfloat16),
            key_total.reshape(NBLK * PBLK, KVH * HD),
            value_total.reshape(NBLK * PBLK, KVH * HD))
```

```python
import functools

import jax
import jax.numpy as jnp
from jax import lax
from jax.experimental import pallas as pl
from jax.experimental.pallas import tpu as pltpu
from jax.sharding import PartitionSpec as P

HD = 128
PBLK = 64
LOG2E = 1.4426950408889634
F32 = jnp.float32
BF16 = jnp.bfloat16
VMEM = pl.BlockSpec(memory_space=pltpu.VMEM)
SMEM = pl.BlockSpec(memory_space=pltpu.SMEM)
ANY = pl.BlockSpec(memory_space=pl.ANY)


def dot(a, b, dims):
    return lax.dot_general(a, b, (dims, ((), ())), preferred_element_type=F32)


def cost(flops, nbytes, trans=0):
    return pl.CostEstimate(flops=int(flops), bytes_accessed=int(nbytes), transcendentals=int(trans))


def pick_kernel(n, cap, here, me_ref, reads_ref, keys_ref, values_ref, *outs):
    me = me_ref[0]
    for k in range(n):
        for r in range(cap):
            block = reads_ref[me ^ k, cap * me + r] - here * me
            rows = pl.ds(pl.multiple_of(block * PBLK, PBLK), PBLK)
            outs[k][r * PBLK:(r + 1) * PBLK, :HD] = keys_ref[rows, :]
            outs[k][r * PBLK:(r + 1) * PBLK, HD:] = values_ref[rows, :]


def place_kernel(n, cap, here, me_ref, reads_ref, *refs):
    parts, keys_ref, values_ref = refs[:n], refs[n], refs[n + 1]
    me = me_ref[0]
    keys_ref[...] = jnp.zeros_like(keys_ref)
    values_ref[...] = jnp.zeros_like(values_ref)
    for k in range(n):
        for r in range(cap):
            block = reads_ref[me ^ k, cap * me + r] - here * me
            rows = pl.ds(pl.multiple_of(block * PBLK, PBLK), PBLK)
            piece = parts[k][r * PBLK:(r + 1) * PBLK, :].astype(F32)
            keys_ref[rows, :] += piece[:, :HD]
            values_ref[rows, :] += piece[:, HD:]


def forward_kernel(n_tp, n_pre, scaling, me_ref, *refs):
    hidden = refs[:n_tp]
    wk_ref, wv_ref, q_ref = refs[n_tp:n_tp + 3]
    prefix = refs[n_tp + 3:n_tp + 3 + n_pre]
    ctx_ref, newv_ref, probs_hbm, k_all, vt_all, pbuf, sem = refs[n_tp + 3 + n_pre:]
    me = me_ref[0]
    length, width = hidden[0].shape
    heads = q_ref.shape[1] // HD
    new_k = jnp.zeros((length, HD), F32)
    new_v = jnp.zeros((length, HD), F32)
    for i in range(n_tp):
        rows = pl.ds(pl.multiple_of((me ^ i) * width, width), width)
        piece = hidden[i][...]
        new_k += dot(piece, wk_ref[rows, :], ((1,), (0,)))
        new_v += dot(piece, wv_ref[rows, :], ((1,), (0,)))
    at = 0
    for ref in prefix:
        size = ref.shape[0]
        k_all[at:at + size, :] = ref[:, :HD]
        vt_all[:, at:at + size] = ref[:, HD:].astype(F32).T.astype(BF16)
        at += size
    new_v = new_v.astype(BF16)
    newv_ref[...] = new_v
    k_all[at:, :] = new_k.astype(BF16)
    vt_all[:, at:] = new_v.astype(F32).T.astype(BF16)
    factor = scaling * LOG2E
    visible = lax.broadcasted_iota(jnp.int32, (length, length), 0) <= lax.broadcasted_iota(
        jnp.int32, (length, length), 1)

    def send(h):
        lanes = pl.ds(pl.multiple_of(h * length, length), length)
        return pltpu.make_async_copy(pbuf.at[:, lanes], probs_hbm.at[:, lanes], sem)

    def head(h, carry):
        cols = pl.ds(pl.multiple_of(h * HD, HD), HD)
        lanes = pl.ds(pl.multiple_of(h * length, length), length)
        qh = q_ref[:, cols]
        s_pre = dot(k_all[:at, :], qh, ((1,), (1,)))
        s_own = jnp.where(visible, dot(k_all[at:, :], qh, ((1,), (1,))), -jnp.inf)
        peak = jnp.maximum(jnp.max(s_pre, axis=0, keepdims=True), jnp.max(s_own, axis=0, keepdims=True))
        e_pre = jnp.exp2((s_pre - peak) * factor)
        e_own = jnp.exp2((s_own - peak) * factor)
        total = jnp.sum(e_pre, axis=0, keepdims=True) + jnp.sum(e_own, axis=0, keepdims=True)
        inverse = 1.0 / total
        pbuf[:at, lanes] = (e_pre * inverse).astype(BF16)
        pbuf[at:, lanes] = (e_own * inverse).astype(BF16)
        send(h).start()
        ctx_t = dot(vt_all[...], pbuf[:, lanes], ((1,), (0,)))
        ctx_ref[:, cols] = ctx_t.T.astype(BF16)
        return carry

    lax.fori_loop(0, heads, head, 0)
    pltpu.make_async_copy(pbuf, probs_hbm, sem).wait()


def project_kernel(n_tp, me_ref, ctx_ref, w_hbm, *refs):
    outs, w_buf, sems = refs[:n_tp], refs[n_tp], refs[n_tp + 1]
    me = me_ref[0]
    width = outs[0].shape[1]
    order = list(range(n_tp))[::-1]

    def fetch(i):
        cols = pl.ds(pl.multiple_of((me ^ i) * width, 128), width)
        return pltpu.make_async_copy(w_hbm.at[:, cols], w_buf.at[i], sems.at[i])

    for i in order:
        fetch(i).start()
    ctx = ctx_ref[...]
    for i in order:
        fetch(i).wait()
        outs[i][...] = dot(ctx, w_buf[i], ((1,), (0,))).astype(BF16)


def backward_kernel(n_tp, n_pre, scaling, me_ref, *refs):
    grads = refs[:n_tp]
    w_hbm, q_ref, newv_ref, probs_hbm = refs[n_tp:n_tp + 4]
    prefix = refs[n_tp + 4:n_tp + 4 + n_pre]
    outs = refs[n_tp + 4 + n_pre:n_tp + 4 + 2 * n_pre]
    w_buf, v_all, g_all, q_all, pbuf, dbuf, sems, psem = refs[n_tp + 4 + 2 * n_pre:]
    me = me_ref[0]
    length, width = grads[0].shape
    heads = q_ref.shape[1] // HD

    def fetch(i):
        cols = pl.ds(pl.multiple_of((me ^ i) * width, 128), width)
        return pltpu.make_async_copy(w_hbm.at[:, cols], w_buf.at[i], sems.at[i])

    for i in range(n_tp):
        fetch(i).start()
    fetch_probs = pltpu.make_async_copy(probs_hbm, pbuf, psem)
    fetch_probs.start()
    at = 0
    for ref in prefix:
        size = ref.shape[0]
        v_all[at:at + size, :] = ref[:, HD:]
        at += size
    v_all[at:, :] = newv_ref[...]
    for h in range(heads):
        q_all[h * length:(h + 1) * length, :] = q_ref[:, h * HD:(h + 1) * HD]
    total = jnp.zeros((length, heads * HD), F32)
    for i in range(n_tp):
        fetch(i).wait()
        total += dot(grads[i][...], w_buf[i], ((1,), (1,)))
    for h in range(heads):
        g_all[h * length:(h + 1) * length, :] = total[:, h * HD:(h + 1) * HD].astype(BF16)
    fetch_probs.wait()

    def head(h, carry):
        lanes = pl.ds(pl.multiple_of(h * length, length), length)
        gh = g_all[lanes, :]
        slope = dot(v_all[...], gh, ((1,), (1,)))
        probs = pbuf[:, lanes].astype(F32)
        delta = jnp.sum(probs * slope, axis=0, keepdims=True)
        dbuf[:, lanes] = (probs[:at] * (slope[:at] - delta)).astype(BF16)
        return carry

    lax.fori_loop(0, heads, head, 0)
    at = 0
    for out in outs:
        size = out.shape[0]
        out[:, :HD] = (dot(dbuf[at:at + size, :], q_all[...], ((1,), (0,))) * scaling).astype(out.dtype)
        out[:, HD:] = dot(pbuf[at:at + size, :], g_all[...], ((1,), (0,))).astype(out.dtype)
        at += size


def local(hidden_states, queries, key_weight, value_weight, output_weight, prefix_keys, prefix_values, reads, out_grad):
    length, width = hidden_states.shape
    scaling = HD ** (-0.5)
    heads = queries.shape[1] // HD
    n_tp = lax.axis_size("tp")
    n_seq = lax.axis_size("seq")
    here = prefix_keys.shape[0] // PBLK
    read_count = reads.shape[1]
    cap = max(1, read_count // n_seq)
    dense = cap * n_seq == read_count and n_seq & (n_seq - 1) == 0 and here * n_seq % read_count == 0
    me_tp = lax.axis_index("tp").astype(jnp.int32).reshape(1)
    me_seq = lax.axis_index("seq").astype(jnp.int32).reshape(1)
    n_rows = read_count * PBLK
    keys = n_rows + length

    def hop(x, axis, k):
        n = n_tp if axis == "tp" else n_seq
        return lax.ppermute(x, axis, [(i, i ^ k) for i in range(n)])

    def gather(x):
        far = hop(x, "tp", 2)
        near = hop(x, "tp", 1)
        return [x, near, far, hop(far, "tp", 1)]

    hidden = gather(hidden_states)
    grads = gather(out_grad)

    if dense:
        shape = jax.ShapeDtypeStruct((cap * PBLK, 2 * HD), BF16)
        picked = pl.pallas_call(
            functools.partial(pick_kernel, n_seq, cap, here),
            out_shape=[shape] * n_seq,
            in_specs=[SMEM, SMEM, VMEM, VMEM],
            out_specs=[VMEM] * n_seq,
            cost_estimate=cost(0, 2 ** 20),
            name="pick",
        )(me_seq, reads, prefix_keys, prefix_values)
        prefix = [picked[0]] + [hop(picked[k], "seq", k) for k in range(1, n_seq)]
    else:
        flat = PBLK * 2 * HD
        local_cache = jnp.concatenate([prefix_keys, prefix_values], axis=1).reshape(here, flat)
        own = me_seq[0]
        owners = reads // here
        slot_here = reads % here
        earlier = jnp.arange(read_count)[None, :] < jnp.arange(read_count)[:, None]
        ranks = jnp.sum((owners[:, :, None] == owners[:, None, :]) & earlier[None], axis=2)
        slots = jnp.arange(cap, dtype=jnp.int32)
        picker = jnp.sum(
            ((owners == own)[:, :, None, None]
             & (ranks[:, :, None, None] == slots[None, None, :, None])
             & (slot_here[:, :, None, None] == jnp.arange(here, dtype=jnp.int32))).astype(F32), axis=1)
        outgoing = jnp.einsum("dcb,bf->dcf", picker.astype(BF16), local_cache, preferred_element_type=F32).astype(BF16)
        incoming = lax.all_to_all(outgoing, "seq", split_axis=0, concat_axis=0, tiled=True)
        my_owner, my_rank = owners[own], ranks[own]
        fetched = jnp.take(incoming.reshape(n_seq * cap, flat), my_owner * cap + my_rank, axis=0)
        prefix = [fetched.reshape(n_rows, 2 * HD)]
    n_pre = len(prefix)

    ctx, new_v, probs = pl.pallas_call(
        functools.partial(forward_kernel, n_tp, n_pre, scaling),
        out_shape=[
            jax.ShapeDtypeStruct((length, heads * HD), BF16),
            jax.ShapeDtypeStruct((length, HD), BF16),
            jax.ShapeDtypeStruct((keys, heads * length), BF16),
        ],
        in_specs=[SMEM] + [VMEM] * (n_tp + 3 + n_pre),
        out_specs=[VMEM, VMEM, ANY],
        scratch_shapes=[
            pltpu.VMEM((keys, HD), BF16),
            pltpu.VMEM((HD, keys), BF16),
            pltpu.VMEM((keys, heads * length), BF16),
            pltpu.SemaphoreType.DMA,
        ],
        compiler_params=pltpu.CompilerParams(vmem_limit_bytes=40 * 2 ** 20),
        cost_estimate=cost(6e9, 1.2e7, 3e6),
        name="forward",
    )(me_tp, *hidden, key_weight, value_weight, queries, *prefix)

    shares = pl.pallas_call(
        functools.partial(project_kernel, n_tp),
        out_shape=[jax.ShapeDtypeStruct((length, width), BF16)] * n_tp,
        in_specs=[SMEM, VMEM, ANY],
        out_specs=[VMEM] * n_tp,
        scratch_shapes=[
            pltpu.VMEM((n_tp, heads * HD, width), BF16),
            pltpu.SemaphoreType.DMA((n_tp,)),
        ],
        compiler_params=pltpu.CompilerParams(vmem_limit_bytes=40 * 2 ** 20),
        cost_estimate=cost(2e9, 1e7),
        name="project",
    )(me_tp, ctx, output_weight)
    cross = shares[2].astype(F32) + hop(shares[3], "tp", 1).astype(F32)
    mine = shares[0].astype(F32) + hop(shares[1], "tp", 1).astype(F32)
    layer_output = (mine + hop(cross.astype(BF16), "tp", 2).astype(F32)).astype(BF16)

    grad_type = BF16 if dense else F32
    parts = pl.pallas_call(
        functools.partial(backward_kernel, n_tp, n_pre, scaling),
        out_shape=[jax.ShapeDtypeStruct(x.shape, grad_type) for x in prefix],
        in_specs=[SMEM] + [VMEM] * n_tp + [ANY, VMEM, VMEM, ANY] + [VMEM] * n_pre,
        out_specs=[VMEM] * n_pre,
        scratch_shapes=[
            pltpu.VMEM((n_tp, heads * HD, width), BF16),
            pltpu.VMEM((keys, HD), BF16),
            pltpu.VMEM((heads * length, HD), BF16),
            pltpu.VMEM((heads * length, HD), BF16),
            pltpu.VMEM((keys, heads * length), BF16),
            pltpu.VMEM((n_rows, heads * length), BF16),
            pltpu.SemaphoreType.DMA((n_tp,)),
            pltpu.SemaphoreType.DMA,
        ],
        compiler_params=pltpu.CompilerParams(vmem_limit_bytes=48 * 2 ** 20),
        cost_estimate=cost(8e9, 1.6e7),
        name="backward",
    )(me_tp, *grads, output_weight, queries, new_v, probs, *prefix)

    if dense:
        returned = [parts[0]] + [hop(parts[k], "seq", k) for k in range(1, n_seq)]
        shape = jax.ShapeDtypeStruct(prefix_keys.shape, F32)
        key_grad, value_grad = pl.pallas_call(
            functools.partial(place_kernel, n_seq, cap, here),
            out_shape=[shape] * 2,
            in_specs=[SMEM, SMEM] + [VMEM] * n_seq,
            out_specs=[VMEM] * 2,
            cost_estimate=cost(0, 2 ** 20),
            name="place",
        )(me_seq, reads, *returned)
    else:
        cache_grads = parts[0].reshape(read_count, flat)
        placer = ((my_owner[None, None, :] == jnp.arange(n_seq, dtype=jnp.int32)[:, None, None])
                  & (my_rank[None, None, :] == slots[None, :, None])).astype(F32)
        leaving = jnp.einsum("ocr,rf->ocf", placer, cache_grads, precision=lax.Precision.HIGHEST)
        back = lax.all_to_all(leaving.astype(BF16), "seq", split_axis=0, concat_axis=0, tiled=True).astype(F32)
        summed = jnp.einsum("dcb,dcf->bf", picker, back, precision=lax.Precision.HIGHEST).reshape(here * PBLK, 2 * HD)
        key_grad, value_grad = summed[:, :HD], summed[:, HD:]
    return layer_output, key_grad, value_grad


def solution(mesh):
    in_specs = (P("seq", "tp"), P("seq", "tp"), P(None, "tp"), P(None, "tp"), P("tp", None),
                P("seq", "tp"), P("seq", "tp"), P(), P("seq", "tp"))
    out_specs = (P("seq", "tp"), P("seq", "tp"), P("seq", "tp"))
    return jax.shard_map(local, mesh=mesh, in_specs=in_specs, out_specs=out_specs, check_vma=False)
```

```python
import functools

import jax
import jax.numpy as jnp
from jax import lax
from jax.experimental import pallas as pl
from jax.experimental.pallas import tpu as pltpu
from jax.sharding import PartitionSpec as P


HD = 128
PBLK = 64
LOG2E = 1.4426950408889634
F32 = jnp.float32
BF16 = jnp.bfloat16
VMEM = pl.BlockSpec(memory_space=pltpu.VMEM)
SMEM = pl.BlockSpec(memory_space=pltpu.SMEM)
ANY = pl.BlockSpec(memory_space=pl.ANY)


def dot(a, b, dims):
    return lax.dot_general(a, b, (dims, ((), ())), preferred_element_type=F32)


def cost(flops, nbytes, trans=0):
    return pl.CostEstimate(flops=int(flops), bytes_accessed=int(nbytes), transcendentals=int(trans))


def pick_kernel(n, cap, here, me_ref, reads_ref, keys_ref, values_ref, *outs):
    me = me_ref[0]
    for k in range(n):
        for r in range(cap):
            block = reads_ref[me ^ k, cap * me + r] - here * me
            rows = pl.ds(pl.multiple_of(block * PBLK, PBLK), PBLK)
            outs[k][r * PBLK:(r + 1) * PBLK, :HD] = keys_ref[rows, :]
            outs[k][r * PBLK:(r + 1) * PBLK, HD:] = values_ref[rows, :]


def place_kernel(n, cap, here, me_ref, reads_ref, *refs):
    parts, keys_ref, values_ref = refs[:n], refs[n], refs[n + 1]
    me = me_ref[0]
    keys_ref[...] = jnp.zeros_like(keys_ref)
    values_ref[...] = jnp.zeros_like(values_ref)
    for k in range(n):
        for r in range(cap):
            block = reads_ref[me ^ k, cap * me + r] - here * me
            rows = pl.ds(pl.multiple_of(block * PBLK, PBLK), PBLK)
            piece = parts[k][r * PBLK:(r + 1) * PBLK, :].astype(F32)
            keys_ref[rows, :] += piece[:, :HD]
            values_ref[rows, :] += piece[:, HD:]


def kv_kernel(n_tp, me_ref, *refs):
    hidden, (wk_ref, wv_ref, k_ref, v_ref) = refs[:n_tp], refs[n_tp:]
    me = me_ref[0]
    length, width = hidden[0].shape
    new_k = jnp.zeros((length, HD), F32)
    new_v = jnp.zeros((length, HD), F32)
    for i in range(n_tp):
        rows = pl.ds(pl.multiple_of((me ^ i) * width, width), width)
        piece = hidden[i][...]
        new_k += dot(piece, wk_ref[rows, :], ((1,), (0,)))
        new_v += dot(piece, wv_ref[rows, :], ((1,), (0,)))
    k_ref[...] = new_k.astype(BF16)
    v_ref[...] = new_v.astype(BF16)


def forward_kernel(n_pre, scaling, q_ref, newk_ref, newv_ref, *refs):
    prefix = refs[:n_pre]
    ctx_ref, exps_ref, row_ref, col_ref, vt_all, s_buf, sums = refs[n_pre:]
    length = q_ref.shape[0]
    heads = q_ref.shape[1] // HD
    factor = scaling * LOG2E
    chunks = []
    at = 0
    for ref in prefix:
        size = ref.shape[0]
        vt_all[:, at:at + size] = ref[:, HD:].astype(F32).T.astype(BF16)
        chunks.append((at, size, ref))
        at += size
    vt_all[:, at:] = newv_ref[...].astype(F32).T.astype(BF16)
    visible = lax.broadcasted_iota(jnp.int32, (length, length), 0) <= lax.broadcasted_iota(
        jnp.int32, (length, length), 1)
    sums[...] = jnp.ones_like(sums)

    def scores(h):
        qh = q_ref[:, h * HD:(h + 1) * HD]
        peak = None
        for start, size, ref in chunks:
            s = dot(ref[:, :HD], qh, ((1,), (1,)))
            s_buf[h % 2, start:start + size, :] = s
            top = jnp.max(s, axis=0, keepdims=True)
            peak = top if peak is None else jnp.maximum(peak, top)
        s = jnp.where(visible, dot(newk_ref[...], qh, ((1,), (1,))), -jnp.inf)
        s_buf[h % 2, at:, :] = s
        return jnp.maximum(peak, jnp.max(s, axis=0, keepdims=True))

    def finish(h, peak):
        lanes = slice(h * length, (h + 1) * length)
        total = jnp.zeros((1, length), F32)
        step = length // 2
        for start in range(0, at + length, step):
            e = jnp.exp2((s_buf[h % 2, start:start + step, :] - peak) * factor)
            total += jnp.sum(e, axis=0, keepdims=True)
            exps_ref[start:start + step, lanes] = e.astype(BF16)
        inverse = 1.0 / total
        sums[h:h + 1, :] = inverse
        ctx_t = dot(vt_all[...], exps_ref[:, lanes], ((1,), (0,))) * inverse
        ctx_ref[:, h * HD:(h + 1) * HD] = ctx_t.T.astype(BF16)

    peak = scores(0)
    for h in range(heads):
        later = scores(h + 1) if h + 1 < heads else None
        finish(h, peak)
        peak = later
    row_ref[...] = sums[:row_ref.shape[0], :]
    col_ref[...] = sums[...].T


def project_kernel(order, me_ref, ctx_ref, w_ref, *outs):
    me = me_ref[0]
    width = outs[0].shape[1]
    ctx = ctx_ref[...]
    for i, out in zip(order, outs):
        cols = pl.ds(pl.multiple_of((me ^ i) * width, 128), width)
        out[...] = dot(ctx, w_ref[:, cols], ((1,), (0,))).astype(BF16)


def near_kernel(order, me_ref, w_ref, *refs):
    grads, out = refs[:-1], refs[-1]
    me = me_ref[0]
    width = grads[0].shape[1]
    total = jnp.zeros(out.shape, F32)
    for i, grad in zip(order, grads):
        cols = pl.ds(pl.multiple_of((me ^ i) * width, 128), width)
        total += dot(grad[...], w_ref[:, cols], ((1,), (1,)))
    out[...] = total


def backward_kernel(order, n_pre, scaling, me_ref, w_ref, near_ref, q_ref, newv_ref, exps_ref, row_ref, col_ref, *refs):
    grads, prefix = refs[:len(order)], refs[len(order):len(order) + n_pre]
    outs = refs[len(order) + n_pre:len(order) + 2 * n_pre]
    g_all, q_all, dbuf, slopes = refs[len(order) + 2 * n_pre:]
    me = me_ref[0]
    length, width = grads[0].shape
    heads = q_ref.shape[1] // HD
    total = near_ref[...]
    for i, grad in zip(order, grads):
        cols = pl.ds(pl.multiple_of((me ^ i) * width, 128), width)
        total += dot(grad[...], w_ref[:, cols], ((1,), (1,)))
    for h in range(heads):
        rows = slice(h * length, (h + 1) * length)
        q_all[rows, :] = q_ref[:, h * HD:(h + 1) * HD]
        g_all[rows, :] = (total[:, h * HD:(h + 1) * HD] * col_ref[:, h:h + 1]).astype(BF16)
    n_rows = dbuf.shape[0]

    def slope(h):
        gh = g_all[h * length:(h + 1) * length, :]
        lanes = slice(h * length, (h + 1) * length)
        at = 0
        delta = None
        for ref in prefix:
            size = ref.shape[0]
            s = dot(ref[:, HD:], gh, ((1,), (1,)))
            slopes[h % 2, at:at + size, :] = s
            part = jnp.sum(exps_ref[at:at + size, lanes].astype(F32) * s, axis=0, keepdims=True)
            delta = part if delta is None else delta + part
            at += size
        s = dot(newv_ref[...], gh, ((1,), (1,)))
        delta += jnp.sum(exps_ref[at:, lanes].astype(F32) * s, axis=0, keepdims=True)
        return delta * row_ref[h:h + 1, :]

    def finish(h, delta):
        lanes = slice(h * length, (h + 1) * length)
        step = length // 2
        for start in range(0, n_rows, step):
            e = exps_ref[start:start + step, lanes].astype(F32)
            dbuf[start:start + step, lanes] = (e * (slopes[h % 2, start:start + step, :] - delta)).astype(BF16)

    delta = slope(0)
    for h in range(heads):
        later = slope(h + 1) if h + 1 < heads else None
        finish(h, delta)
        delta = later
    at = 0
    for out in outs:
        size = out.shape[0]
        out[:, HD:] = dot(exps_ref[at:at + size, :], g_all[...], ((1,), (0,))).astype(out.dtype)
        out[:, :HD] = (dot(dbuf[at:at + size, :], q_all[...], ((1,), (0,))) * scaling).astype(out.dtype)
        at += size


def local(hidden_states, queries, key_weight, value_weight, output_weight, prefix_keys, prefix_values, reads, out_grad):
    length, width = hidden_states.shape
    scaling = HD ** (-0.5)
    heads = queries.shape[1] // HD
    n_tp = lax.axis_size("tp")
    n_seq = lax.axis_size("seq")
    here = prefix_keys.shape[0] // PBLK
    read_count = reads.shape[1]
    cap = max(1, read_count // n_seq)
    dense = cap * n_seq == read_count and n_seq & (n_seq - 1) == 0 and here * n_seq % read_count == 0
    me_tp = lax.axis_index("tp").astype(jnp.int32).reshape(1)
    me_seq = lax.axis_index("seq").astype(jnp.int32).reshape(1)
    n_rows = read_count * PBLK
    keys = n_rows + length

    def hop(x, axis, k):
        n = n_tp if axis == "tp" else n_seq
        return lax.ppermute(x, axis, [(i, i ^ k) for i in range(n)])

    def grant(mib):
        return pltpu.CompilerParams(vmem_limit_bytes=mib * 2 ** 20)

    near_grad = hop(out_grad, "tp", 1)
    far_grad = hop(out_grad, "tp", 2)
    near_hidden = hop(hidden_states, "tp", 1)
    far_hidden = hop(hidden_states, "tp", 2)
    last_hidden = hop(far_hidden, "tp", 1)
    last_grad = hop(far_grad, "tp", 1)
    far_first = sorted(range(1, n_seq), key=lambda k: (-(k // 4), k & 1, -k))

    if dense:
        shape = jax.ShapeDtypeStruct((cap * PBLK, 2 * HD), BF16)
        picked = pl.pallas_call(
            functools.partial(pick_kernel, n_seq, cap, here),
            out_shape=[shape] * n_seq,
            in_specs=[SMEM, SMEM, VMEM, VMEM],
            out_specs=[VMEM] * n_seq,
            cost_estimate=cost(0, 2 ** 20),
            compiler_params=grant(4),
            name="pick",
        )(me_seq, reads, prefix_keys, prefix_values)
        moved = {k: hop(picked[k], "seq", k) for k in far_first}
        prefix = [picked[0]] + [moved[k] for k in range(1, n_seq)]
    else:
        flat = PBLK * 2 * HD
        local_cache = jnp.concatenate([prefix_keys, prefix_values], axis=1).reshape(here, flat)
        own = me_seq[0]
        owners = reads // here
        slot_here = reads % here
        earlier = jnp.arange(read_count)[None, :] < jnp.arange(read_count)[:, None]
        ranks = jnp.sum((owners[:, :, None] == owners[:, None, :]) & earlier[None], axis=2)
        slots = jnp.arange(cap, dtype=jnp.int32)
        picker = jnp.sum(
            ((owners == own)[:, :, None, None]
             & (ranks[:, :, None, None] == slots[None, None, :, None])
             & (slot_here[:, :, None, None] == jnp.arange(here, dtype=jnp.int32))).astype(F32), axis=1)
        outgoing = jnp.einsum("dcb,bf->dcf", picker.astype(BF16), local_cache, preferred_element_type=F32).astype(BF16)
        incoming = lax.all_to_all(outgoing, "seq", split_axis=0, concat_axis=0, tiled=True)
        my_owner, my_rank = owners[own], ranks[own]
        fetched = jnp.take(incoming.reshape(n_seq * cap, flat), my_owner * cap + my_rank, axis=0)
        prefix = [fetched.reshape(n_rows, 2 * HD)]
    n_pre = len(prefix)

    new_kv = jax.ShapeDtypeStruct((length, HD), BF16)
    new_k, new_v = pl.pallas_call(
        functools.partial(kv_kernel, n_tp),
        out_shape=[new_kv] * 2,
        in_specs=[SMEM] + [VMEM] * (n_tp + 2),
        out_specs=[VMEM] * 2,
        compiler_params=grant(8),
        cost_estimate=cost(5e8, 4e6),
        name="kv",
    )(me_tp, hidden_states, near_hidden, far_hidden, last_hidden, key_weight, value_weight)

    near = pl.pallas_call(
        functools.partial(near_kernel, (0, 1)),
        out_shape=jax.ShapeDtypeStruct((length, heads * HD), F32),
        in_specs=[SMEM] + [VMEM] * 3,
        out_specs=VMEM,
        compiler_params=grant(16),
        cost_estimate=cost(1e9, 8e6),
        name="near",
    )(me_tp, output_weight, out_grad, near_grad)

    ctx, exps, row, col = pl.pallas_call(
        functools.partial(forward_kernel, n_pre, scaling),
        out_shape=[
            jax.ShapeDtypeStruct((length, heads * HD), BF16),
            jax.ShapeDtypeStruct((keys, heads * length), BF16),
            jax.ShapeDtypeStruct((heads + (-heads) % 8, length), F32),
            jax.ShapeDtypeStruct((length, HD), F32),
        ],
        in_specs=[VMEM] * (3 + n_pre),
        out_specs=[VMEM] * 4,
        scratch_shapes=[
            pltpu.VMEM((HD, keys), BF16),
            pltpu.VMEM((2, keys, length), F32),
            pltpu.VMEM((HD, length), F32),
        ],
        compiler_params=grant(20),
        cost_estimate=cost(5e9, 1e7, 3e6),
        name="forward",
    )(queries, new_k, new_v, *prefix)

    def project(order):
        return pl.pallas_call(
            functools.partial(project_kernel, order),
            out_shape=[jax.ShapeDtypeStruct((length, width), BF16)] * len(order),
            in_specs=[SMEM, VMEM, VMEM],
            out_specs=[VMEM] * len(order),
            compiler_params=grant(16),
            cost_estimate=cost(5e8 * len(order), 2e6 * len(order)),
        )(me_tp, ctx, output_weight)

    share3, = project((3,))
    near3 = hop(share3, "tp", 1)
    share2, share1, share0 = project((2, 1, 0))
    near1 = hop(share1, "tp", 1)
    cross = (share2.astype(F32) + near3.astype(F32)).astype(BF16)
    across = hop(cross, "tp", 2)
    layer_output = (share0.astype(F32) + near1.astype(F32) + across.astype(F32)).astype(BF16)

    grad_type = BF16 if dense else F32
    parts = pl.pallas_call(
        functools.partial(backward_kernel, (2, 3), n_pre, scaling),
        out_shape=[jax.ShapeDtypeStruct(x.shape, grad_type) for x in prefix],
        in_specs=[SMEM] + [VMEM] * (9 + n_pre),
        out_specs=[VMEM] * n_pre,
        scratch_shapes=[
            pltpu.VMEM((heads * length, HD), BF16),
            pltpu.VMEM((heads * length, HD), BF16),
            pltpu.VMEM((n_rows, heads * length), BF16),
            pltpu.VMEM((2, n_rows, length), F32),
        ],
        compiler_params=grant(32),
        cost_estimate=cost(7e9, 1e7),
        name="backward",
    )(me_tp, output_weight, near, queries, new_v, exps, row, col, far_grad, last_grad, *prefix)

    if dense:
        back = {k: hop(parts[k], "seq", k) for k in far_first}
        returned = [parts[0]] + [back[k] for k in range(1, n_seq)]
        shape = jax.ShapeDtypeStruct(prefix_keys.shape, F32)
        key_grad, value_grad = pl.pallas_call(
            functools.partial(place_kernel, n_seq, cap, here),
            out_shape=[shape] * 2,
            in_specs=[SMEM, SMEM] + [VMEM] * n_seq,
            out_specs=[VMEM] * 2,
            cost_estimate=cost(0, 2 ** 20),
            compiler_params=grant(4),
            name="place",
        )(me_seq, reads, *returned)
    else:
        cache_grads = parts[0].reshape(read_count, flat)
        placer = ((my_owner[None, None, :] == jnp.arange(n_seq, dtype=jnp.int32)[:, None, None])
                  & (my_rank[None, None, :] == slots[None, :, None])).astype(F32)
        leaving = jnp.einsum("ocr,rf->ocf", placer, cache_grads, precision=lax.Precision.HIGHEST)
        back = lax.all_to_all(leaving.astype(BF16), "seq", split_axis=0, concat_axis=0, tiled=True).astype(F32)
        summed = jnp.einsum("dcb,dcf->bf", picker, back, precision=lax.Precision.HIGHEST).reshape(here * PBLK, 2 * HD)
        key_grad, value_grad = summed[:, :HD], summed[:, HD:]
    return layer_output, key_grad, value_grad


def solution(mesh):
    in_specs = (P("seq", "tp"), P("seq", "tp"), P(None, "tp"), P(None, "tp"), P("tp", None),
                P("seq", "tp"), P("seq", "tp"), P(), P("seq", "tp"))
    out_specs = (P("seq", "tp"), P("seq", "tp"), P("seq", "tp"))
    return jax.shard_map(local, mesh=mesh, in_specs=in_specs, out_specs=out_specs, check_vma=False)
```

```python
import functools

import jax
import jax.numpy as jnp
from jax import lax
from jax.experimental import pallas as pl
from jax.experimental.pallas import tpu as pltpu
from jax.sharding import PartitionSpec as P


HD = 128
PBLK = 64
LOG2E = 1.4426950408889634
F32 = jnp.float32
BF16 = jnp.bfloat16
VMEM = pl.BlockSpec(memory_space=pltpu.VMEM)
SMEM = pl.BlockSpec(memory_space=pltpu.SMEM)
HBM = pl.BlockSpec(memory_space=pltpu.HBM)


def dot(a, b, dims):
    return lax.dot_general(a, b, (dims, ((), ())), preferred_element_type=F32)


def hbm(x):
    return pltpu.with_memory_space_constraint(x, pltpu.HBM)


def cost(flops, nbytes, trans=0):
    return pl.CostEstimate(flops=int(flops), bytes_accessed=int(nbytes), transcendentals=int(trans))


def pick_kernel(n, cap, here, me_ref, reads_hbm, keys_hbm, values_hbm, *refs):
    outs, reads_ref, read_sem, sem = refs[:n], refs[n], refs[n + 1], refs[n + 2]
    me = me_ref[0]
    fetch = pltpu.make_async_copy(reads_hbm, reads_ref, read_sem)
    fetch.start()
    fetch.wait()
    copies = []
    for k in range(n):
        for r in range(cap):
            block = reads_ref[me ^ k, cap * me + r] - here * me
            rows = pl.ds(pl.multiple_of(block * PBLK, PBLK), PBLK)
            at = pl.ds(r * PBLK, PBLK)
            copies.append(pltpu.make_async_copy(keys_hbm.at[rows], outs[k].at[at, pl.ds(0, HD)], sem))
            copies.append(pltpu.make_async_copy(values_hbm.at[rows], outs[k].at[at, pl.ds(HD, HD)], sem))
    for copy in copies:
        copy.start()
    for copy in copies:
        copy.wait()


def place_kernel(n, cap, here, me_ref, reads_ref, *refs):
    parts, keys_ref, values_ref = refs[:n], refs[n], refs[n + 1]
    me = me_ref[0]
    keys_ref[...] = jnp.zeros_like(keys_ref)
    values_ref[...] = jnp.zeros_like(values_ref)
    for k in range(n):
        for r in range(cap):
            block = reads_ref[me ^ k, cap * me + r] - here * me
            rows = pl.ds(pl.multiple_of(block * PBLK, PBLK), PBLK)
            piece = parts[k][r * PBLK:(r + 1) * PBLK, :].astype(F32)
            keys_ref[rows, :] += piece[:, :HD]
            values_ref[rows, :] += piece[:, HD:]


def kv_kernel(n_tp, me_ref, own_hbm, *refs):
    hidden, (wk_hbm, wv_hbm, k_ref, v_ref, own_ref, wk_ref, wv_ref, sems, own_sem) = refs[:n_tp - 1], refs[n_tp - 1:]
    me = me_ref[0]
    length, width = own_ref.shape

    def fetch(i):
        rows = pl.ds(pl.multiple_of((me ^ i) * width, width), width)
        return (pltpu.make_async_copy(wk_hbm.at[rows], wk_ref.at[i], sems.at[0, i]),
                pltpu.make_async_copy(wv_hbm.at[rows], wv_ref.at[i], sems.at[1, i]))

    order = list(range(1, n_tp)) + [0]
    for i in order:
        for copy in fetch(i):
            copy.start()
    own = pltpu.make_async_copy(own_hbm, own_ref, own_sem)
    own.start()
    new_k = jnp.zeros((length, HD), F32)
    new_v = jnp.zeros((length, HD), F32)
    for i in order:
        for copy in fetch(i):
            copy.wait()
        if i == 0:
            own.wait()
        piece = hidden[i - 1][...] if i else own_ref[...]
        new_k += dot(piece, wk_ref[i], ((1,), (0,)))
        new_v += dot(piece, wv_ref[i], ((1,), (0,)))
    k_ref[...] = new_k.astype(BF16)
    v_ref[...] = new_v.astype(BF16)


def forward_kernel(n_pre, scaling, q_ref, newk_ref, newv_ref, *refs):
    prefix = refs[:n_pre]
    ctx_ref, exps_ref, row_ref, col_ref, vt_all, s_buf, sums = refs[n_pre:]
    length = q_ref.shape[0]
    heads = q_ref.shape[1] // HD
    factor = scaling * LOG2E
    chunks = []
    at = 0
    for ref in prefix:
        size = ref.shape[0]
        vt_all[:, at:at + size] = ref[:, HD:].astype(F32).T.astype(BF16)
        chunks.append((at, size, ref))
        at += size
    vt_all[:, at:] = newv_ref[...].astype(F32).T.astype(BF16)
    visible = lax.broadcasted_iota(jnp.int32, (length, length), 0) <= lax.broadcasted_iota(
        jnp.int32, (length, length), 1)
    sums[...] = jnp.ones_like(sums)

    def scores(h):
        qh = q_ref[:, h * HD:(h + 1) * HD]
        peak = None
        for start, size, ref in chunks:
            s = dot(ref[:, :HD], qh, ((1,), (1,)))
            s_buf[h % 2, start:start + size, :] = s
            top = jnp.max(s, axis=0, keepdims=True)
            peak = top if peak is None else jnp.maximum(peak, top)
        s = jnp.where(visible, dot(newk_ref[...], qh, ((1,), (1,))), -jnp.inf)
        s_buf[h % 2, at:, :] = s
        return jnp.maximum(peak, jnp.max(s, axis=0, keepdims=True))

    def finish(h, peak):
        lanes = slice(h * length, (h + 1) * length)
        total = jnp.zeros((1, length), F32)
        step = length // 2
        for start in range(0, at + length, step):
            e = jnp.exp2((s_buf[h % 2, start:start + step, :] - peak) * factor)
            total += jnp.sum(e, axis=0, keepdims=True)
            exps_ref[start:start + step, lanes] = e.astype(BF16)
        inverse = 1.0 / total
        sums[h:h + 1, :] = inverse
        ctx_t = dot(vt_all[...], exps_ref[:, lanes], ((1,), (0,))) * inverse
        ctx_ref[:, h * HD:(h + 1) * HD] = ctx_t.T.astype(BF16)

    peak = scores(0)
    for h in range(heads):
        later = scores(h + 1) if h + 1 < heads else None
        finish(h, peak)
        peak = later
    row_ref[...] = sums[:row_ref.shape[0], :]
    col_ref[...] = sums[...].T


def project_kernel(order, me_ref, ctx_ref, w_ref, *outs):
    me = me_ref[0]
    width = outs[0].shape[1]
    ctx = ctx_ref[...]
    for i, out in zip(order, outs):
        cols = pl.ds(pl.multiple_of((me ^ i) * width, 128), width)
        out[...] = dot(ctx, w_ref[:, cols], ((1,), (0,))).astype(BF16)


def near_kernel(me_ref, w_hbm, own_hbm, near_ref, out, w_buf, own_ref, sems, own_sem):
    me = me_ref[0]
    width = near_ref.shape[1]

    def fetch(i):
        cols = pl.ds(pl.multiple_of((me ^ i) * width, 128), width)
        return pltpu.make_async_copy(w_hbm.at[:, cols], w_buf.at[i], sems.at[i])

    fetch(1).start()
    fetch(0).start()
    own = pltpu.make_async_copy(own_hbm, own_ref, own_sem)
    own.start()
    fetch(1).wait()
    total = dot(near_ref[...], w_buf[1], ((1,), (1,)))
    fetch(0).wait()
    own.wait()
    out[...] = total + dot(own_ref[...], w_buf[0], ((1,), (1,)))


def backward_kernel(order, n_pre, scaling, me_ref, w_ref, near_ref, q_ref, newv_ref, exps_ref, row_ref, col_ref, *refs):
    grads, prefix = refs[:len(order)], refs[len(order):len(order) + n_pre]
    outs = refs[len(order) + n_pre:len(order) + 2 * n_pre]
    g_all, q_all, dbuf, slopes = refs[len(order) + 2 * n_pre:]
    me = me_ref[0]
    length, width = grads[0].shape
    heads = q_ref.shape[1] // HD
    total = near_ref[...]
    for i, grad in zip(order, grads):
        cols = pl.ds(pl.multiple_of((me ^ i) * width, 128), width)
        total += dot(grad[...], w_ref[:, cols], ((1,), (1,)))
    for h in range(heads):
        rows = slice(h * length, (h + 1) * length)
        q_all[rows, :] = q_ref[:, h * HD:(h + 1) * HD]
        g_all[rows, :] = (total[:, h * HD:(h + 1) * HD] * col_ref[:, h:h + 1]).astype(BF16)
    n_rows = dbuf.shape[0]

    def slope(h):
        gh = g_all[h * length:(h + 1) * length, :]
        lanes = slice(h * length, (h + 1) * length)
        at = 0
        delta = None
        for ref in prefix:
            size = ref.shape[0]
            s = dot(ref[:, HD:], gh, ((1,), (1,)))
            slopes[h % 2, at:at + size, :] = s
            part = jnp.sum(exps_ref[at:at + size, lanes].astype(F32) * s, axis=0, keepdims=True)
            delta = part if delta is None else delta + part
            at += size
        s = dot(newv_ref[...], gh, ((1,), (1,)))
        delta += jnp.sum(exps_ref[at:, lanes].astype(F32) * s, axis=0, keepdims=True)
        return delta * row_ref[h:h + 1, :]

    def finish(h, delta):
        lanes = slice(h * length, (h + 1) * length)
        step = length // 2
        for start in range(0, n_rows, step):
            e = exps_ref[start:start + step, lanes].astype(F32)
            dbuf[start:start + step, lanes] = (e * (slopes[h % 2, start:start + step, :] - delta)).astype(BF16)

    delta = slope(0)
    for h in range(heads):
        later = slope(h + 1) if h + 1 < heads else None
        finish(h, delta)
        delta = later
    at = 0
    for out in outs:
        size = out.shape[0]
        out[:, HD:] = dot(exps_ref[at:at + size, :], g_all[...], ((1,), (0,))).astype(out.dtype)
        out[:, :HD] = (dot(dbuf[at:at + size, :], q_all[...], ((1,), (0,))) * scaling).astype(out.dtype)
        at += size


def local(hidden_states, queries, key_weight, value_weight, output_weight, prefix_keys, prefix_values, reads, out_grad):
    length, width = hidden_states.shape
    scaling = HD ** (-0.5)
    heads = queries.shape[1] // HD
    n_tp = lax.axis_size("tp")
    n_seq = lax.axis_size("seq")
    here = prefix_keys.shape[0] // PBLK
    read_count = reads.shape[1]
    cap = max(1, read_count // n_seq)
    dense = cap * n_seq == read_count and n_seq & (n_seq - 1) == 0 and here * n_seq % read_count == 0
    me_tp = lax.axis_index("tp").astype(jnp.int32).reshape(1)
    me_seq = lax.axis_index("seq").astype(jnp.int32).reshape(1)
    n_rows = read_count * PBLK
    keys = n_rows + length

    def hop(x, axis, k):
        n = n_tp if axis == "tp" else n_seq
        return lax.ppermute(x, axis, [(i, i ^ k) for i in range(n)])

    def grant(mib):
        return pltpu.CompilerParams(vmem_limit_bytes=mib * 2 ** 20)

    near_grad = hop(out_grad, "tp", 1)
    far_grad = hop(out_grad, "tp", 2)
    near_hidden = hop(hidden_states, "tp", 1)
    far_hidden = hop(hidden_states, "tp", 2)
    last_hidden = hop(far_hidden, "tp", 1)
    last_grad = hop(far_grad, "tp", 1)
    far_first = sorted(range(1, n_seq), key=lambda k: (-(k // 4), k & 1, -k))

    if dense:
        shape = jax.ShapeDtypeStruct((cap * PBLK, 2 * HD), BF16)
        picked = pl.pallas_call(
            functools.partial(pick_kernel, n_seq, cap, here),
            out_shape=[shape] * n_seq,
            in_specs=[SMEM, HBM, HBM, HBM],
            out_specs=[VMEM] * n_seq,
            scratch_shapes=[pltpu.SMEM(reads.shape, jnp.int32), pltpu.SemaphoreType.DMA, pltpu.SemaphoreType.DMA],
            cost_estimate=cost(0, 2 ** 20),
            compiler_params=grant(4),
            name="pick",
        )(me_seq, hbm(reads), hbm(prefix_keys), hbm(prefix_values))
        moved = {k: hop(picked[k], "seq", k) for k in far_first}
        prefix = [picked[0]] + [moved[k] for k in range(1, n_seq)]
    else:
        flat = PBLK * 2 * HD
        local_cache = jnp.concatenate([prefix_keys, prefix_values], axis=1).reshape(here, flat)
        own = me_seq[0]
        owners = reads // here
        slot_here = reads % here
        earlier = jnp.arange(read_count)[None, :] < jnp.arange(read_count)[:, None]
        ranks = jnp.sum((owners[:, :, None] == owners[:, None, :]) & earlier[None], axis=2)
        slots = jnp.arange(cap, dtype=jnp.int32)
        picker = jnp.sum(
            ((owners == own)[:, :, None, None]
             & (ranks[:, :, None, None] == slots[None, None, :, None])
             & (slot_here[:, :, None, None] == jnp.arange(here, dtype=jnp.int32))).astype(F32), axis=1)
        outgoing = jnp.einsum("dcb,bf->dcf", picker.astype(BF16), local_cache, preferred_element_type=F32).astype(BF16)
        incoming = lax.all_to_all(outgoing, "seq", split_axis=0, concat_axis=0, tiled=True)
        my_owner, my_rank = owners[own], ranks[own]
        fetched = jnp.take(incoming.reshape(n_seq * cap, flat), my_owner * cap + my_rank, axis=0)
        prefix = [fetched.reshape(n_rows, 2 * HD)]
    n_pre = len(prefix)

    new_kv = jax.ShapeDtypeStruct((length, HD), BF16)
    new_k, new_v = pl.pallas_call(
        functools.partial(kv_kernel, n_tp),
        out_shape=[new_kv] * 2,
        in_specs=[SMEM, HBM] + [VMEM] * (n_tp - 1) + [HBM] * 2,
        out_specs=[VMEM] * 2,
        scratch_shapes=[
            pltpu.VMEM((length, width), BF16),
            pltpu.VMEM((n_tp, width, HD), BF16),
            pltpu.VMEM((n_tp, width, HD), BF16),
            pltpu.SemaphoreType.DMA((2, n_tp)),
            pltpu.SemaphoreType.DMA,
        ],
        compiler_params=grant(8),
        cost_estimate=cost(5e8, 4e6),
        name="kv",
    )(me_tp, hbm(hidden_states), near_hidden, far_hidden, last_hidden, hbm(key_weight), hbm(value_weight))

    near = pl.pallas_call(
        near_kernel,
        out_shape=jax.ShapeDtypeStruct((length, heads * HD), F32),
        in_specs=[SMEM, HBM, HBM, VMEM],
        out_specs=VMEM,
        scratch_shapes=[
            pltpu.VMEM((2, heads * HD, width), BF16),
            pltpu.VMEM((length, width), BF16),
            pltpu.SemaphoreType.DMA((2,)),
            pltpu.SemaphoreType.DMA,
        ],
        compiler_params=grant(16),
        cost_estimate=cost(1e9, 8e6),
        name="near",
    )(me_tp, hbm(output_weight), hbm(out_grad), near_grad)

    ctx, exps, row, col = pl.pallas_call(
        functools.partial(forward_kernel, n_pre, scaling),
        out_shape=[
            jax.ShapeDtypeStruct((length, heads * HD), BF16),
            jax.ShapeDtypeStruct((keys, heads * length), BF16),
            jax.ShapeDtypeStruct((heads + (-heads) % 8, length), F32),
            jax.ShapeDtypeStruct((length, HD), F32),
        ],
        in_specs=[VMEM] * (3 + n_pre),
        out_specs=[VMEM] * 4,
        scratch_shapes=[
            pltpu.VMEM((HD, keys), BF16),
            pltpu.VMEM((2, keys, length), F32),
            pltpu.VMEM((HD, length), F32),
        ],
        compiler_params=grant(20),
        cost_estimate=cost(5e9, 1e7, 3e6),
        name="forward",
    )(queries, new_k, new_v, *prefix)

    def project(order):
        return pl.pallas_call(
            functools.partial(project_kernel, order),
            out_shape=[jax.ShapeDtypeStruct((length, width), BF16)] * len(order),
            in_specs=[SMEM, VMEM, VMEM],
            out_specs=[VMEM] * len(order),
            compiler_params=grant(16),
            cost_estimate=cost(5e8 * len(order), 2e6 * len(order)),
        )(me_tp, ctx, output_weight)

    share3, = project((3,))
    near3 = hop(share3, "tp", 1)
    share2, share1, share0 = project((2, 1, 0))
    near1 = hop(share1, "tp", 1)
    cross = (share2.astype(F32) + near3.astype(F32)).astype(BF16)
    across = hop(cross, "tp", 2)
    layer_output = (share0.astype(F32) + near1.astype(F32) + across.astype(F32)).astype(BF16)

    grad_type = BF16 if dense else F32
    parts = pl.pallas_call(
        functools.partial(backward_kernel, (2, 3), n_pre, scaling),
        out_shape=[jax.ShapeDtypeStruct(x.shape, grad_type) for x in prefix],
        in_specs=[SMEM] + [VMEM] * (9 + n_pre),
        out_specs=[VMEM] * n_pre,
        scratch_shapes=[
            pltpu.VMEM((heads * length, HD), BF16),
            pltpu.VMEM((heads * length, HD), BF16),
            pltpu.VMEM((n_rows, heads * length), BF16),
            pltpu.VMEM((2, n_rows, length), F32),
        ],
        compiler_params=grant(32),
        cost_estimate=cost(7e9, 1e7),
        name="backward",
    )(me_tp, output_weight, near, queries, new_v, exps, row, col, far_grad, last_grad, *prefix)

    if dense:
        back = {k: hop(parts[k], "seq", k) for k in far_first}
        returned = [parts[0]] + [back[k] for k in range(1, n_seq)]
        shape = jax.ShapeDtypeStruct(prefix_keys.shape, F32)
        key_grad, value_grad = pl.pallas_call(
            functools.partial(place_kernel, n_seq, cap, here),
            out_shape=[shape] * 2,
            in_specs=[SMEM, SMEM] + [VMEM] * n_seq,
            out_specs=[VMEM] * 2,
            cost_estimate=cost(0, 2 ** 20),
            compiler_params=grant(4),
            name="place",
        )(me_seq, reads, *returned)
    else:
        cache_grads = parts[0].reshape(read_count, flat)
        placer = ((my_owner[None, None, :] == jnp.arange(n_seq, dtype=jnp.int32)[:, None, None])
                  & (my_rank[None, None, :] == slots[None, :, None])).astype(F32)
        leaving = jnp.einsum("ocr,rf->ocf", placer, cache_grads, precision=lax.Precision.HIGHEST)
        back = lax.all_to_all(leaving.astype(BF16), "seq", split_axis=0, concat_axis=0, tiled=True).astype(F32)
        summed = jnp.einsum("dcb,dcf->bf", picker, back, precision=lax.Precision.HIGHEST).reshape(here * PBLK, 2 * HD)
        key_grad, value_grad = summed[:, :HD], summed[:, HD:]
    return layer_output, key_grad, value_grad


def solution(mesh):
    in_specs = (P("seq", "tp"), P("seq", "tp"), P(None, "tp"), P(None, "tp"), P("tp", None),
                P("seq", "tp"), P("seq", "tp"), P(), P("seq", "tp"))
    out_specs = (P("seq", "tp"), P("seq", "tp"), P("seq", "tp"))
    return jax.shard_map(local, mesh=mesh, in_specs=in_specs, out_specs=out_specs, check_vma=False)
```

```python
import functools

import jax
import jax.numpy as jnp
from jax import lax
from jax.experimental import pallas as pl
from jax.experimental.pallas import tpu as pltpu
from jax.sharding import PartitionSpec as P


HD = 128
PBLK = 64
LOG2E = 1.4426950408889634
F32 = jnp.float32
BF16 = jnp.bfloat16
VMEM = pl.BlockSpec(memory_space=pltpu.VMEM)
SMEM = pl.BlockSpec(memory_space=pltpu.SMEM)
HBM = pl.BlockSpec(memory_space=pltpu.HBM)


def dot(a, b, dims):
    return lax.dot_general(a, b, (dims, ((), ())), preferred_element_type=F32)


def hbm(x):
    return pltpu.with_memory_space_constraint(x, pltpu.HBM)


def cost(flops, nbytes, trans=0):
    return pl.CostEstimate(flops=int(flops), bytes_accessed=int(nbytes), transcendentals=int(trans))


def pick_kernel(n, cap, here, me_ref, reads_hbm, keys_hbm, values_hbm, *refs):
    outs, (reads_ref, keys_ref, values_ref, sems) = refs[:n], refs[n:]
    me = me_ref[0]
    copies = [
        pltpu.make_async_copy(src, dst, sems.at[i])
        for i, (src, dst) in enumerate(
            ((reads_hbm, reads_ref), (keys_hbm, keys_ref), (values_hbm, values_ref)))
    ]
    for copy in copies:
        copy.start()
    for copy in copies:
        copy.wait()
    for k in range(n):
        for r in range(cap):
            block = reads_ref[me ^ k, cap * me + r] - here * me
            rows = pl.ds(pl.multiple_of(block * PBLK, PBLK), PBLK)
            outs[k][r * PBLK:(r + 1) * PBLK, :HD] = keys_ref[rows, :]
            outs[k][r * PBLK:(r + 1) * PBLK, HD:] = values_ref[rows, :]


def place_kernel(n, cap, here, me_ref, reads_ref, *refs):
    parts, keys_ref, values_ref = refs[:n], refs[n], refs[n + 1]
    me = me_ref[0]
    keys_ref[...] = jnp.zeros_like(keys_ref)
    values_ref[...] = jnp.zeros_like(values_ref)
    for k in range(n):
        for r in range(cap):
            block = reads_ref[me ^ k, cap * me + r] - here * me
            rows = pl.ds(pl.multiple_of(block * PBLK, PBLK), PBLK)
            piece = parts[k][r * PBLK:(r + 1) * PBLK, :].astype(F32)
            keys_ref[rows, :] += piece[:, :HD]
            values_ref[rows, :] += piece[:, HD:]


def weight_copies(i, me, width, hbms, bufs, slot, sems):
    rows = pl.ds(pl.multiple_of((me ^ i) * width, width), width)
    return [pltpu.make_async_copy(w.at[rows], buf.at[slot], sems.at[j, slot]) for j, (w, buf) in enumerate(zip(hbms, bufs))]


def kv_kernel(order, me_ref, own_hbm, *refs):
    hidden, (wk_hbm, wv_hbm, k_ref, v_ref, own_ref, wk_ref, wv_ref, sems, own_sem) = refs[:-9], refs[-9:]
    me = me_ref[0]
    width = own_ref.shape[1]

    def fetch(slot, i):
        return weight_copies(i, me, width, (wk_hbm, wv_hbm), (wk_ref, wv_ref), slot, sems)

    for slot, i in enumerate(order):
        for copy in fetch(slot, i):
            copy.start()
    own = pltpu.make_async_copy(own_hbm, own_ref, own_sem)
    own.start()
    new_k = jnp.zeros(k_ref.shape, F32)
    new_v = jnp.zeros(k_ref.shape, F32)
    for slot, i in enumerate(order):
        for copy in fetch(slot, i):
            copy.wait()
        if i == 0:
            own.wait()
        piece = hidden[i - 1][...] if i else own_ref[...]
        new_k += dot(piece, wk_ref[slot], ((1,), (0,)))
        new_v += dot(piece, wv_ref[slot], ((1,), (0,)))
    k_ref[...] = new_k
    v_ref[...] = new_v


def forward_kernel(n_pre, scaling, last, me_ref, wk_hbm, wv_hbm, hidden_ref, q_ref, partk_ref, partv_ref, *refs):
    prefix = refs[:n_pre]
    ctx_ref, exps_ref, row_ref, col_ref, newv_ref, newk_ref, wk_ref, wv_ref, vt_all, s_buf, sums, sems = refs[n_pre:]
    length, width = hidden_ref.shape
    copies = weight_copies(last, me_ref[0], width, (wk_hbm, wv_hbm), (wk_ref, wv_ref), 0, sems)
    for copy in copies:
        copy.start()
    heads = q_ref.shape[1] // HD
    factor = scaling * LOG2E
    chunks = []
    at = 0
    for ref in prefix:
        size = ref.shape[0]
        vt_all[:, at:at + size] = ref[:, HD:].astype(F32).T.astype(BF16)
        chunks.append((at, size, ref))
        at += size
    for copy in copies:
        copy.wait()
    piece = hidden_ref[...]
    newk_ref[...] = (partk_ref[...] + dot(piece, wk_ref[0], ((1,), (0,)))).astype(BF16)
    newv_ref[...] = (partv_ref[...] + dot(piece, wv_ref[0], ((1,), (0,)))).astype(BF16)
    vt_all[:, at:] = newv_ref[...].astype(F32).T.astype(BF16)
    visible = lax.broadcasted_iota(jnp.int32, (length, length), 0) <= lax.broadcasted_iota(
        jnp.int32, (length, length), 1)
    sums[...] = jnp.ones_like(sums)

    def scores(h):
        qh = q_ref[:, h * HD:(h + 1) * HD]
        peak = None
        for start, size, ref in chunks:
            s = dot(ref[:, :HD], qh, ((1,), (1,)))
            s_buf[h % 2, start:start + size, :] = s
            top = jnp.max(s, axis=0, keepdims=True)
            peak = top if peak is None else jnp.maximum(peak, top)
        s = jnp.where(visible, dot(newk_ref[...], qh, ((1,), (1,))), -jnp.inf)
        s_buf[h % 2, at:, :] = s
        return jnp.maximum(peak, jnp.max(s, axis=0, keepdims=True))

    def finish(h, peak):
        lanes = slice(h * length, (h + 1) * length)
        total = jnp.zeros((1, length), F32)
        step = length // 2
        for start in range(0, at + length, step):
            e = jnp.exp2((s_buf[h % 2, start:start + step, :] - peak) * factor)
            total += jnp.sum(e, axis=0, keepdims=True)
            exps_ref[start:start + step, lanes] = e.astype(BF16)
        inverse = 1.0 / total
        sums[h:h + 1, :] = inverse
        ctx_t = dot(vt_all[...], exps_ref[:, lanes], ((1,), (0,))) * inverse
        ctx_ref[:, h * HD:(h + 1) * HD] = ctx_t.T.astype(BF16)

    peak = scores(0)
    for h in range(heads):
        later = scores(h + 1) if h + 1 < heads else None
        finish(h, peak)
        peak = later
    row_ref[...] = sums[:row_ref.shape[0], :]
    col_ref[...] = sums[...].T


def project_kernel(order, me_ref, ctx_ref, w_ref, *outs):
    me = me_ref[0]
    width = outs[0].shape[1]
    ctx = ctx_ref[...]
    for i, out in zip(order, outs):
        cols = pl.ds(pl.multiple_of((me ^ i) * width, 128), width)
        out[...] = dot(ctx, w_ref[:, cols], ((1,), (0,))).astype(BF16)


def backward_kernel(order, n_pre, scaling, me_ref, w_ref, q_ref, newv_ref, exps_ref, row_ref, col_ref, *refs):
    grads, prefix = refs[:len(order)], refs[len(order):len(order) + n_pre]
    outs = refs[len(order) + n_pre:len(order) + 2 * n_pre]
    g_all, q_all, dbuf, slopes = refs[len(order) + 2 * n_pre:]
    me = me_ref[0]
    length, width = grads[0].shape
    heads = q_ref.shape[1] // HD
    total = jnp.zeros((length, heads * HD), F32)
    for i, grad in zip(order, grads):
        cols = pl.ds(pl.multiple_of((me ^ i) * width, 128), width)
        total += dot(grad[...], w_ref[:, cols], ((1,), (1,)))
    for h in range(heads):
        rows = slice(h * length, (h + 1) * length)
        q_all[rows, :] = q_ref[:, h * HD:(h + 1) * HD]
        g_all[rows, :] = (total[:, h * HD:(h + 1) * HD] * col_ref[:, h:h + 1]).astype(BF16)
    n_rows = dbuf.shape[0]

    def slope(h):
        gh = g_all[h * length:(h + 1) * length, :]
        lanes = slice(h * length, (h + 1) * length)
        at = 0
        delta = None
        for ref in prefix:
            size = ref.shape[0]
            s = dot(ref[:, HD:], gh, ((1,), (1,)))
            slopes[h % 2, at:at + size, :] = s
            part = jnp.sum(exps_ref[at:at + size, lanes].astype(F32) * s, axis=0, keepdims=True)
            delta = part if delta is None else delta + part
            at += size
        s = dot(newv_ref[...], gh, ((1,), (1,)))
        delta += jnp.sum(exps_ref[at:, lanes].astype(F32) * s, axis=0, keepdims=True)
        return delta * row_ref[h:h + 1, :]

    def finish(h, delta):
        lanes = slice(h * length, (h + 1) * length)
        step = length // 2
        for start in range(0, n_rows, step):
            e = exps_ref[start:start + step, lanes].astype(F32)
            dbuf[start:start + step, lanes] = (e * (slopes[h % 2, start:start + step, :] - delta)).astype(BF16)

    delta = slope(0)
    for h in range(heads):
        later = slope(h + 1) if h + 1 < heads else None
        finish(h, delta)
        delta = later
    at = 0
    for out in outs:
        size = out.shape[0]
        out[:, HD:] = dot(exps_ref[at:at + size, :], g_all[...], ((1,), (0,))).astype(out.dtype)
        out[:, :HD] = (dot(dbuf[at:at + size, :], q_all[...], ((1,), (0,))) * scaling).astype(out.dtype)
        at += size


def local(hidden_states, queries, key_weight, value_weight, output_weight, prefix_keys, prefix_values, reads, out_grad):
    length, width = hidden_states.shape
    scaling = HD ** (-0.5)
    heads = queries.shape[1] // HD
    n_tp = lax.axis_size("tp")
    n_seq = lax.axis_size("seq")
    here = prefix_keys.shape[0] // PBLK
    read_count = reads.shape[1]
    cap = max(1, read_count // n_seq)
    dense = cap * n_seq == read_count and n_seq & (n_seq - 1) == 0 and here * n_seq % read_count == 0
    me_tp = lax.axis_index("tp").astype(jnp.int32).reshape(1)
    me_seq = lax.axis_index("seq").astype(jnp.int32).reshape(1)
    n_rows = read_count * PBLK
    keys = n_rows + length

    def hop(x, axis, k):
        n = n_tp if axis == "tp" else n_seq
        return lax.ppermute(x, axis, [(i, i ^ k) for i in range(n)])

    def grant(mib):
        return pltpu.CompilerParams(vmem_limit_bytes=mib * 2 ** 20)

    near_grad = hop(out_grad, "tp", 1)
    far_grad = hop(out_grad, "tp", 2)
    near_hidden = hop(hidden_states, "tp", 1)
    far_hidden = hop(hidden_states, "tp", 2)
    last_hidden = hop(far_hidden, "tp", 1)
    last_grad = hop(far_grad, "tp", 1)
    far_first = sorted(range(1, n_seq), key=lambda k: (-(k // 4), k & 1, -k))

    if dense:
        shape = jax.ShapeDtypeStruct((cap * PBLK, 2 * HD), BF16)
        picked = pl.pallas_call(
            functools.partial(pick_kernel, n_seq, cap, here),
            out_shape=[shape] * n_seq,
            in_specs=[SMEM, HBM, HBM, HBM],
            out_specs=[VMEM] * n_seq,
            scratch_shapes=[
                pltpu.SMEM(reads.shape, jnp.int32),
                pltpu.VMEM(prefix_keys.shape, BF16),
                pltpu.VMEM(prefix_keys.shape, BF16),
                pltpu.SemaphoreType.DMA((3,)),
            ],
            cost_estimate=cost(0, 2 ** 20),
            compiler_params=grant(4),
            name="pick",
        )(me_seq, hbm(reads), hbm(prefix_keys), hbm(prefix_values))
        moved = {k: hop(picked[k], "seq", k) for k in far_first}
        prefix = [picked[0]] + [moved[k] for k in range(1, n_seq)]
    else:
        flat = PBLK * 2 * HD
        local_cache = jnp.concatenate([prefix_keys, prefix_values], axis=1).reshape(here, flat)
        own = me_seq[0]
        owners = reads // here
        slot_here = reads % here
        earlier = jnp.arange(read_count)[None, :] < jnp.arange(read_count)[:, None]
        ranks = jnp.sum((owners[:, :, None] == owners[:, None, :]) & earlier[None], axis=2)
        slots = jnp.arange(cap, dtype=jnp.int32)
        picker = jnp.sum(
            ((owners == own)[:, :, None, None]
             & (ranks[:, :, None, None] == slots[None, None, :, None])
             & (slot_here[:, :, None, None] == jnp.arange(here, dtype=jnp.int32))).astype(F32), axis=1)
        outgoing = jnp.einsum("dcb,bf->dcf", picker.astype(BF16), local_cache, preferred_element_type=F32).astype(BF16)
        incoming = lax.all_to_all(outgoing, "seq", split_axis=0, concat_axis=0, tiled=True)
        my_owner, my_rank = owners[own], ranks[own]
        fetched = jnp.take(incoming.reshape(n_seq * cap, flat), my_owner * cap + my_rank, axis=0)
        prefix = [fetched.reshape(n_rows, 2 * HD)]
    n_pre = len(prefix)

    weight_bufs = [pltpu.VMEM((n_tp - 1, width, HD), BF16)] * 2
    part_k, part_v = pl.pallas_call(
        functools.partial(kv_kernel, (1, 0, 2)),
        out_shape=[jax.ShapeDtypeStruct((length, HD), F32)] * 2,
        in_specs=[SMEM, HBM] + [VMEM] * (n_tp - 2) + [HBM] * 2,
        out_specs=[VMEM] * 2,
        scratch_shapes=[
            pltpu.VMEM((length, width), BF16),
            *weight_bufs,
            pltpu.SemaphoreType.DMA((2, n_tp - 1)),
            pltpu.SemaphoreType.DMA,
        ],
        compiler_params=grant(8),
        cost_estimate=cost(4e8, 3e6),
        name="kv",
    )(me_tp, hbm(hidden_states), near_hidden, far_hidden, hbm(key_weight), hbm(value_weight))

    ctx, exps, row, col, new_v = pl.pallas_call(
        functools.partial(forward_kernel, n_pre, scaling, n_tp - 1),
        out_shape=[
            jax.ShapeDtypeStruct((length, heads * HD), BF16),
            jax.ShapeDtypeStruct((keys, heads * length), BF16),
            jax.ShapeDtypeStruct((heads + (-heads) % 8, length), F32),
            jax.ShapeDtypeStruct((length, HD), F32),
            jax.ShapeDtypeStruct((length, HD), BF16),
        ],
        in_specs=[SMEM, HBM, HBM] + [VMEM] * (4 + n_pre),
        out_specs=[VMEM] * 5,
        scratch_shapes=[
            pltpu.VMEM((length, HD), BF16),
            pltpu.VMEM((1, width, HD), BF16),
            pltpu.VMEM((1, width, HD), BF16),
            pltpu.VMEM((HD, keys), BF16),
            pltpu.VMEM((2, keys, length), F32),
            pltpu.VMEM((HD, length), F32),
            pltpu.SemaphoreType.DMA((2, 1)),
        ],
        compiler_params=grant(20),
        cost_estimate=cost(5e9, 1e7, 3e6),
        name="forward",
    )(me_tp, hbm(key_weight), hbm(value_weight), last_hidden, queries, part_k, part_v, *prefix)

    def project(order):
        return pl.pallas_call(
            functools.partial(project_kernel, order),
            out_shape=[jax.ShapeDtypeStruct((length, width), BF16)] * len(order),
            in_specs=[SMEM, VMEM, VMEM],
            out_specs=[VMEM] * len(order),
            compiler_params=grant(16),
            cost_estimate=cost(5e8 * len(order), 2e6 * len(order)),
        )(me_tp, ctx, output_weight)

    share3, = project((3,))
    near3 = hop(share3, "tp", 1)
    share2, share1, share0 = project((2, 1, 0))
    near1 = hop(share1, "tp", 1)
    cross = (share2.astype(F32) + near3.astype(F32)).astype(BF16)
    across = hop(cross, "tp", 2)
    layer_output = (share0.astype(F32) + near1.astype(F32) + across.astype(F32)).astype(BF16)

    grad_type = BF16 if dense else F32
    parts = pl.pallas_call(
        functools.partial(backward_kernel, (0, 1, 2, 3), n_pre, scaling),
        out_shape=[jax.ShapeDtypeStruct(x.shape, grad_type) for x in prefix],
        in_specs=[SMEM] + [VMEM] * (10 + n_pre),
        out_specs=[VMEM] * n_pre,
        scratch_shapes=[
            pltpu.VMEM((heads * length, HD), BF16),
            pltpu.VMEM((heads * length, HD), BF16),
            pltpu.VMEM((n_rows, heads * length), BF16),
            pltpu.VMEM((2, n_rows, length), F32),
        ],
        compiler_params=grant(32),
        cost_estimate=cost(7e9, 1e7),
        name="backward",
    )(me_tp, output_weight, queries, new_v, exps, row, col, out_grad, near_grad, far_grad, last_grad, *prefix)

    if dense:
        back = {k: hop(parts[k], "seq", k) for k in far_first}
        returned = [parts[0]] + [back[k] for k in range(1, n_seq)]
        shape = jax.ShapeDtypeStruct(prefix_keys.shape, F32)
        key_grad, value_grad = pl.pallas_call(
            functools.partial(place_kernel, n_seq, cap, here),
            out_shape=[shape] * 2,
            in_specs=[SMEM, SMEM] + [VMEM] * n_seq,
            out_specs=[VMEM] * 2,
            cost_estimate=cost(0, 2 ** 20),
            compiler_params=grant(4),
            name="place",
        )(me_seq, reads, *returned)
    else:
        cache_grads = parts[0].reshape(read_count, flat)
        placer = ((my_owner[None, None, :] == jnp.arange(n_seq, dtype=jnp.int32)[:, None, None])
                  & (my_rank[None, None, :] == slots[None, :, None])).astype(F32)
        leaving = jnp.einsum("ocr,rf->ocf", placer, cache_grads, precision=lax.Precision.HIGHEST)
        back = lax.all_to_all(leaving.astype(BF16), "seq", split_axis=0, concat_axis=0, tiled=True).astype(F32)
        summed = jnp.einsum("dcb,dcf->bf", picker, back, precision=lax.Precision.HIGHEST).reshape(here * PBLK, 2 * HD)
        key_grad, value_grad = summed[:, :HD], summed[:, HD:]
    return layer_output, key_grad, value_grad


def solution(mesh):
    in_specs = (P("seq", "tp"), P("seq", "tp"), P(None, "tp"), P(None, "tp"), P("tp", None),
                P("seq", "tp"), P("seq", "tp"), P(), P("seq", "tp"))
    out_specs = (P("seq", "tp"), P("seq", "tp"), P("seq", "tp"))
    return jax.shard_map(local, mesh=mesh, in_specs=in_specs, out_specs=out_specs, check_vma=False)
```

```python
import functools

import jax
import jax.numpy as jnp
from jax import lax
from jax.experimental import pallas as pl
from jax.experimental.pallas import tpu as pltpu
from jax.sharding import PartitionSpec as P


HD = 128
PBLK = 64
LOG2E = 1.4426950408889634
F32 = jnp.float32
BF16 = jnp.bfloat16
VMEM = pl.BlockSpec(memory_space=pltpu.VMEM)
SMEM = pl.BlockSpec(memory_space=pltpu.SMEM)
HBM = pl.BlockSpec(memory_space=pltpu.HBM)


def dot(a, b, dims):
    return lax.dot_general(a, b, (dims, ((), ())), preferred_element_type=F32)


def hbm(x):
    return pltpu.with_memory_space_constraint(x, pltpu.HBM)


def cost(flops, nbytes, trans=0):
    return pl.CostEstimate(flops=int(flops), bytes_accessed=int(nbytes), transcendentals=int(trans))


def pick_kernel(n, cap, here, me_ref, reads_hbm, keys_hbm, values_hbm, *refs):
    outs, (reads_ref, keys_ref, values_ref, sems) = refs[:n], refs[n:]
    me = me_ref[0]
    copies = [
        pltpu.make_async_copy(src, dst, sems.at[i])
        for i, (src, dst) in enumerate(
            ((reads_hbm, reads_ref), (keys_hbm, keys_ref), (values_hbm, values_ref)))
    ]
    for copy in copies:
        copy.start()
    for copy in copies:
        copy.wait()
    for k in range(n):
        for r in range(cap):
            block = reads_ref[me ^ k, cap * me + r] - here * me
            rows = pl.ds(pl.multiple_of(block * PBLK, PBLK), PBLK)
            outs[k][r * PBLK:(r + 1) * PBLK, :HD] = keys_ref[rows, :]
            outs[k][r * PBLK:(r + 1) * PBLK, HD:] = values_ref[rows, :]


def place_kernel(n, cap, here, me_ref, reads_ref, *refs):
    parts, keys_ref, values_ref = refs[:n], refs[n], refs[n + 1]
    me = me_ref[0]
    keys_ref[...] = jnp.zeros_like(keys_ref)
    values_ref[...] = jnp.zeros_like(values_ref)
    for k in range(n):
        for r in range(cap):
            block = reads_ref[me ^ k, cap * me + r] - here * me
            rows = pl.ds(pl.multiple_of(block * PBLK, PBLK), PBLK)
            piece = parts[k][r * PBLK:(r + 1) * PBLK, :].astype(F32)
            keys_ref[rows, :] += piece[:, :HD]
            values_ref[rows, :] += piece[:, HD:]


def weight_copies(i, me, width, hbms, bufs, slot, sems):
    rows = pl.ds(pl.multiple_of((me ^ i) * width, width), width)
    return [pltpu.make_async_copy(w.at[rows], buf.at[slot], sems.at[j, slot]) for j, (w, buf) in enumerate(zip(hbms, bufs))]


def kv_kernel(order, last, me_ref, own_hbm, *refs):
    hidden, (wk_hbm, wv_hbm, q_hbm, k_ref, v_ref, q_ref, lastk_ref, lastv_ref) = refs[:-13], refs[-13:-5]
    own_ref, wk_ref, wv_ref, sems, far_sems = refs[-5:]
    me = me_ref[0]
    width = own_ref.shape[1]

    def fetch(slot, i):
        return weight_copies(i, me, width, (wk_hbm, wv_hbm), (wk_ref, wv_ref), slot, sems)

    for slot, i in enumerate(order):
        for copy in fetch(slot, i):
            copy.start()
    own = pltpu.make_async_copy(own_hbm, own_ref, far_sems.at[0])
    own.start()
    rows = pl.ds(pl.multiple_of((me ^ last) * width, width), width)
    later = [
        pltpu.make_async_copy(q_hbm, q_ref, far_sems.at[1]),
        pltpu.make_async_copy(wk_hbm.at[rows], lastk_ref, far_sems.at[2]),
        pltpu.make_async_copy(wv_hbm.at[rows], lastv_ref, far_sems.at[3]),
    ]
    for copy in later:
        copy.start()
    new_k = jnp.zeros(k_ref.shape, F32)
    new_v = jnp.zeros(k_ref.shape, F32)
    for slot, i in enumerate(order):
        for copy in fetch(slot, i):
            copy.wait()
        if i == 0:
            own.wait()
        piece = hidden[i - 1][...] if i else own_ref[...]
        new_k += dot(piece, wk_ref[slot], ((1,), (0,)))
        new_v += dot(piece, wv_ref[slot], ((1,), (0,)))
    k_ref[...] = new_k
    v_ref[...] = new_v
    for copy in later:
        copy.wait()


def forward_kernel(n_pre, scaling, wk_ref, wv_ref, hidden_ref, q_ref, partk_ref, partv_ref, *refs):
    prefix = refs[:n_pre]
    ctx_ref, exps_ref, row_ref, v_all, k_all, vt_all, s_buf, sums = refs[n_pre:]
    length = hidden_ref.shape[0]
    heads = q_ref.shape[1] // HD
    factor = scaling * LOG2E
    at = 0
    for ref in prefix:
        size = ref.shape[0]
        k_all[at:at + size, :] = ref[:, :HD]
        v_all[at:at + size, :] = ref[:, HD:]
        at += size
    piece = hidden_ref[...]
    k_all[at:, :] = (partk_ref[...] + dot(piece, wk_ref[...], ((1,), (0,)))).astype(BF16)
    v_all[at:, :] = (partv_ref[...] + dot(piece, wv_ref[...], ((1,), (0,)))).astype(BF16)
    vt_all[...] = v_all[...].astype(F32).T.astype(BF16)
    visible = lax.broadcasted_iota(jnp.int32, (length, length), 0) <= lax.broadcasted_iota(
        jnp.int32, (length, length), 1)

    def scores(h):
        qh = q_ref[:, h * HD:(h + 1) * HD]
        s = dot(k_all[:at, :], qh, ((1,), (1,)))
        s_buf[h % 2, :at, :] = s
        peak = jnp.max(s, axis=0, keepdims=True)
        s = jnp.where(visible, dot(k_all[at:, :], qh, ((1,), (1,))), -jnp.inf)
        s_buf[h % 2, at:, :] = s
        return jnp.maximum(peak, jnp.max(s, axis=0, keepdims=True))

    def finish(h, peak):
        lanes = slice(h * length, (h + 1) * length)
        total = jnp.zeros((1, length), F32)
        step = length // 2
        for start in range(0, at + length, step):
            e = jnp.exp2((s_buf[h % 2, start:start + step, :] - peak) * factor)
            total += jnp.sum(e, axis=0, keepdims=True)
            exps_ref[start:start + step, lanes] = e.astype(BF16)
        inverse = 1.0 / total
        sums[h:h + 1, :] = inverse
        ctx_t = dot(vt_all[...], exps_ref[:, lanes], ((1,), (0,))) * inverse
        ctx_ref[:, h * HD:(h + 1) * HD] = ctx_t.T.astype(BF16)

    peak = scores(0)
    for h in range(heads):
        later = scores(h + 1) if h + 1 < heads else None
        finish(h, peak)
        peak = later
    row_ref[:heads, :] = sums[:heads, :]


def project_kernel(order, me_ref, ctx_ref, w_ref, *outs):
    me = me_ref[0]
    width = outs[0].shape[1]
    ctx = ctx_ref[...]
    for i, out in zip(order, outs):
        cols = pl.ds(pl.multiple_of((me ^ i) * width, 128), width)
        out[...] = dot(ctx, w_ref[:, cols], ((1,), (0,))).astype(BF16)


def grad_kernel(order, me_ref, w_ref, *refs):
    grads, out = refs[:-1], refs[-1]
    me = me_ref[0]
    width = grads[0].shape[1]
    total = jnp.zeros(out.shape, F32)
    for i, grad in zip(order, grads):
        cols = pl.ds(pl.multiple_of((me ^ i) * width, 128), width)
        total += dot(w_ref[:, cols], grad[...], ((1,), (1,)))
    out[...] = total


def backward_kernel(last, n_pre, scaling, me_ref, w_ref, part_ref, grad_ref, q_ref, v_all, exps_ref, row_ref, *refs):
    outs = refs[:n_pre]
    gt_all, q_all, dbuf, slopes = refs[n_pre:]
    me = me_ref[0]
    length, width = grad_ref.shape
    heads = q_ref.shape[1] // HD
    cols = pl.ds(pl.multiple_of((me ^ last) * width, 128), width)
    total = part_ref[...] + dot(w_ref[:, cols], grad_ref[...], ((1,), (1,)))
    for h in range(heads):
        lanes = slice(h * length, (h + 1) * length)
        q_all[lanes, :] = q_ref[:, h * HD:(h + 1) * HD]
        gt_all[:, lanes] = (total[h * HD:(h + 1) * HD, :] * row_ref[h:h + 1, :]).astype(BF16)
    n_rows = dbuf.shape[0]

    def slope(h):
        lanes = slice(h * length, (h + 1) * length)
        s = dot(v_all[...], gt_all[:, lanes], ((1,), (0,)))
        slopes[h % 2] = s[:n_rows]
        delta = jnp.sum(exps_ref[:, lanes].astype(F32) * s, axis=0, keepdims=True)
        return delta * row_ref[h:h + 1, :]

    def finish(h, delta):
        lanes = slice(h * length, (h + 1) * length)
        step = length // 2
        for start in range(0, n_rows, step):
            e = exps_ref[start:start + step, lanes].astype(F32)
            dbuf[start:start + step, lanes] = (e * (slopes[h % 2, start:start + step, :] - delta)).astype(BF16)

    delta = slope(0)
    for h in range(heads):
        later = slope(h + 1) if h + 1 < heads else None
        finish(h, delta)
        delta = later
    value_grad = dot(exps_ref[:n_rows, :], gt_all[...], ((1,), (1,)))
    key_grad = dot(dbuf[...], q_all[...], ((1,), (0,))) * scaling
    at = 0
    for out in outs:
        size = out.shape[0]
        out[:, HD:] = value_grad[at:at + size].astype(out.dtype)
        out[:, :HD] = key_grad[at:at + size].astype(out.dtype)
        at += size


def local(hidden_states, queries, key_weight, value_weight, output_weight, prefix_keys, prefix_values, reads, out_grad):
    length, width = hidden_states.shape
    scaling = HD ** (-0.5)
    heads = queries.shape[1] // HD
    n_tp = lax.axis_size("tp")
    n_seq = lax.axis_size("seq")
    here = prefix_keys.shape[0] // PBLK
    read_count = reads.shape[1]
    cap = max(1, read_count // n_seq)
    dense = cap * n_seq == read_count and n_seq & (n_seq - 1) == 0 and here * n_seq % read_count == 0
    me_tp = lax.axis_index("tp").astype(jnp.int32).reshape(1)
    me_seq = lax.axis_index("seq").astype(jnp.int32).reshape(1)
    n_rows = read_count * PBLK
    keys = n_rows + length

    def hop(x, axis, k):
        n = n_tp if axis == "tp" else n_seq
        return lax.ppermute(x, axis, [(i, i ^ k) for i in range(n)])

    def grant(mib):
        return pltpu.CompilerParams(vmem_limit_bytes=mib * 2 ** 20)

    near_grad = hop(out_grad, "tp", 1)
    far_grad = hop(out_grad, "tp", 2)
    near_hidden = hop(hidden_states, "tp", 1)
    far_hidden = hop(hidden_states, "tp", 2)
    last_hidden = hop(far_hidden, "tp", 1)
    last_grad = hop(far_grad, "tp", 1)
    far_first = sorted(range(1, n_seq), key=lambda k: (-(k // 4), k & 1, -k))

    if dense:
        shape = jax.ShapeDtypeStruct((cap * PBLK, 2 * HD), BF16)
        picked = pl.pallas_call(
            functools.partial(pick_kernel, n_seq, cap, here),
            out_shape=[shape] * n_seq,
            in_specs=[SMEM, HBM, HBM, HBM],
            out_specs=[VMEM] * n_seq,
            scratch_shapes=[
                pltpu.SMEM(reads.shape, jnp.int32),
                pltpu.VMEM(prefix_keys.shape, BF16),
                pltpu.VMEM(prefix_keys.shape, BF16),
                pltpu.SemaphoreType.DMA((3,)),
            ],
            cost_estimate=cost(0, 2 ** 20),
            compiler_params=grant(4),
            name="pick",
        )(me_seq, hbm(reads), hbm(prefix_keys), hbm(prefix_values))
        moved = {k: hop(picked[k], "seq", k) for k in far_first}
        prefix = [picked[0]] + [moved[k] for k in range(1, n_seq)]
    else:
        flat = PBLK * 2 * HD
        local_cache = jnp.concatenate([prefix_keys, prefix_values], axis=1).reshape(here, flat)
        own = me_seq[0]
        owners = reads // here
        slot_here = reads % here
        earlier = jnp.arange(read_count)[None, :] < jnp.arange(read_count)[:, None]
        ranks = jnp.sum((owners[:, :, None] == owners[:, None, :]) & earlier[None], axis=2)
        slots = jnp.arange(cap, dtype=jnp.int32)
        picker = jnp.sum(
            ((owners == own)[:, :, None, None]
             & (ranks[:, :, None, None] == slots[None, None, :, None])
             & (slot_here[:, :, None, None] == jnp.arange(here, dtype=jnp.int32))).astype(F32), axis=1)
        outgoing = jnp.einsum("dcb,bf->dcf", picker.astype(BF16), local_cache, preferred_element_type=F32).astype(BF16)
        incoming = lax.all_to_all(outgoing, "seq", split_axis=0, concat_axis=0, tiled=True)
        my_owner, my_rank = owners[own], ranks[own]
        fetched = jnp.take(incoming.reshape(n_seq * cap, flat), my_owner * cap + my_rank, axis=0)
        prefix = [fetched.reshape(n_rows, 2 * HD)]
    n_pre = len(prefix)

    part = jax.ShapeDtypeStruct((length, HD), F32)
    weight = jax.ShapeDtypeStruct((width, HD), BF16)
    part_k, part_v, q, last_k, last_v = pl.pallas_call(
        functools.partial(kv_kernel, (1, 0, 2), n_tp - 1),
        out_shape=[part, part, jax.ShapeDtypeStruct(queries.shape, BF16), weight, weight],
        in_specs=[SMEM, HBM] + [VMEM] * (n_tp - 2) + [HBM] * 3,
        out_specs=[VMEM] * 5,
        scratch_shapes=[
            pltpu.VMEM((length, width), BF16),
            pltpu.VMEM((n_tp - 1, width, HD), BF16),
            pltpu.VMEM((n_tp - 1, width, HD), BF16),
            pltpu.SemaphoreType.DMA((2, n_tp - 1)),
            pltpu.SemaphoreType.DMA((4,)),
        ],
        compiler_params=grant(8),
        cost_estimate=cost(4e8, 3e6),
        name="kv",
    )(me_tp, hbm(hidden_states), near_hidden, far_hidden, hbm(key_weight), hbm(value_weight), hbm(queries))

    ctx, exps, row, v_all = pl.pallas_call(
        functools.partial(forward_kernel, n_pre, scaling),
        out_shape=[
            jax.ShapeDtypeStruct((length, heads * HD), BF16),
            jax.ShapeDtypeStruct((keys, heads * length), BF16),
            jax.ShapeDtypeStruct((heads + (-heads) % 8, length), F32),
            jax.ShapeDtypeStruct((keys, HD), BF16),
        ],
        in_specs=[VMEM] * (6 + n_pre),
        out_specs=[VMEM] * 4,
        scratch_shapes=[
            pltpu.VMEM((keys, HD), BF16),
            pltpu.VMEM((HD, keys), BF16),
            pltpu.VMEM((2, keys, length), F32),
            pltpu.VMEM((heads + (-heads) % 8, length), F32),
        ],
        compiler_params=grant(20),
        cost_estimate=cost(5e9, 1e7, 3e6),
        name="forward",
    )(last_k, last_v, last_hidden, q, part_k, part_v, *prefix)

    part_grad = pl.pallas_call(
        functools.partial(grad_kernel, (0, 1, 2)),
        out_shape=jax.ShapeDtypeStruct((heads * HD, length), F32),
        in_specs=[SMEM] + [VMEM] * 4,
        out_specs=VMEM,
        compiler_params=grant(16),
        cost_estimate=cost(1.5e9, 8e6),
        name="grad",
    )(me_tp, output_weight, out_grad, near_grad, far_grad)

    def project(order):
        return pl.pallas_call(
            functools.partial(project_kernel, order),
            out_shape=[jax.ShapeDtypeStruct((length, width), BF16)] * len(order),
            in_specs=[SMEM, VMEM, VMEM],
            out_specs=[VMEM] * len(order),
            compiler_params=grant(16),
            cost_estimate=cost(5e8 * len(order), 2e6 * len(order)),
        )(me_tp, ctx, output_weight)

    share3, share2 = project((3, 2))
    near3 = hop(share3, "tp", 1)
    share1, share0 = project((1, 0))
    near1 = hop(share1, "tp", 1)
    cross = (share2.astype(F32) + near3.astype(F32)).astype(BF16)
    across = hop(cross, "tp", 2)
    layer_output = (share0.astype(F32) + near1.astype(F32) + across.astype(F32)).astype(BF16)

    grad_type = BF16 if dense else F32
    parts = pl.pallas_call(
        functools.partial(backward_kernel, n_tp - 1, n_pre, scaling),
        out_shape=[jax.ShapeDtypeStruct(x.shape, grad_type) for x in prefix],
        in_specs=[SMEM] + [VMEM] * 7,
        out_specs=[VMEM] * n_pre,
        scratch_shapes=[
            pltpu.VMEM((HD, heads * length), BF16),
            pltpu.VMEM((heads * length, HD), BF16),
            pltpu.VMEM((n_rows, heads * length), BF16),
            pltpu.VMEM((2, n_rows, length), F32),
        ],
        compiler_params=grant(32),
        cost_estimate=cost(7e9, 1e7),
        name="backward",
    )(me_tp, output_weight, part_grad, last_grad, q, v_all, exps, row)

    if dense:
        back = {k: hop(parts[k], "seq", k) for k in far_first}
        returned = [parts[0]] + [back[k] for k in range(1, n_seq)]
        shape = jax.ShapeDtypeStruct(prefix_keys.shape, F32)
        key_grad, value_grad = pl.pallas_call(
            functools.partial(place_kernel, n_seq, cap, here),
            out_shape=[shape] * 2,
            in_specs=[SMEM, SMEM] + [VMEM] * n_seq,
            out_specs=[VMEM] * 2,
            cost_estimate=cost(0, 2 ** 20),
            compiler_params=grant(4),
            name="place",
        )(me_seq, reads, *returned)
    else:
        cache_grads = parts[0].reshape(read_count, flat)
        placer = ((my_owner[None, None, :] == jnp.arange(n_seq, dtype=jnp.int32)[:, None, None])
                  & (my_rank[None, None, :] == slots[None, :, None])).astype(F32)
        leaving = jnp.einsum("ocr,rf->ocf", placer, cache_grads, precision=lax.Precision.HIGHEST)
        back = lax.all_to_all(leaving.astype(BF16), "seq", split_axis=0, concat_axis=0, tiled=True).astype(F32)
        summed = jnp.einsum("dcb,dcf->bf", picker, back, precision=lax.Precision.HIGHEST).reshape(here * PBLK, 2 * HD)
        key_grad, value_grad = summed[:, :HD], summed[:, HD:]
    return layer_output, key_grad, value_grad


def solution(mesh):
    in_specs = (P("seq", "tp"), P("seq", "tp"), P(None, "tp"), P(None, "tp"), P("tp", None),
                P("seq", "tp"), P("seq", "tp"), P(), P("seq", "tp"))
    out_specs = (P("seq", "tp"), P("seq", "tp"), P("seq", "tp"))
    return jax.shard_map(local, mesh=mesh, in_specs=in_specs, out_specs=out_specs, check_vma=False)
```

```python
import functools

import jax
import jax.numpy as jnp
from jax import lax
from jax.experimental import pallas as pl
from jax.experimental.pallas import tpu as pltpu
from jax.sharding import PartitionSpec as P


HD = 128
PBLK = 64
LOG2E = 1.4426950408889634
F32 = jnp.float32
BF16 = jnp.bfloat16
VMEM = pl.BlockSpec(memory_space=pltpu.VMEM)
SMEM = pl.BlockSpec(memory_space=pltpu.SMEM)
HBM = pl.BlockSpec(memory_space=pltpu.HBM)


def dot(a, b, dims):
    return lax.dot_general(a, b, (dims, ((), ())), preferred_element_type=F32)


def hbm(x):
    return pltpu.with_memory_space_constraint(x, pltpu.HBM)


def cost(flops, nbytes, trans=0):
    return pl.CostEstimate(flops=int(flops), bytes_accessed=int(nbytes), transcendentals=int(trans))


def pick_into(outs, cap, here, me, holder, reads_ref, keys_ref, values_ref):
    for k, out in enumerate(outs):
        for r in range(cap):
            block = reads_ref[me ^ k, cap * holder + r] - here * holder
            rows = pl.ds(pl.multiple_of(block * PBLK, PBLK), PBLK)
            out[r * PBLK:(r + 1) * PBLK, :HD] = keys_ref[rows, :]
            out[r * PBLK:(r + 1) * PBLK, HD:] = values_ref[rows, :]


def pick_kernel(cap, here, me_ref, reads_hbm, keys_hbm, values_hbm, *refs):
    outs, (kept_ref, reads_ref, keys_ref, values_ref, sems) = refs[:-5], refs[-5:]
    copies = [
        pltpu.make_async_copy(src, dst, sems.at[i])
        for i, (src, dst) in enumerate(
            ((reads_hbm, reads_ref), (keys_hbm, keys_ref), (values_hbm, values_ref), (reads_hbm, kept_ref)))
    ]
    for copy in copies:
        copy.start()
    for copy in copies:
        copy.wait()
    me = me_ref[0]
    pick_into(outs, cap, here, me, me, reads_ref, keys_ref, values_ref)


def pick_far_kernel(cap, here, flip, me_ref, reads_ref, keys_ref, values_ref, *outs):
    me = me_ref[0]
    pick_into(outs, cap, here, me, me ^ flip, reads_ref, keys_ref, values_ref)


def place_kernel(n, cap, here, me_ref, reads_ref, *refs):
    parts, keys_ref, values_ref = refs[:n], refs[n], refs[n + 1]
    me = me_ref[0]
    keys_ref[...] = jnp.zeros_like(keys_ref)
    values_ref[...] = jnp.zeros_like(values_ref)
    for k in range(n):
        for r in range(cap):
            block = reads_ref[me ^ k, cap * me + r] - here * me
            rows = pl.ds(pl.multiple_of(block * PBLK, PBLK), PBLK)
            piece = parts[k][r * PBLK:(r + 1) * PBLK, :].astype(F32)
            keys_ref[rows, :] += piece[:, :HD]
            values_ref[rows, :] += piece[:, HD:]


def weight_copies(i, me, width, hbms, bufs, slot, sems):
    rows = pl.ds(pl.multiple_of((me ^ i) * width, width), width)
    return [pltpu.make_async_copy(w.at[rows], buf.at[slot], sems.at[j, slot]) for j, (w, buf) in enumerate(zip(hbms, bufs))]


def kv_kernel(order, rest, me_ref, own_hbm, *refs):
    hidden, (wk_hbm, wv_hbm, q_hbm, k_ref, v_ref, q_ref, restk_ref, restv_ref) = refs[:-13], refs[-13:-5]
    own_ref, wk_ref, wv_ref, sems, far_sems = refs[-5:]
    me = me_ref[0]
    width = own_ref.shape[1]

    def fetch(slot, i):
        return weight_copies(i, me, width, (wk_hbm, wv_hbm), (wk_ref, wv_ref), slot, sems)

    for slot, i in enumerate(order):
        for copy in fetch(slot, i):
            copy.start()
    own = pltpu.make_async_copy(own_hbm, own_ref, far_sems.at[0])
    own.start()
    later = [pltpu.make_async_copy(q_hbm, q_ref, far_sems.at[1])]
    for slot, i in enumerate(rest):
        rows = pl.ds(pl.multiple_of((me ^ i) * width, width), width)
        later.append(pltpu.make_async_copy(wk_hbm.at[rows], restk_ref.at[slot], far_sems.at[2 + 2 * slot]))
        later.append(pltpu.make_async_copy(wv_hbm.at[rows], restv_ref.at[slot], far_sems.at[3 + 2 * slot]))
    for copy in later:
        copy.start()
    new_k = jnp.zeros(k_ref.shape, F32)
    new_v = jnp.zeros(k_ref.shape, F32)
    for slot, i in enumerate(order):
        for copy in fetch(slot, i):
            copy.wait()
        if i == 0:
            own.wait()
        piece = hidden[i - 1][...] if i else own_ref[...]
        new_k += dot(piece, wk_ref[slot], ((1,), (0,)))
        new_v += dot(piece, wv_ref[slot], ((1,), (0,)))
    k_ref[...] = new_k
    v_ref[...] = new_v
    for copy in later:
        copy.wait()


def forward_kernel(n_rest, n_pre, scaling, wk_ref, wv_ref, *refs):
    hidden, (q_ref, partk_ref, partv_ref), refs = refs[:n_rest], refs[n_rest:n_rest + 3], refs[n_rest + 3:]
    prefix = refs[:n_pre]
    ctx_ref, exps_ref, row_ref, v_all, k_all, vt_all, s_buf, sums = refs[n_pre:]
    length = q_ref.shape[0]
    heads = q_ref.shape[1] // HD
    factor = scaling * LOG2E
    at = 0
    for ref in prefix:
        size = ref.shape[0]
        k_all[at:at + size, :] = ref[:, :HD]
        v_all[at:at + size, :] = ref[:, HD:]
        at += size
    new_k, new_v = partk_ref[...], partv_ref[...]
    for slot, ref in enumerate(hidden):
        new_k += dot(ref[...], wk_ref[slot], ((1,), (0,)))
        new_v += dot(ref[...], wv_ref[slot], ((1,), (0,)))
    k_all[at:, :] = new_k.astype(BF16)
    v_all[at:, :] = new_v.astype(BF16)
    vt_all[...] = v_all[...].astype(F32).T.astype(BF16)
    visible = lax.broadcasted_iota(jnp.int32, (length, length), 0) <= lax.broadcasted_iota(
        jnp.int32, (length, length), 1)

    def scores(h):
        qh = q_ref[:, h * HD:(h + 1) * HD]
        s = dot(k_all[:at, :], qh, ((1,), (1,)))
        s_buf[h % 2, :at, :] = s
        peak = jnp.max(s, axis=0, keepdims=True)
        s = jnp.where(visible, dot(k_all[at:, :], qh, ((1,), (1,))), -jnp.inf)
        s_buf[h % 2, at:, :] = s
        return jnp.maximum(peak, jnp.max(s, axis=0, keepdims=True))

    def finish(h, peak):
        lanes = slice(h * length, (h + 1) * length)
        total = jnp.zeros((1, length), F32)
        step = length // 2
        for start in range(0, at + length, step):
            e = jnp.exp2((s_buf[h % 2, start:start + step, :] - peak) * factor)
            total += jnp.sum(e, axis=0, keepdims=True)
            exps_ref[start:start + step, lanes] = e.astype(BF16)
        inverse = 1.0 / total
        sums[h:h + 1, :] = inverse
        ctx_t = dot(vt_all[...], exps_ref[:, lanes], ((1,), (0,))) * inverse
        ctx_ref[:, h * HD:(h + 1) * HD] = ctx_t.T.astype(BF16)

    peak = scores(0)
    for h in range(heads):
        later = scores(h + 1) if h + 1 < heads else None
        finish(h, peak)
        peak = later
    row_ref[:heads, :] = sums[:heads, :]


def project_kernel(order, me_ref, ctx_ref, w_ref, *outs):
    me = me_ref[0]
    width = outs[0].shape[1]
    ctx = ctx_ref[...]
    for i, out in zip(order, outs):
        cols = pl.ds(pl.multiple_of((me ^ i) * width, 128), width)
        out[...] = dot(ctx, w_ref[:, cols], ((1,), (0,))).astype(BF16)


def grad_kernel(order, me_ref, w_ref, *refs):
    grads, out = refs[:-1], refs[-1]
    me = me_ref[0]
    width = grads[0].shape[1]
    total = jnp.zeros(out.shape, F32)
    for i, grad in zip(order, grads):
        cols = pl.ds(pl.multiple_of((me ^ i) * width, 128), width)
        total += dot(w_ref[:, cols], grad[...], ((1,), (1,)))
    out[...] = total


def backward_kernel(last, n_pre, scaling, me_ref, w_ref, part_ref, grad_ref, q_ref, v_all, exps_ref, row_ref, *refs):
    outs = refs[:n_pre]
    gt_all, q_all, dbuf, slopes = refs[n_pre:]
    me = me_ref[0]
    length, width = grad_ref.shape
    heads = q_ref.shape[1] // HD
    cols = pl.ds(pl.multiple_of((me ^ last) * width, 128), width)
    total = part_ref[...] + dot(w_ref[:, cols], grad_ref[...], ((1,), (1,)))
    for h in range(heads):
        lanes = slice(h * length, (h + 1) * length)
        q_all[lanes, :] = q_ref[:, h * HD:(h + 1) * HD]
        gt_all[:, lanes] = (total[h * HD:(h + 1) * HD, :] * row_ref[h:h + 1, :]).astype(BF16)
    n_rows = dbuf.shape[0]

    def slope(h):
        lanes = slice(h * length, (h + 1) * length)
        s = dot(v_all[...], gt_all[:, lanes], ((1,), (0,)))
        slopes[h % 2] = s[:n_rows]
        delta = jnp.sum(exps_ref[:, lanes].astype(F32) * s, axis=0, keepdims=True)
        return delta * row_ref[h:h + 1, :]

    def finish(h, delta):
        lanes = slice(h * length, (h + 1) * length)
        step = length // 2
        for start in range(0, n_rows, step):
            e = exps_ref[start:start + step, lanes].astype(F32)
            dbuf[start:start + step, lanes] = (e * (slopes[h % 2, start:start + step, :] - delta)).astype(BF16)

    delta = slope(0)
    for h in range(heads):
        later = slope(h + 1) if h + 1 < heads else None
        finish(h, delta)
        delta = later
    value_grad = dot(exps_ref[:n_rows, :], gt_all[...], ((1,), (1,)))
    key_grad = dot(dbuf[...], q_all[...], ((1,), (0,))) * scaling
    at = 0
    for out in outs:
        size = out.shape[0]
        out[:, HD:] = value_grad[at:at + size].astype(out.dtype)
        out[:, :HD] = key_grad[at:at + size].astype(out.dtype)
        at += size


def local(hidden_states, queries, key_weight, value_weight, output_weight, prefix_keys, prefix_values, reads, out_grad):
    length, width = hidden_states.shape
    scaling = HD ** (-0.5)
    heads = queries.shape[1] // HD
    n_tp = lax.axis_size("tp")
    n_seq = lax.axis_size("seq")
    here = prefix_keys.shape[0] // PBLK
    read_count = reads.shape[1]
    cap = max(1, read_count // n_seq)
    dense = cap * n_seq == read_count and n_seq & (n_seq - 1) == 0 and here * n_seq % read_count == 0
    me_tp = lax.axis_index("tp").astype(jnp.int32).reshape(1)
    me_seq = lax.axis_index("seq").astype(jnp.int32).reshape(1)
    n_rows = read_count * PBLK
    keys = n_rows + length

    def hop(x, axis, k):
        n = n_tp if axis == "tp" else n_seq
        return lax.ppermute(x, axis, [(i, i ^ k) for i in range(n)])

    def grant(mib):
        return pltpu.CompilerParams(vmem_limit_bytes=mib * 2 ** 20)

    near_grad = hop(out_grad, "tp", 1)
    far_grad = hop(out_grad, "tp", 2)
    near_hidden = hop(hidden_states, "tp", 1)
    far_hidden = hop(hidden_states, "tp", 2)
    last_hidden = hop(far_hidden, "tp", 1)
    last_grad = hop(far_grad, "tp", 1)
    far_first = sorted(range(1, n_seq), key=lambda k: (-(k // 4), k & 1, -k))

    if dense:
        shape = jax.ShapeDtypeStruct((cap * PBLK, 2 * HD), BF16)
        half = max(1, n_seq // 2)
        out_types = [shape] * half
        far_keys = hop(prefix_keys, "seq", half)
        far_values = hop(prefix_values, "seq", half)
        *picked, kept_reads = pl.pallas_call(
            functools.partial(pick_kernel, cap, here),
            out_shape=out_types + [jax.ShapeDtypeStruct(reads.shape, jnp.int32)],
            in_specs=[SMEM, HBM, HBM, HBM],
            out_specs=[VMEM] * (half + 1),
            scratch_shapes=[
                pltpu.SMEM(reads.shape, jnp.int32),
                pltpu.VMEM(prefix_keys.shape, BF16),
                pltpu.VMEM(prefix_keys.shape, BF16),
                pltpu.SemaphoreType.DMA((4,)),
            ],
            cost_estimate=cost(0, 2 ** 20),
            compiler_params=grant(4),
            name="pick",
        )(me_seq, hbm(reads), hbm(prefix_keys), hbm(prefix_values))
        picked_far = pl.pallas_call(
            functools.partial(pick_far_kernel, cap, here, half),
            out_shape=out_types,
            in_specs=[SMEM, SMEM, VMEM, VMEM],
            out_specs=[VMEM] * half,
            cost_estimate=cost(0, 2 ** 20),
            compiler_params=grant(4),
            name="pick_far",
        )(me_seq, kept_reads, far_keys, far_values)
        prefix = [picked[0]] + [hop(picked[k], "seq", k) for k in range(1, half)]
        prefix += [picked_far[0]] + [hop(picked_far[k], "seq", k) for k in range(1, half)]
    else:
        flat = PBLK * 2 * HD
        local_cache = jnp.concatenate([prefix_keys, prefix_values], axis=1).reshape(here, flat)
        own = me_seq[0]
        owners = reads // here
        slot_here = reads % here
        earlier = jnp.arange(read_count)[None, :] < jnp.arange(read_count)[:, None]
        ranks = jnp.sum((owners[:, :, None] == owners[:, None, :]) & earlier[None], axis=2)
        slots = jnp.arange(cap, dtype=jnp.int32)
        picker = jnp.sum(
            ((owners == own)[:, :, None, None]
             & (ranks[:, :, None, None] == slots[None, None, :, None])
             & (slot_here[:, :, None, None] == jnp.arange(here, dtype=jnp.int32))).astype(F32), axis=1)
        outgoing = jnp.einsum("dcb,bf->dcf", picker.astype(BF16), local_cache, preferred_element_type=F32).astype(BF16)
        incoming = lax.all_to_all(outgoing, "seq", split_axis=0, concat_axis=0, tiled=True)
        my_owner, my_rank = owners[own], ranks[own]
        fetched = jnp.take(incoming.reshape(n_seq * cap, flat), my_owner * cap + my_rank, axis=0)
        prefix = [fetched.reshape(n_rows, 2 * HD)]
    n_pre = len(prefix)

    part = jax.ShapeDtypeStruct((length, HD), F32)
    n_rest = n_tp - 2
    weight = jax.ShapeDtypeStruct((n_rest, width, HD), BF16)
    part_k, part_v, q, rest_k, rest_v = pl.pallas_call(
        functools.partial(kv_kernel, (0, 1), tuple(range(2, n_tp))),
        out_shape=[part, part, jax.ShapeDtypeStruct(queries.shape, BF16), weight, weight],
        in_specs=[SMEM, HBM, VMEM] + [HBM] * 3,
        out_specs=[VMEM] * 5,
        scratch_shapes=[
            pltpu.VMEM((length, width), BF16),
            pltpu.VMEM((2, width, HD), BF16),
            pltpu.VMEM((2, width, HD), BF16),
            pltpu.SemaphoreType.DMA((2, 2)),
            pltpu.SemaphoreType.DMA((2 + 2 * n_rest,)),
        ],
        compiler_params=grant(8),
        cost_estimate=cost(4e8, 3e6),
        name="kv",
    )(me_tp, hbm(hidden_states), near_hidden, hbm(key_weight), hbm(value_weight), hbm(queries))

    ctx, exps, row, v_all = pl.pallas_call(
        functools.partial(forward_kernel, n_rest, n_pre, scaling),
        out_shape=[
            jax.ShapeDtypeStruct((length, heads * HD), BF16),
            jax.ShapeDtypeStruct((keys, heads * length), BF16),
            jax.ShapeDtypeStruct((heads + (-heads) % 8, length), F32),
            jax.ShapeDtypeStruct((keys, HD), BF16),
        ],
        in_specs=[VMEM] * (5 + n_rest + n_pre),
        out_specs=[VMEM] * 4,
        scratch_shapes=[
            pltpu.VMEM((keys, HD), BF16),
            pltpu.VMEM((HD, keys), BF16),
            pltpu.VMEM((2, keys, length), F32),
            pltpu.VMEM((heads + (-heads) % 8, length), F32),
        ],
        compiler_params=grant(20),
        cost_estimate=cost(5e9, 1e7, 3e6),
        name="forward",
    )(rest_k, rest_v, far_hidden, last_hidden, q, part_k, part_v, *prefix)

    part_grad = pl.pallas_call(
        functools.partial(grad_kernel, (0, 1, 2)),
        out_shape=jax.ShapeDtypeStruct((heads * HD, length), F32),
        in_specs=[SMEM] + [VMEM] * 4,
        out_specs=VMEM,
        compiler_params=grant(16),
        cost_estimate=cost(1.5e9, 8e6),
        name="grad",
    )(me_tp, output_weight, out_grad, near_grad, far_grad)

    def project(order):
        return pl.pallas_call(
            functools.partial(project_kernel, order),
            out_shape=[jax.ShapeDtypeStruct((length, width), BF16)] * len(order),
            in_specs=[SMEM, VMEM, VMEM],
            out_specs=[VMEM] * len(order),
            compiler_params=grant(16),
            cost_estimate=cost(5e8 * len(order), 2e6 * len(order)),
        )(me_tp, ctx, output_weight)

    share3, share2 = project((3, 2))
    near3 = hop(share3, "tp", 1)
    share1, share0 = project((1, 0))
    near1 = hop(share1, "tp", 1)
    cross = (share2.astype(F32) + near3.astype(F32)).astype(BF16)
    across = hop(cross, "tp", 2)
    layer_output = (share0.astype(F32) + near1.astype(F32) + across.astype(F32)).astype(BF16)

    grad_type = BF16 if dense else F32
    parts = pl.pallas_call(
        functools.partial(backward_kernel, n_tp - 1, n_pre, scaling),
        out_shape=[jax.ShapeDtypeStruct(x.shape, grad_type) for x in prefix],
        in_specs=[SMEM] + [VMEM] * 7,
        out_specs=[VMEM] * n_pre,
        scratch_shapes=[
            pltpu.VMEM((HD, heads * length), BF16),
            pltpu.VMEM((heads * length, HD), BF16),
            pltpu.VMEM((n_rows, heads * length), BF16),
            pltpu.VMEM((2, n_rows, length), F32),
        ],
        compiler_params=grant(32),
        cost_estimate=cost(7e9, 1e7),
        name="backward",
    )(me_tp, output_weight, part_grad, last_grad, q, v_all, exps, row)

    if dense:
        back = {k: hop(parts[k], "seq", k) for k in far_first}
        returned = [parts[0]] + [back[k] for k in range(1, n_seq)]
        shape = jax.ShapeDtypeStruct(prefix_keys.shape, F32)
        key_grad, value_grad = pl.pallas_call(
            functools.partial(place_kernel, n_seq, cap, here),
            out_shape=[shape] * 2,
            in_specs=[SMEM, SMEM] + [VMEM] * n_seq,
            out_specs=[VMEM] * 2,
            cost_estimate=cost(0, 2 ** 20),
            compiler_params=grant(4),
            name="place",
        )(me_seq, kept_reads, *returned)
    else:
        cache_grads = parts[0].reshape(read_count, flat)
        placer = ((my_owner[None, None, :] == jnp.arange(n_seq, dtype=jnp.int32)[:, None, None])
                  & (my_rank[None, None, :] == slots[None, :, None])).astype(F32)
        leaving = jnp.einsum("ocr,rf->ocf", placer, cache_grads, precision=lax.Precision.HIGHEST)
        back = lax.all_to_all(leaving.astype(BF16), "seq", split_axis=0, concat_axis=0, tiled=True).astype(F32)
        summed = jnp.einsum("dcb,dcf->bf", picker, back, precision=lax.Precision.HIGHEST).reshape(here * PBLK, 2 * HD)
        key_grad, value_grad = summed[:, :HD], summed[:, HD:]
    return layer_output, key_grad, value_grad


def solution(mesh):
    in_specs = (P("seq", "tp"), P("seq", "tp"), P(None, "tp"), P(None, "tp"), P("tp", None),
                P("seq", "tp"), P("seq", "tp"), P(), P("seq", "tp"))
    out_specs = (P("seq", "tp"), P("seq", "tp"), P("seq", "tp"))
    return jax.shard_map(local, mesh=mesh, in_specs=in_specs, out_specs=out_specs, check_vma=False)
```

```python
import functools

import jax
import jax.numpy as jnp
from jax import lax
from jax.experimental import pallas as pl
from jax.experimental.pallas import tpu as pltpu
from jax.sharding import PartitionSpec as P


HD = 128
PBLK = 64
LOG2E = 1.4426950408889634
F32 = jnp.float32
BF16 = jnp.bfloat16
VMEM = pl.BlockSpec(memory_space=pltpu.VMEM)
SMEM = pl.BlockSpec(memory_space=pltpu.SMEM)
HBM = pl.BlockSpec(memory_space=pltpu.HBM)


def dot(a, b, dims):
    return lax.dot_general(a, b, (dims, ((), ())), preferred_element_type=F32)


def hbm(x):
    return pltpu.with_memory_space_constraint(x, pltpu.HBM)


def cost(flops, nbytes, trans=0):
    return pl.CostEstimate(flops=int(flops), bytes_accessed=int(nbytes), transcendentals=int(trans))


def pick_into(outs, cap, here, me, holder, reads_ref, keys_ref, values_ref):
    for k, out in enumerate(outs):
        for r in range(cap):
            block = reads_ref[me ^ k, cap * holder + r] - here * holder
            rows = pl.ds(pl.multiple_of(block * PBLK, PBLK), PBLK)
            out[r * PBLK:(r + 1) * PBLK, :HD] = keys_ref[rows, :]
            out[r * PBLK:(r + 1) * PBLK, HD:] = values_ref[rows, :]


def pick_kernel(cap, here, me_ref, reads_hbm, keys_hbm, values_hbm, *refs):
    outs, (kept_ref, reads_ref, keys_ref, values_ref, sems) = refs[:-5], refs[-5:]
    copies = [
        pltpu.make_async_copy(src, dst, sems.at[i])
        for i, (src, dst) in enumerate(
            ((reads_hbm, reads_ref), (keys_hbm, keys_ref), (values_hbm, values_ref), (reads_hbm, kept_ref)))
    ]
    for copy in copies:
        copy.start()
    for copy in copies:
        copy.wait()
    me = me_ref[0]
    pick_into(outs, cap, here, me, me, reads_ref, keys_ref, values_ref)


def pick_far_kernel(cap, here, flip, me_ref, reads_ref, keys_ref, values_ref, *outs):
    me = me_ref[0]
    pick_into(outs, cap, here, me, me ^ flip, reads_ref, keys_ref, values_ref)


def place_kernel(n, cap, here, me_ref, reads_ref, *refs):
    parts, keys_ref, values_ref = refs[:n], refs[n], refs[n + 1]
    me = me_ref[0]
    keys_ref[...] = jnp.zeros_like(keys_ref)
    values_ref[...] = jnp.zeros_like(values_ref)
    for k in range(n):
        for r in range(cap):
            block = reads_ref[me ^ k, cap * me + r] - here * me
            rows = pl.ds(pl.multiple_of(block * PBLK, PBLK), PBLK)
            piece = parts[k][r * PBLK:(r + 1) * PBLK, :].astype(F32)
            keys_ref[rows, :] += piece[:, :HD]
            values_ref[rows, :] += piece[:, HD:]


def weight_copies(i, me, width, hbms, bufs, slot, sems):
    rows = pl.ds(pl.multiple_of((me ^ i) * width, width), width)
    return [pltpu.make_async_copy(w.at[rows], buf.at[slot], sems.at[j, slot]) for j, (w, buf) in enumerate(zip(hbms, bufs))]


def kv_kernel(order, rest, me_ref, own_hbm, *refs):
    hidden, (wk_hbm, wv_hbm, q_hbm, k_ref, v_ref, q_ref, restk_ref, restv_ref) = refs[:-13], refs[-13:-5]
    own_ref, wk_ref, wv_ref, sems, far_sems = refs[-5:]
    me = me_ref[0]
    width = own_ref.shape[1]

    def fetch(slot, i):
        return weight_copies(i, me, width, (wk_hbm, wv_hbm), (wk_ref, wv_ref), slot, sems)

    for slot, i in enumerate(order):
        for copy in fetch(slot, i):
            copy.start()
    own = pltpu.make_async_copy(own_hbm, own_ref, far_sems.at[0])
    own.start()
    later = [pltpu.make_async_copy(q_hbm, q_ref, far_sems.at[1])]
    for slot, i in enumerate(rest):
        rows = pl.ds(pl.multiple_of((me ^ i) * width, width), width)
        later.append(pltpu.make_async_copy(wk_hbm.at[rows], restk_ref.at[slot], far_sems.at[2 + 2 * slot]))
        later.append(pltpu.make_async_copy(wv_hbm.at[rows], restv_ref.at[slot], far_sems.at[3 + 2 * slot]))
    for copy in later:
        copy.start()
    new_k = jnp.zeros(k_ref.shape, F32)
    new_v = jnp.zeros(k_ref.shape, F32)
    for slot, i in enumerate(order):
        for copy in fetch(slot, i):
            copy.wait()
        if i == 0:
            own.wait()
        piece = hidden[i - 1][...] if i else own_ref[...]
        new_k += dot(piece, wk_ref[slot], ((1,), (0,)))
        new_v += dot(piece, wv_ref[slot], ((1,), (0,)))
    k_ref[...] = new_k
    v_ref[...] = new_v
    for copy in later:
        copy.wait()


def forward_kernel(n_rest, n_pre, scaling, wk_ref, wv_ref, *refs):
    hidden, (q_ref, partk_ref, partv_ref), refs = refs[:n_rest], refs[n_rest:n_rest + 3], refs[n_rest + 3:]
    prefix = refs[:n_pre]
    ctx_ref, exps_ref, row_ref, v_all, k_all, vt_all, s_buf, sums = refs[n_pre:]
    length = q_ref.shape[0]
    heads = q_ref.shape[1] // HD
    factor = scaling * LOG2E
    at = 0
    for ref in prefix:
        size = ref.shape[0]
        k_all[at:at + size, :] = ref[:, :HD]
        v_all[at:at + size, :] = ref[:, HD:]
        at += size
    new_k, new_v = partk_ref[...], partv_ref[...]
    for slot, ref in enumerate(hidden):
        new_k += dot(ref[...], wk_ref[slot], ((1,), (0,)))
        new_v += dot(ref[...], wv_ref[slot], ((1,), (0,)))
    k_all[at:, :] = new_k.astype(BF16)
    v_all[at:, :] = new_v.astype(BF16)
    vt_all[...] = v_all[...].astype(F32).T.astype(BF16)
    visible = lax.broadcasted_iota(jnp.int32, (length, length), 0) <= lax.broadcasted_iota(
        jnp.int32, (length, length), 1)

    def scores(h):
        qh = q_ref[:, h * HD:(h + 1) * HD]
        s = dot(k_all[:at, :], qh, ((1,), (1,)))
        s_buf[h % 2, :at, :] = s
        peak = jnp.max(s, axis=0, keepdims=True)
        s = jnp.where(visible, dot(k_all[at:, :], qh, ((1,), (1,))), -jnp.inf)
        s_buf[h % 2, at:, :] = s
        return jnp.maximum(peak, jnp.max(s, axis=0, keepdims=True))

    def finish(h, peak):
        lanes = slice(h * length, (h + 1) * length)
        total = jnp.zeros((1, length), F32)
        step = length // 2
        for start in range(0, at + length, step):
            e = jnp.exp2((s_buf[h % 2, start:start + step, :] - peak) * factor)
            total += jnp.sum(e, axis=0, keepdims=True)
            exps_ref[start:start + step, lanes] = e.astype(BF16)
        inverse = 1.0 / total
        sums[h:h + 1, :] = inverse
        ctx_t = dot(vt_all[...], exps_ref[:, lanes], ((1,), (0,))) * inverse
        ctx_ref[:, h * HD:(h + 1) * HD] = ctx_t.T.astype(BF16)

    peak = scores(0)
    for h in range(heads):
        later = scores(h + 1) if h + 1 < heads else None
        finish(h, peak)
        peak = later
    row_ref[:heads, :] = sums[:heads, :]


def project_kernel(order, me_ref, ctx_ref, w_ref, *outs):
    me = me_ref[0]
    width = outs[0].shape[1]
    ctx = ctx_ref[...]
    for i, out in zip(order, outs):
        cols = pl.ds(pl.multiple_of((me ^ i) * width, 128), width)
        out[...] = dot(ctx, w_ref[:, cols], ((1,), (0,))).astype(BF16)


def grad_kernel(order, me_ref, w_ref, *refs):
    grads, out = refs[:-1], refs[-1]
    me = me_ref[0]
    width = grads[0].shape[1]
    total = jnp.zeros(out.shape, F32)
    for i, grad in zip(order, grads):
        cols = pl.ds(pl.multiple_of((me ^ i) * width, 128), width)
        total += dot(w_ref[:, cols], grad[...], ((1,), (1,)))
    out[...] = total


def backward_kernel(last, n_pre, scaling, me_ref, w_ref, part_ref, grad_ref, q_ref, v_all, exps_ref, row_ref, *refs):
    outs = refs[:n_pre]
    gt_all, q_all, dbuf, slopes = refs[n_pre:]
    me = me_ref[0]
    length, width = grad_ref.shape
    heads = q_ref.shape[1] // HD
    cols = pl.ds(pl.multiple_of((me ^ last) * width, 128), width)
    total = part_ref[...] + dot(w_ref[:, cols], grad_ref[...], ((1,), (1,)))
    for h in range(heads):
        lanes = slice(h * length, (h + 1) * length)
        q_all[lanes, :] = q_ref[:, h * HD:(h + 1) * HD]
        gt_all[:, lanes] = (total[h * HD:(h + 1) * HD, :] * row_ref[h:h + 1, :]).astype(BF16)
    n_rows = dbuf.shape[0]

    def slope(h):
        lanes = slice(h * length, (h + 1) * length)
        s = dot(v_all[...], gt_all[:, lanes], ((1,), (0,)))
        slopes[h % 2] = s[:n_rows]
        delta = jnp.sum(exps_ref[:, lanes].astype(F32) * s, axis=0, keepdims=True)
        return delta * row_ref[h:h + 1, :]

    def finish(h, delta):
        lanes = slice(h * length, (h + 1) * length)
        step = length // 2
        for start in range(0, n_rows, step):
            e = exps_ref[start:start + step, lanes].astype(F32)
            dbuf[start:start + step, lanes] = (e * (slopes[h % 2, start:start + step, :] - delta)).astype(BF16)

    delta = slope(0)
    for h in range(heads):
        later = slope(h + 1) if h + 1 < heads else None
        finish(h, delta)
        delta = later
    value_grad = dot(exps_ref[:n_rows, :], gt_all[...], ((1,), (1,)))
    key_grad = dot(dbuf[...], q_all[...], ((1,), (0,))) * scaling
    at = 0
    for out in outs:
        size = out.shape[0]
        out[:, HD:] = value_grad[at:at + size].astype(out.dtype)
        out[:, :HD] = key_grad[at:at + size].astype(out.dtype)
        at += size


def local(hidden_states, queries, key_weight, value_weight, output_weight, prefix_keys, prefix_values, reads, out_grad):
    length, width = hidden_states.shape
    scaling = HD ** (-0.5)
    heads = queries.shape[1] // HD
    n_tp = lax.axis_size("tp")
    n_seq = lax.axis_size("seq")
    here = prefix_keys.shape[0] // PBLK
    read_count = reads.shape[1]
    cap = max(1, read_count // n_seq)
    dense = cap * n_seq == read_count and n_seq & (n_seq - 1) == 0 and here * n_seq % read_count == 0
    me_tp = lax.axis_index("tp").astype(jnp.int32).reshape(1)
    me_seq = lax.axis_index("seq").astype(jnp.int32).reshape(1)
    n_rows = read_count * PBLK
    keys = n_rows + length

    def hop(x, axis, k):
        n = n_tp if axis == "tp" else n_seq
        return lax.ppermute(x, axis, [(i, i ^ k) for i in range(n)])

    def grant(mib):
        return pltpu.CompilerParams(vmem_limit_bytes=mib * 2 ** 20)

    near_grad = hop(out_grad, "tp", 1)
    far_grad = hop(out_grad, "tp", 2)
    near_hidden = hop(hidden_states, "tp", 1)
    far_hidden = hop(hidden_states, "tp", 2)
    last_hidden = hop(far_hidden, "tp", 1)
    last_grad = hop(far_grad, "tp", 1)
    far_first = sorted(range(1, n_seq), key=lambda k: (-(k // 4), k & 1, -k))

    if dense:
        shape = jax.ShapeDtypeStruct((cap * PBLK, 2 * HD), BF16)
        half = max(1, n_seq // 2)
        out_types = [shape] * half
        far_keys = hop(prefix_keys, "seq", half)
        far_values = hop(prefix_values, "seq", half)
        *picked, kept_reads = pl.pallas_call(
            functools.partial(pick_kernel, cap, here),
            out_shape=out_types + [jax.ShapeDtypeStruct(reads.shape, jnp.int32)],
            in_specs=[SMEM, HBM, HBM, HBM],
            out_specs=[VMEM] * (half + 1),
            scratch_shapes=[
                pltpu.SMEM(reads.shape, jnp.int32),
                pltpu.VMEM(prefix_keys.shape, BF16),
                pltpu.VMEM(prefix_keys.shape, BF16),
                pltpu.SemaphoreType.DMA((4,)),
            ],
            cost_estimate=cost(0, 2 ** 20),
            compiler_params=grant(4),
            name="pick",
        )(me_seq, hbm(reads), hbm(prefix_keys), hbm(prefix_values))
        picked_far = pl.pallas_call(
            functools.partial(pick_far_kernel, cap, here, half),
            out_shape=out_types,
            in_specs=[SMEM, SMEM, VMEM, VMEM],
            out_specs=[VMEM] * half,
            cost_estimate=cost(0, 2 ** 20),
            compiler_params=grant(4),
            name="pick_far",
        )(me_seq, kept_reads, far_keys, far_values)
        prefix = [picked[0]] + [hop(picked[k], "seq", k) for k in range(1, half)]
        prefix += [picked_far[0]] + [hop(picked_far[k], "seq", k) for k in range(1, half)]
    else:
        flat = PBLK * 2 * HD
        local_cache = jnp.concatenate([prefix_keys, prefix_values], axis=1).reshape(here, flat)
        own = me_seq[0]
        owners = reads // here
        slot_here = reads % here
        earlier = jnp.arange(read_count)[None, :] < jnp.arange(read_count)[:, None]
        ranks = jnp.sum((owners[:, :, None] == owners[:, None, :]) & earlier[None], axis=2)
        slots = jnp.arange(cap, dtype=jnp.int32)
        picker = jnp.sum(
            ((owners == own)[:, :, None, None]
             & (ranks[:, :, None, None] == slots[None, None, :, None])
             & (slot_here[:, :, None, None] == jnp.arange(here, dtype=jnp.int32))).astype(F32), axis=1)
        outgoing = jnp.einsum("dcb,bf->dcf", picker.astype(BF16), local_cache, preferred_element_type=F32).astype(BF16)
        incoming = lax.all_to_all(outgoing, "seq", split_axis=0, concat_axis=0, tiled=True)
        my_owner, my_rank = owners[own], ranks[own]
        fetched = jnp.take(incoming.reshape(n_seq * cap, flat), my_owner * cap + my_rank, axis=0)
        prefix = [fetched.reshape(n_rows, 2 * HD)]
    n_pre = len(prefix)

    part = jax.ShapeDtypeStruct((length, HD), F32)
    n_rest = n_tp - 3
    weight = jax.ShapeDtypeStruct((n_rest, width, HD), BF16)
    part_k, part_v, q, rest_k, rest_v = pl.pallas_call(
        functools.partial(kv_kernel, (1, 0, 2), tuple(range(3, n_tp))),
        out_shape=[part, part, jax.ShapeDtypeStruct(queries.shape, BF16), weight, weight],
        in_specs=[SMEM, HBM, VMEM, VMEM] + [HBM] * 3,
        out_specs=[VMEM] * 5,
        scratch_shapes=[
            pltpu.VMEM((length, width), BF16),
            pltpu.VMEM((3, width, HD), BF16),
            pltpu.VMEM((3, width, HD), BF16),
            pltpu.SemaphoreType.DMA((2, 3)),
            pltpu.SemaphoreType.DMA((2 + 2 * n_rest,)),
        ],
        compiler_params=grant(8),
        cost_estimate=cost(4e8, 3e6),
        name="kv",
    )(me_tp, hbm(hidden_states), near_hidden, far_hidden, hbm(key_weight), hbm(value_weight), hbm(queries))

    ctx, exps, row, v_all = pl.pallas_call(
        functools.partial(forward_kernel, n_rest, n_pre, scaling),
        out_shape=[
            jax.ShapeDtypeStruct((length, heads * HD), BF16),
            jax.ShapeDtypeStruct((keys, heads * length), BF16),
            jax.ShapeDtypeStruct((heads + (-heads) % 8, length), F32),
            jax.ShapeDtypeStruct((keys, HD), BF16),
        ],
        in_specs=[VMEM] * (5 + n_rest + n_pre),
        out_specs=[VMEM] * 4,
        scratch_shapes=[
            pltpu.VMEM((keys, HD), BF16),
            pltpu.VMEM((HD, keys), BF16),
            pltpu.VMEM((2, keys, length), F32),
            pltpu.VMEM((heads + (-heads) % 8, length), F32),
        ],
        compiler_params=grant(20),
        cost_estimate=cost(5e9, 1e7, 3e6),
        name="forward",
    )(rest_k, rest_v, last_hidden, q, part_k, part_v, *prefix)

    part_grad = pl.pallas_call(
        functools.partial(grad_kernel, (0, 1, 2)),
        out_shape=jax.ShapeDtypeStruct((heads * HD, length), F32),
        in_specs=[SMEM] + [VMEM] * 4,
        out_specs=VMEM,
        compiler_params=grant(16),
        cost_estimate=cost(1.5e9, 8e6),
        name="grad",
    )(me_tp, output_weight, out_grad, near_grad, far_grad)

    def project(order):
        return pl.pallas_call(
            functools.partial(project_kernel, order),
            out_shape=[jax.ShapeDtypeStruct((length, width), BF16)] * len(order),
            in_specs=[SMEM, VMEM, VMEM],
            out_specs=[VMEM] * len(order),
            compiler_params=grant(16),
            cost_estimate=cost(5e8 * len(order), 2e6 * len(order)),
        )(me_tp, ctx, output_weight)

    share3, share2 = project((3, 2))
    near3 = hop(share3, "tp", 1)
    share1, share0 = project((1, 0))
    near1 = hop(share1, "tp", 1)
    cross = (share2.astype(F32) + near3.astype(F32)).astype(BF16)
    across = hop(cross, "tp", 2)
    layer_output = (share0.astype(F32) + near1.astype(F32) + across.astype(F32)).astype(BF16)

    grad_type = BF16 if dense else F32
    parts = pl.pallas_call(
        functools.partial(backward_kernel, n_tp - 1, n_pre, scaling),
        out_shape=[jax.ShapeDtypeStruct(x.shape, grad_type) for x in prefix],
        in_specs=[SMEM] + [VMEM] * 7,
        out_specs=[VMEM] * n_pre,
        scratch_shapes=[
            pltpu.VMEM((HD, heads * length), BF16),
            pltpu.VMEM((heads * length, HD), BF16),
            pltpu.VMEM((n_rows, heads * length), BF16),
            pltpu.VMEM((2, n_rows, length), F32),
        ],
        compiler_params=grant(32),
        cost_estimate=cost(7e9, 1e7),
        name="backward",
    )(me_tp, output_weight, part_grad, last_grad, q, v_all, exps, row)

    if dense:
        back = {k: hop(parts[k], "seq", k) for k in far_first}
        returned = [parts[0]] + [back[k] for k in range(1, n_seq)]
        shape = jax.ShapeDtypeStruct(prefix_keys.shape, F32)
        key_grad, value_grad = pl.pallas_call(
            functools.partial(place_kernel, n_seq, cap, here),
            out_shape=[shape] * 2,
            in_specs=[SMEM, SMEM] + [VMEM] * n_seq,
            out_specs=[VMEM] * 2,
            cost_estimate=cost(0, 2 ** 20),
            compiler_params=grant(4),
            name="place",
        )(me_seq, kept_reads, *returned)
    else:
        cache_grads = parts[0].reshape(read_count, flat)
        placer = ((my_owner[None, None, :] == jnp.arange(n_seq, dtype=jnp.int32)[:, None, None])
                  & (my_rank[None, None, :] == slots[None, :, None])).astype(F32)
        leaving = jnp.einsum("ocr,rf->ocf", placer, cache_grads, precision=lax.Precision.HIGHEST)
        back = lax.all_to_all(leaving.astype(BF16), "seq", split_axis=0, concat_axis=0, tiled=True).astype(F32)
        summed = jnp.einsum("dcb,dcf->bf", picker, back, precision=lax.Precision.HIGHEST).reshape(here * PBLK, 2 * HD)
        key_grad, value_grad = summed[:, :HD], summed[:, HD:]
    return layer_output, key_grad, value_grad


def solution(mesh):
    in_specs = (P("seq", "tp"), P("seq", "tp"), P(None, "tp"), P(None, "tp"), P("tp", None),
                P("seq", "tp"), P("seq", "tp"), P(), P("seq", "tp"))
    out_specs = (P("seq", "tp"), P("seq", "tp"), P("seq", "tp"))
    return jax.shard_map(local, mesh=mesh, in_specs=in_specs, out_specs=out_specs, check_vma=False)
```

```python
import functools

import jax
import jax.numpy as jnp
from jax import lax
from jax.experimental import pallas as pl
from jax.experimental.pallas import tpu as pltpu
from jax.sharding import PartitionSpec as P


HD = 128
PBLK = 64
LOG2E = 1.4426950408889634
F32 = jnp.float32
BF16 = jnp.bfloat16
VMEM = pl.BlockSpec(memory_space=pltpu.VMEM)
SMEM = pl.BlockSpec(memory_space=pltpu.SMEM)
HBM = pl.BlockSpec(memory_space=pltpu.HBM)


def dot(a, b, dims):
    return lax.dot_general(a, b, (dims, ((), ())), preferred_element_type=F32)


def hbm(x):
    return pltpu.with_memory_space_constraint(x, pltpu.HBM)


def cost(flops, nbytes, trans=0):
    return pl.CostEstimate(flops=int(flops), bytes_accessed=int(nbytes), transcendentals=int(trans))


def pick_kernel(n, cap, here, me_ref, reads_hbm, keys_hbm, values_hbm, *refs):
    outs, (reads_ref, keys_ref, values_ref, sems) = refs[:n], refs[n:]
    me = me_ref[0]
    copies = [
        pltpu.make_async_copy(src, dst, sems.at[i])
        for i, (src, dst) in enumerate(
            ((reads_hbm, reads_ref), (keys_hbm, keys_ref), (values_hbm, values_ref)))
    ]
    for copy in copies:
        copy.start()
    for copy in copies:
        copy.wait()
    for k in range(n):
        for r in range(cap):
            block = reads_ref[me ^ k, cap * me + r] - here * me
            rows = pl.ds(pl.multiple_of(block * PBLK, PBLK), PBLK)
            outs[k][r * PBLK:(r + 1) * PBLK, :HD] = keys_ref[rows, :]
            outs[k][r * PBLK:(r + 1) * PBLK, HD:] = values_ref[rows, :]


def place_kernel(n, cap, here, me_ref, reads_ref, *refs):
    parts, keys_ref, values_ref = refs[:n], refs[n], refs[n + 1]
    me = me_ref[0]
    keys_ref[...] = jnp.zeros_like(keys_ref)
    values_ref[...] = jnp.zeros_like(values_ref)
    for k in range(n):
        for r in range(cap):
            block = reads_ref[me ^ k, cap * me + r] - here * me
            rows = pl.ds(pl.multiple_of(block * PBLK, PBLK), PBLK)
            piece = parts[k][r * PBLK:(r + 1) * PBLK, :].astype(F32)
            keys_ref[rows, :] += piece[:, :HD]
            values_ref[rows, :] += piece[:, HD:]


def weight_copies(i, me, width, hbms, bufs, slot, sems):
    rows = pl.ds(pl.multiple_of((me ^ i) * width, width), width)
    return [pltpu.make_async_copy(w.at[rows], buf.at[slot], sems.at[j, slot]) for j, (w, buf) in enumerate(zip(hbms, bufs))]


def kv_kernel(order, last, me_ref, own_hbm, *refs):
    hidden, (wk_hbm, wv_hbm, q_hbm, k_ref, v_ref, q_ref, lastk_ref, lastv_ref) = refs[:-13], refs[-13:-5]
    own_ref, wk_ref, wv_ref, sems, far_sems = refs[-5:]
    me = me_ref[0]
    width = own_ref.shape[1]

    def fetch(slot, i):
        return weight_copies(i, me, width, (wk_hbm, wv_hbm), (wk_ref, wv_ref), slot, sems)

    for slot, i in enumerate(order):
        for copy in fetch(slot, i):
            copy.start()
    own = pltpu.make_async_copy(own_hbm, own_ref, far_sems.at[0])
    own.start()
    rows = pl.ds(pl.multiple_of((me ^ last) * width, width), width)
    later = [
        pltpu.make_async_copy(q_hbm, q_ref, far_sems.at[1]),
        pltpu.make_async_copy(wk_hbm.at[rows], lastk_ref, far_sems.at[2]),
        pltpu.make_async_copy(wv_hbm.at[rows], lastv_ref, far_sems.at[3]),
    ]
    for copy in later:
        copy.start()
    new_k = jnp.zeros(k_ref.shape, F32)
    new_v = jnp.zeros(k_ref.shape, F32)
    for slot, i in enumerate(order):
        for copy in fetch(slot, i):
            copy.wait()
        if i == 0:
            own.wait()
        piece = hidden[i - 1][...] if i else own_ref[...]
        new_k += dot(piece, wk_ref[slot], ((1,), (0,)))
        new_v += dot(piece, wv_ref[slot], ((1,), (0,)))
    k_ref[...] = new_k
    v_ref[...] = new_v
    for copy in later:
        copy.wait()


def forward_kernel(n_pre, scaling, wk_ref, wv_ref, hidden_ref, q_ref, partk_ref, partv_ref, *refs):
    prefix = refs[:n_pre]
    ctx_ref, exps_ref, row_ref, v_all, k_all, vt_all, s_buf, sums = refs[n_pre:]
    length = hidden_ref.shape[0]
    heads = q_ref.shape[1] // HD
    factor = scaling * LOG2E
    at = 0
    for ref in prefix:
        size = ref.shape[0]
        k_all[at:at + size, :] = ref[:, :HD]
        v_all[at:at + size, :] = ref[:, HD:]
        at += size
    piece = hidden_ref[...]
    k_all[at:, :] = (partk_ref[...] + dot(piece, wk_ref[...], ((1,), (0,)))).astype(BF16)
    v_all[at:, :] = (partv_ref[...] + dot(piece, wv_ref[...], ((1,), (0,)))).astype(BF16)
    vt_all[...] = v_all[...].astype(F32).T.astype(BF16)
    visible = lax.broadcasted_iota(jnp.int32, (length, length), 0) <= lax.broadcasted_iota(
        jnp.int32, (length, length), 1)

    def scores(h):
        qh = q_ref[:, h * HD:(h + 1) * HD]
        s = dot(k_all[:at, :], qh, ((1,), (1,)))
        s_buf[h % 2, :at, :] = s
        peak = jnp.max(s, axis=0, keepdims=True)
        s = jnp.where(visible, dot(k_all[at:, :], qh, ((1,), (1,))), -jnp.inf)
        s_buf[h % 2, at:, :] = s
        return jnp.maximum(peak, jnp.max(s, axis=0, keepdims=True))

    def finish(h, peak):
        lanes = slice(h * length, (h + 1) * length)
        total = jnp.zeros((1, length), F32)
        step = length // 2
        for start in range(0, at + length, step):
            e = jnp.exp2((s_buf[h % 2, start:start + step, :] - peak) * factor)
            total += jnp.sum(e, axis=0, keepdims=True)
            exps_ref[start:start + step, lanes] = e.astype(BF16)
        inverse = 1.0 / total
        sums[h:h + 1, :] = inverse
        ctx_t = dot(vt_all[...], exps_ref[:, lanes], ((1,), (0,))) * inverse
        ctx_ref[:, h * HD:(h + 1) * HD] = ctx_t.T.astype(BF16)

    peak = scores(0)
    for h in range(heads):
        later = scores(h + 1) if h + 1 < heads else None
        finish(h, peak)
        peak = later
    row_ref[:heads, :] = sums[:heads, :]


def project_kernel(order, me_ref, ctx_ref, w_ref, *outs):
    me = me_ref[0]
    width = outs[0].shape[1]
    ctx = ctx_ref[...]
    for i, out in zip(order, outs):
        cols = pl.ds(pl.multiple_of((me ^ i) * width, 128), width)
        out[...] = dot(ctx, w_ref[:, cols], ((1,), (0,))).astype(BF16)


def grad_kernel(order, me_ref, w_ref, *refs):
    grads, out = refs[:-1], refs[-1]
    me = me_ref[0]
    width = grads[0].shape[1]
    total = jnp.zeros(out.shape, F32)
    for i, grad in zip(order, grads):
        cols = pl.ds(pl.multiple_of((me ^ i) * width, 128), width)
        total += dot(w_ref[:, cols], grad[...], ((1,), (1,)))
    out[...] = total


def give(outs, start, probs_ref, slopes_ref, gt_ref, q_ref, scaling):
    stop = start + sum(out.shape[0] for out in outs)
    value_grad = dot(probs_ref[start:stop, :], gt_ref[...], ((1,), (1,)))
    key_grad = dot(slopes_ref[start:stop, :], q_ref[...], ((1,), (0,))) * scaling
    at = 0
    for out in outs:
        size = out.shape[0]
        out[:, HD:] = value_grad[at:at + size].astype(out.dtype)
        out[:, :HD] = key_grad[at:at + size].astype(out.dtype)
        at += size


def near_kernel(scaling, exps_ref, dbuf, gt_all, q_all, *outs):
    give(outs, 0, exps_ref, dbuf, gt_all, q_all, scaling)


def backward_kernel(last, n_pre, scaling, me_ref, w_ref, part_ref, grad_ref, q_ref, v_all, exps_ref, row_ref, *refs):
    outs, (gt_all, q_all, dbuf, slopes) = refs[:n_pre], refs[n_pre:]
    me = me_ref[0]
    length, width = grad_ref.shape
    heads = q_ref.shape[1] // HD
    cols = pl.ds(pl.multiple_of((me ^ last) * width, 128), width)
    total = part_ref[...] + dot(w_ref[:, cols], grad_ref[...], ((1,), (1,)))
    for h in range(heads):
        lanes = slice(h * length, (h + 1) * length)
        q_all[lanes, :] = q_ref[:, h * HD:(h + 1) * HD]
        gt_all[:, lanes] = (total[h * HD:(h + 1) * HD, :] * row_ref[h:h + 1, :]).astype(BF16)
    n_rows = dbuf.shape[0]

    def slope(h):
        lanes = slice(h * length, (h + 1) * length)
        s = dot(v_all[...], gt_all[:, lanes], ((1,), (0,)))
        slopes[h % 2] = s[:n_rows]
        delta = jnp.sum(exps_ref[:, lanes].astype(F32) * s, axis=0, keepdims=True)
        return delta * row_ref[h:h + 1, :]

    def finish(h, delta):
        lanes = slice(h * length, (h + 1) * length)
        step = length // 2
        for start in range(0, n_rows, step):
            e = exps_ref[start:start + step, lanes].astype(F32)
            dbuf[start:start + step, lanes] = (e * (slopes[h % 2, start:start + step, :] - delta)).astype(BF16)

    delta = slope(0)
    for h in range(heads):
        later = slope(h + 1) if h + 1 < heads else None
        finish(h, delta)
        delta = later
    give(outs, n_rows - sum(out.shape[0] for out in outs), exps_ref, dbuf, gt_all, q_all, scaling)


def local(hidden_states, queries, key_weight, value_weight, output_weight, prefix_keys, prefix_values, reads, out_grad):
    length, width = hidden_states.shape
    scaling = HD ** (-0.5)
    heads = queries.shape[1] // HD
    n_tp = lax.axis_size("tp")
    n_seq = lax.axis_size("seq")
    here = prefix_keys.shape[0] // PBLK
    read_count = reads.shape[1]
    cap = max(1, read_count // n_seq)
    dense = cap * n_seq == read_count and n_seq & (n_seq - 1) == 0 and here * n_seq % read_count == 0
    me_tp = lax.axis_index("tp").astype(jnp.int32).reshape(1)
    me_seq = lax.axis_index("seq").astype(jnp.int32).reshape(1)
    n_rows = read_count * PBLK
    keys = n_rows + length

    def hop(x, axis, k):
        n = n_tp if axis == "tp" else n_seq
        return lax.ppermute(x, axis, [(i, i ^ k) for i in range(n)])

    def grant(mib):
        return pltpu.CompilerParams(vmem_limit_bytes=mib * 2 ** 20)

    near_grad = hop(out_grad, "tp", 1)
    far_grad = hop(out_grad, "tp", 2)
    near_hidden = hop(hidden_states, "tp", 1)
    far_hidden = hop(hidden_states, "tp", 2)
    last_hidden = hop(far_hidden, "tp", 1)
    last_grad = hop(far_grad, "tp", 1)
    far_first = sorted(range(1, n_seq), key=lambda k: (-(k // 4), k & 1, -k))

    if dense:
        shape = jax.ShapeDtypeStruct((cap * PBLK, 2 * HD), BF16)
        picked = pl.pallas_call(
            functools.partial(pick_kernel, n_seq, cap, here),
            out_shape=[shape] * n_seq,
            in_specs=[SMEM, HBM, HBM, HBM],
            out_specs=[VMEM] * n_seq,
            scratch_shapes=[
                pltpu.SMEM(reads.shape, jnp.int32),
                pltpu.VMEM(prefix_keys.shape, BF16),
                pltpu.VMEM(prefix_keys.shape, BF16),
                pltpu.SemaphoreType.DMA((3,)),
            ],
            cost_estimate=cost(0, 2 ** 20),
            compiler_params=grant(4),
            name="pick",
        )(me_seq, hbm(reads), hbm(prefix_keys), hbm(prefix_values))
        moved = {k: hop(picked[k], "seq", k) for k in far_first}
        prefix = [picked[0]] + [moved[k] for k in range(1, n_seq)]
    else:
        flat = PBLK * 2 * HD
        local_cache = jnp.concatenate([prefix_keys, prefix_values], axis=1).reshape(here, flat)
        own = me_seq[0]
        owners = reads // here
        slot_here = reads % here
        earlier = jnp.arange(read_count)[None, :] < jnp.arange(read_count)[:, None]
        ranks = jnp.sum((owners[:, :, None] == owners[:, None, :]) & earlier[None], axis=2)
        slots = jnp.arange(cap, dtype=jnp.int32)
        picker = jnp.sum(
            ((owners == own)[:, :, None, None]
             & (ranks[:, :, None, None] == slots[None, None, :, None])
             & (slot_here[:, :, None, None] == jnp.arange(here, dtype=jnp.int32))).astype(F32), axis=1)
        outgoing = jnp.einsum("dcb,bf->dcf", picker.astype(BF16), local_cache, preferred_element_type=F32).astype(BF16)
        incoming = lax.all_to_all(outgoing, "seq", split_axis=0, concat_axis=0, tiled=True)
        my_owner, my_rank = owners[own], ranks[own]
        fetched = jnp.take(incoming.reshape(n_seq * cap, flat), my_owner * cap + my_rank, axis=0)
        prefix = [fetched.reshape(n_rows, 2 * HD)]
    n_pre = len(prefix)

    part = jax.ShapeDtypeStruct((length, HD), F32)
    weight = jax.ShapeDtypeStruct((width, HD), BF16)
    part_k, part_v, q, last_k, last_v = pl.pallas_call(
        functools.partial(kv_kernel, (1, 0, 2), n_tp - 1),
        out_shape=[part, part, jax.ShapeDtypeStruct(queries.shape, BF16), weight, weight],
        in_specs=[SMEM, HBM] + [VMEM] * (n_tp - 2) + [HBM] * 3,
        out_specs=[VMEM] * 5,
        scratch_shapes=[
            pltpu.VMEM((length, width), BF16),
            pltpu.VMEM((n_tp - 1, width, HD), BF16),
            pltpu.VMEM((n_tp - 1, width, HD), BF16),
            pltpu.SemaphoreType.DMA((2, n_tp - 1)),
            pltpu.SemaphoreType.DMA((4,)),
        ],
        compiler_params=grant(8),
        cost_estimate=cost(4e8, 3e6),
        name="kv",
    )(me_tp, hbm(hidden_states), near_hidden, far_hidden, hbm(key_weight), hbm(value_weight), hbm(queries))

    ctx, exps, row, v_all = pl.pallas_call(
        functools.partial(forward_kernel, n_pre, scaling),
        out_shape=[
            jax.ShapeDtypeStruct((length, heads * HD), BF16),
            jax.ShapeDtypeStruct((keys, heads * length), BF16),
            jax.ShapeDtypeStruct((heads + (-heads) % 8, length), F32),
            jax.ShapeDtypeStruct((keys, HD), BF16),
        ],
        in_specs=[VMEM] * (6 + n_pre),
        out_specs=[VMEM] * 4,
        scratch_shapes=[
            pltpu.VMEM((keys, HD), BF16),
            pltpu.VMEM((HD, keys), BF16),
            pltpu.VMEM((2, keys, length), F32),
            pltpu.VMEM((heads + (-heads) % 8, length), F32),
        ],
        compiler_params=grant(20),
        cost_estimate=cost(5e9, 1e7, 3e6),
        name="forward",
    )(last_k, last_v, last_hidden, q, part_k, part_v, *prefix)

    part_grad = pl.pallas_call(
        functools.partial(grad_kernel, (0, 1, 2)),
        out_shape=jax.ShapeDtypeStruct((heads * HD, length), F32),
        in_specs=[SMEM] + [VMEM] * 4,
        out_specs=VMEM,
        compiler_params=grant(16),
        cost_estimate=cost(1.5e9, 8e6),
        name="grad",
    )(me_tp, output_weight, out_grad, near_grad, far_grad)

    def project(order):
        return pl.pallas_call(
            functools.partial(project_kernel, order),
            out_shape=[jax.ShapeDtypeStruct((length, width), BF16)] * len(order),
            in_specs=[SMEM, VMEM, VMEM],
            out_specs=[VMEM] * len(order),
            compiler_params=grant(16),
            cost_estimate=cost(5e8 * len(order), 2e6 * len(order)),
        )(me_tp, ctx, output_weight)

    share3, share2 = project((3, 2))
    near3 = hop(share3, "tp", 1)
    share1, share0 = project((1, 0))
    near1 = hop(share1, "tp", 1)
    cross = (share2.astype(F32) + near3.astype(F32)).astype(BF16)
    across = hop(cross, "tp", 2)
    layer_output = (share0.astype(F32) + near1.astype(F32) + across.astype(F32)).astype(BF16)

    grad_type = BF16 if dense else F32
    types = [jax.ShapeDtypeStruct(x.shape, grad_type) for x in prefix]
    n_near = n_pre // 2
    n_far = n_pre - n_near
    *far_parts, gt, q_rows, slopes = pl.pallas_call(
        functools.partial(backward_kernel, n_tp - 1, n_far, scaling),
        out_shape=types[n_near:] + [
            jax.ShapeDtypeStruct((HD, heads * length), BF16),
            jax.ShapeDtypeStruct((heads * length, HD), BF16),
            jax.ShapeDtypeStruct((n_rows, heads * length), BF16),
        ],
        in_specs=[SMEM] + [VMEM] * 7,
        out_specs=[VMEM] * (n_far + 3),
        scratch_shapes=[pltpu.VMEM((2, n_rows, length), F32)],
        compiler_params=grant(28),
        cost_estimate=cost(6e9, 1e7),
        name="backward",
    )(me_tp, output_weight, part_grad, last_grad, q, v_all, exps, row)
    near_parts = []
    if n_near:
        near_parts = pl.pallas_call(
            functools.partial(near_kernel, scaling),
            out_shape=types[:n_near],
            in_specs=[VMEM] * 4,
            out_specs=[VMEM] * n_near,
            compiler_params=grant(16),
            cost_estimate=cost(1e9, 5e6),
            name="near_half",
        )(exps, slopes, gt, q_rows)
    parts = [*near_parts, *far_parts]

    if dense:
        back = {k: hop(parts[k], "seq", k) for k in far_first}
        returned = [parts[0]] + [back[k] for k in range(1, n_seq)]
        shape = jax.ShapeDtypeStruct(prefix_keys.shape, F32)
        key_grad, value_grad = pl.pallas_call(
            functools.partial(place_kernel, n_seq, cap, here),
            out_shape=[shape] * 2,
            in_specs=[SMEM, SMEM] + [VMEM] * n_seq,
            out_specs=[VMEM] * 2,
            cost_estimate=cost(0, 2 ** 20),
            compiler_params=grant(4),
            name="place",
        )(me_seq, reads, *returned)
    else:
        cache_grads = parts[0].reshape(read_count, flat)
        placer = ((my_owner[None, None, :] == jnp.arange(n_seq, dtype=jnp.int32)[:, None, None])
                  & (my_rank[None, None, :] == slots[None, :, None])).astype(F32)
        leaving = jnp.einsum("ocr,rf->ocf", placer, cache_grads, precision=lax.Precision.HIGHEST)
        back = lax.all_to_all(leaving.astype(BF16), "seq", split_axis=0, concat_axis=0, tiled=True).astype(F32)
        summed = jnp.einsum("dcb,dcf->bf", picker, back, precision=lax.Precision.HIGHEST).reshape(here * PBLK, 2 * HD)
        key_grad, value_grad = summed[:, :HD], summed[:, HD:]
    return layer_output, key_grad, value_grad


def solution(mesh):
    in_specs = (P("seq", "tp"), P("seq", "tp"), P(None, "tp"), P(None, "tp"), P("tp", None),
                P("seq", "tp"), P("seq", "tp"), P(), P("seq", "tp"))
    out_specs = (P("seq", "tp"), P("seq", "tp"), P("seq", "tp"))
    return jax.shard_map(local, mesh=mesh, in_specs=in_specs, out_specs=out_specs, check_vma=False)
```

```python
import functools

import jax
import jax.numpy as jnp
from jax import lax
from jax.experimental import pallas as pl
from jax.experimental.pallas import tpu as pltpu
from jax.sharding import PartitionSpec as P


HD = 128
PBLK = 64
LOG2E = 1.4426950408889634
F32 = jnp.float32
BF16 = jnp.bfloat16
VMEM = pl.BlockSpec(memory_space=pltpu.VMEM)
SMEM = pl.BlockSpec(memory_space=pltpu.SMEM)
HBM = pl.BlockSpec(memory_space=pltpu.HBM)


def dot(a, b, dims):
    return lax.dot_general(a, b, (dims, ((), ())), preferred_element_type=F32)


def hbm(x):
    return pltpu.with_memory_space_constraint(x, pltpu.HBM)


def cost(flops, nbytes, trans=0):
    return pl.CostEstimate(flops=int(flops), bytes_accessed=int(nbytes), transcendentals=int(trans))


def pick_kernel(n, cap, here, me_ref, reads_hbm, keys_hbm, values_hbm, *refs):
    outs, (reads_ref, keys_ref, values_ref, sems) = refs[:n], refs[n:]
    me = me_ref[0]
    copies = [
        pltpu.make_async_copy(src, dst, sems.at[i])
        for i, (src, dst) in enumerate(
            ((reads_hbm, reads_ref), (keys_hbm, keys_ref), (values_hbm, values_ref)))
    ]
    for copy in copies:
        copy.start()
    for copy in copies:
        copy.wait()
    for k in range(n):
        for r in range(cap):
            block = reads_ref[me ^ k, cap * me + r] - here * me
            rows = pl.ds(pl.multiple_of(block * PBLK, PBLK), PBLK)
            outs[k][r * PBLK:(r + 1) * PBLK, :HD] = keys_ref[rows, :]
            outs[k][r * PBLK:(r + 1) * PBLK, HD:] = values_ref[rows, :]


def place_kernel(n, cap, here, me_ref, reads_ref, *refs):
    parts, (keys_out, values_out, keys_buf, values_buf, sems) = refs[:n], refs[n:]
    me = me_ref[0]
    level = here // cap
    copies = []
    for r in range(cap):
        picked = [reads_ref[me ^ k, cap * me + r] - here * me for k in range(n)]
        for c in range(level):
            rows = slice((r * level + c) * PBLK, (r * level + c + 1) * PBLK)
            total = jnp.zeros((PBLK, 2 * HD), F32)
            for k in range(n):
                piece = parts[k][r * PBLK:(r + 1) * PBLK, :].astype(F32)
                total += jnp.where(picked[k] == r * level + c, piece, 0.0)
            keys_buf[rows, :] = total[:, :HD]
            values_buf[rows, :] = total[:, HD:]
        done = pl.ds(r * level * PBLK, level * PBLK)
        copies.append(pltpu.make_async_copy(keys_buf.at[done], keys_out.at[done], sems.at[r, 0]))
        copies.append(pltpu.make_async_copy(values_buf.at[done], values_out.at[done], sems.at[r, 1]))
        for copy in copies[-2:]:
            copy.start()
    for copy in copies:
        copy.wait()


def weight_copies(i, me, width, hbms, bufs, slot, sems):
    rows = pl.ds(pl.multiple_of((me ^ i) * width, width), width)
    return [pltpu.make_async_copy(w.at[rows], buf.at[slot], sems.at[j, slot]) for j, (w, buf) in enumerate(zip(hbms, bufs))]


def kv_kernel(order, last, me_ref, own_hbm, *refs):
    hidden, (wk_hbm, wv_hbm, q_hbm, k_ref, v_ref, q_ref, lastk_ref, lastv_ref) = refs[:-13], refs[-13:-5]
    own_ref, wk_ref, wv_ref, sems, far_sems = refs[-5:]
    me = me_ref[0]
    width = own_ref.shape[1]

    def fetch(slot, i):
        return weight_copies(i, me, width, (wk_hbm, wv_hbm), (wk_ref, wv_ref), slot, sems)

    for slot, i in enumerate(order):
        for copy in fetch(slot, i):
            copy.start()
    own = pltpu.make_async_copy(own_hbm, own_ref, far_sems.at[0])
    own.start()
    rows = pl.ds(pl.multiple_of((me ^ last) * width, width), width)
    later = [
        pltpu.make_async_copy(q_hbm, q_ref, far_sems.at[1]),
        pltpu.make_async_copy(wk_hbm.at[rows], lastk_ref, far_sems.at[2]),
        pltpu.make_async_copy(wv_hbm.at[rows], lastv_ref, far_sems.at[3]),
    ]
    for copy in later:
        copy.start()
    new_k = jnp.zeros(k_ref.shape, F32)
    new_v = jnp.zeros(k_ref.shape, F32)
    for slot, i in enumerate(order):
        for copy in fetch(slot, i):
            copy.wait()
        if i == 0:
            own.wait()
        piece = hidden[i - 1][...] if i else own_ref[...]
        new_k += dot(piece, wk_ref[slot], ((1,), (0,)))
        new_v += dot(piece, wv_ref[slot], ((1,), (0,)))
    k_ref[...] = new_k
    v_ref[...] = new_v
    for copy in later:
        copy.wait()


def forward_kernel(n_pre, scaling, wk_ref, wv_ref, hidden_ref, q_ref, partk_ref, partv_ref, *refs):
    prefix = refs[:n_pre]
    ctx_ref, exps_ref, row_ref, v_all, k_all, vt_all, s_buf, sums = refs[n_pre:]
    length = hidden_ref.shape[0]
    heads = q_ref.shape[1] // HD
    factor = scaling * LOG2E
    at = 0
    for ref in prefix:
        size = ref.shape[0]
        k_all[at:at + size, :] = ref[:, :HD]
        v_all[at:at + size, :] = ref[:, HD:]
        at += size
    piece = hidden_ref[...]
    k_all[at:, :] = (partk_ref[...] + dot(piece, wk_ref[...], ((1,), (0,)))).astype(BF16)
    v_all[at:, :] = (partv_ref[...] + dot(piece, wv_ref[...], ((1,), (0,)))).astype(BF16)
    vt_all[...] = v_all[...].astype(F32).T.astype(BF16)
    visible = lax.broadcasted_iota(jnp.int32, (length, length), 0) <= lax.broadcasted_iota(
        jnp.int32, (length, length), 1)

    def scores(h):
        qh = q_ref[:, h * HD:(h + 1) * HD]
        s = dot(k_all[:at, :], qh, ((1,), (1,)))
        s_buf[h % 2, :at, :] = s
        peak = jnp.max(s, axis=0, keepdims=True)
        s = jnp.where(visible, dot(k_all[at:, :], qh, ((1,), (1,))), -jnp.inf)
        s_buf[h % 2, at:, :] = s
        return jnp.maximum(peak, jnp.max(s, axis=0, keepdims=True))

    def finish(h, peak):
        lanes = slice(h * length, (h + 1) * length)
        total = jnp.zeros((1, length), F32)
        step = length // 2
        for start in range(0, at + length, step):
            e = jnp.exp2((s_buf[h % 2, start:start + step, :] - peak) * factor)
            total += jnp.sum(e, axis=0, keepdims=True)
            exps_ref[start:start + step, lanes] = e.astype(BF16)
        inverse = 1.0 / total
        sums[h:h + 1, :] = inverse
        ctx_t = dot(vt_all[...], exps_ref[:, lanes], ((1,), (0,))) * inverse
        ctx_ref[:, h * HD:(h + 1) * HD] = ctx_t.T.astype(BF16)

    peak = scores(0)
    for h in range(heads):
        later = scores(h + 1) if h + 1 < heads else None
        finish(h, peak)
        peak = later
    row_ref[:heads, :] = sums[:heads, :]


def project_kernel(order, me_ref, ctx_ref, w_ref, *outs):
    me = me_ref[0]
    width = outs[0].shape[1]
    ctx = ctx_ref[...]
    for i, out in zip(order, outs):
        cols = pl.ds(pl.multiple_of((me ^ i) * width, 128), width)
        out[...] = dot(ctx, w_ref[:, cols], ((1,), (0,))).astype(BF16)


def grad_kernel(order, me_ref, w_ref, *refs):
    grads, out = refs[:-1], refs[-1]
    me = me_ref[0]
    width = grads[0].shape[1]
    total = jnp.zeros(out.shape, F32)
    for i, grad in zip(order, grads):
        cols = pl.ds(pl.multiple_of((me ^ i) * width, 128), width)
        total += dot(w_ref[:, cols], grad[...], ((1,), (1,)))
    out[...] = total


def backward_kernel(last, n_pre, scaling, me_ref, w_ref, part_ref, grad_ref, q_ref, v_all, exps_ref, row_ref, *refs):
    outs = refs[:n_pre]
    gt_all, q_all, dbuf, slopes = refs[n_pre:]
    me = me_ref[0]
    length, width = grad_ref.shape
    heads = q_ref.shape[1] // HD
    cols = pl.ds(pl.multiple_of((me ^ last) * width, 128), width)
    total = part_ref[...] + dot(w_ref[:, cols], grad_ref[...], ((1,), (1,)))
    for h in range(heads):
        lanes = slice(h * length, (h + 1) * length)
        q_all[lanes, :] = q_ref[:, h * HD:(h + 1) * HD]
        gt_all[:, lanes] = (total[h * HD:(h + 1) * HD, :] * row_ref[h:h + 1, :]).astype(BF16)
    n_rows = dbuf.shape[0]

    def slope(h):
        lanes = slice(h * length, (h + 1) * length)
        s = dot(v_all[...], gt_all[:, lanes], ((1,), (0,)))
        slopes[h % 2] = s[:n_rows]
        delta = jnp.sum(exps_ref[:, lanes].astype(F32) * s, axis=0, keepdims=True)
        return delta * row_ref[h:h + 1, :]

    def finish(h, delta):
        lanes = slice(h * length, (h + 1) * length)
        step = length // 2
        for start in range(0, n_rows, step):
            e = exps_ref[start:start + step, lanes].astype(F32)
            dbuf[start:start + step, lanes] = (e * (slopes[h % 2, start:start + step, :] - delta)).astype(BF16)

    delta = slope(0)
    for h in range(heads):
        later = slope(h + 1) if h + 1 < heads else None
        finish(h, delta)
        delta = later
    value_grad = dot(exps_ref[:n_rows, :], gt_all[...], ((1,), (1,)))
    key_grad = dot(dbuf[...], q_all[...], ((1,), (0,))) * scaling
    at = 0
    for out in outs:
        size = out.shape[0]
        out[:, HD:] = value_grad[at:at + size].astype(out.dtype)
        out[:, :HD] = key_grad[at:at + size].astype(out.dtype)
        at += size


def local(hidden_states, queries, key_weight, value_weight, output_weight, prefix_keys, prefix_values, reads, out_grad):
    length, width = hidden_states.shape
    scaling = HD ** (-0.5)
    heads = queries.shape[1] // HD
    n_tp = lax.axis_size("tp")
    n_seq = lax.axis_size("seq")
    here = prefix_keys.shape[0] // PBLK
    read_count = reads.shape[1]
    cap = max(1, read_count // n_seq)
    dense = cap * n_seq == read_count and here % cap == 0 and n_seq & (n_seq - 1) == 0 and here * n_seq % read_count == 0
    me_tp = lax.axis_index("tp").astype(jnp.int32).reshape(1)
    me_seq = lax.axis_index("seq").astype(jnp.int32).reshape(1)
    n_rows = read_count * PBLK
    keys = n_rows + length

    def hop(x, axis, k):
        n = n_tp if axis == "tp" else n_seq
        return lax.ppermute(x, axis, [(i, i ^ k) for i in range(n)])

    def grant(mib):
        return pltpu.CompilerParams(vmem_limit_bytes=mib * 2 ** 20)

    near_grad = hop(out_grad, "tp", 1)
    far_grad = hop(out_grad, "tp", 2)
    near_hidden = hop(hidden_states, "tp", 1)
    far_hidden = hop(hidden_states, "tp", 2)
    last_hidden = hop(far_hidden, "tp", 1)
    last_grad = hop(far_grad, "tp", 1)
    far_first = sorted(range(1, n_seq), key=lambda k: (-(k // 4), k & 1, -k))

    if dense:
        shape = jax.ShapeDtypeStruct((cap * PBLK, 2 * HD), BF16)
        picked = pl.pallas_call(
            functools.partial(pick_kernel, n_seq, cap, here),
            out_shape=[shape] * n_seq,
            in_specs=[SMEM, HBM, HBM, HBM],
            out_specs=[VMEM] * n_seq,
            scratch_shapes=[
                pltpu.SMEM(reads.shape, jnp.int32),
                pltpu.VMEM(prefix_keys.shape, BF16),
                pltpu.VMEM(prefix_keys.shape, BF16),
                pltpu.SemaphoreType.DMA((3,)),
            ],
            cost_estimate=cost(0, 2 ** 20),
            compiler_params=grant(4),
            name="pick",
        )(me_seq, hbm(reads), hbm(prefix_keys), hbm(prefix_values))
        moved = {k: hop(picked[k], "seq", k) for k in far_first}
        prefix = [picked[0]] + [moved[k] for k in range(1, n_seq)]
    else:
        flat = PBLK * 2 * HD
        local_cache = jnp.concatenate([prefix_keys, prefix_values], axis=1).reshape(here, flat)
        own = me_seq[0]
        owners = reads // here
        slot_here = reads % here
        earlier = jnp.arange(read_count)[None, :] < jnp.arange(read_count)[:, None]
        ranks = jnp.sum((owners[:, :, None] == owners[:, None, :]) & earlier[None], axis=2)
        slots = jnp.arange(cap, dtype=jnp.int32)
        picker = jnp.sum(
            ((owners == own)[:, :, None, None]
             & (ranks[:, :, None, None] == slots[None, None, :, None])
             & (slot_here[:, :, None, None] == jnp.arange(here, dtype=jnp.int32))).astype(F32), axis=1)
        outgoing = jnp.einsum("dcb,bf->dcf", picker.astype(BF16), local_cache, preferred_element_type=F32).astype(BF16)
        incoming = lax.all_to_all(outgoing, "seq", split_axis=0, concat_axis=0, tiled=True)
        my_owner, my_rank = owners[own], ranks[own]
        fetched = jnp.take(incoming.reshape(n_seq * cap, flat), my_owner * cap + my_rank, axis=0)
        prefix = [fetched.reshape(n_rows, 2 * HD)]
    n_pre = len(prefix)

    part = jax.ShapeDtypeStruct((length, HD), F32)
    weight = jax.ShapeDtypeStruct((width, HD), BF16)
    part_k, part_v, q, last_k, last_v = pl.pallas_call(
        functools.partial(kv_kernel, (1, 0, 2), n_tp - 1),
        out_shape=[part, part, jax.ShapeDtypeStruct(queries.shape, BF16), weight, weight],
        in_specs=[SMEM, HBM] + [VMEM] * (n_tp - 2) + [HBM] * 3,
        out_specs=[VMEM] * 5,
        scratch_shapes=[
            pltpu.VMEM((length, width), BF16),
            pltpu.VMEM((n_tp - 1, width, HD), BF16),
            pltpu.VMEM((n_tp - 1, width, HD), BF16),
            pltpu.SemaphoreType.DMA((2, n_tp - 1)),
            pltpu.SemaphoreType.DMA((4,)),
        ],
        compiler_params=grant(8),
        cost_estimate=cost(4e8, 3e6),
        name="kv",
    )(me_tp, hbm(hidden_states), near_hidden, far_hidden, hbm(key_weight), hbm(value_weight), hbm(queries))

    ctx, exps, row, v_all = pl.pallas_call(
        functools.partial(forward_kernel, n_pre, scaling),
        out_shape=[
            jax.ShapeDtypeStruct((length, heads * HD), BF16),
            jax.ShapeDtypeStruct((keys, heads * length), BF16),
            jax.ShapeDtypeStruct((heads + (-heads) % 8, length), F32),
            jax.ShapeDtypeStruct((keys, HD), BF16),
        ],
        in_specs=[VMEM] * (6 + n_pre),
        out_specs=[VMEM] * 4,
        scratch_shapes=[
            pltpu.VMEM((keys, HD), BF16),
            pltpu.VMEM((HD, keys), BF16),
            pltpu.VMEM((2, keys, length), F32),
            pltpu.VMEM((heads + (-heads) % 8, length), F32),
        ],
        compiler_params=grant(20),
        cost_estimate=cost(5e9, 1e7, 3e6),
        name="forward",
    )(last_k, last_v, last_hidden, q, part_k, part_v, *prefix)

    part_grad = pl.pallas_call(
        functools.partial(grad_kernel, (0, 1, 2)),
        out_shape=jax.ShapeDtypeStruct((heads * HD, length), F32),
        in_specs=[SMEM] + [VMEM] * 4,
        out_specs=VMEM,
        compiler_params=grant(16),
        cost_estimate=cost(1.5e9, 8e6),
        name="grad",
    )(me_tp, output_weight, out_grad, near_grad, far_grad)

    def project(order):
        return pl.pallas_call(
            functools.partial(project_kernel, order),
            out_shape=[jax.ShapeDtypeStruct((length, width), BF16)] * len(order),
            in_specs=[SMEM, VMEM, VMEM],
            out_specs=[VMEM] * len(order),
            compiler_params=grant(16),
            cost_estimate=cost(5e8 * len(order), 2e6 * len(order)),
        )(me_tp, ctx, output_weight)

    share3, share2 = project((3, 2))
    near3 = hop(share3, "tp", 1)
    share1, share0 = project((1, 0))
    near1 = hop(share1, "tp", 1)
    cross = (share2.astype(F32) + near3.astype(F32)).astype(BF16)
    across = hop(cross, "tp", 2)
    layer_output = (share0.astype(F32) + near1.astype(F32) + across.astype(F32)).astype(BF16)

    grad_type = BF16 if dense else F32
    parts = pl.pallas_call(
        functools.partial(backward_kernel, n_tp - 1, n_pre, scaling),
        out_shape=[jax.ShapeDtypeStruct(x.shape, grad_type) for x in prefix],
        in_specs=[SMEM] + [VMEM] * 7,
        out_specs=[VMEM] * n_pre,
        scratch_shapes=[
            pltpu.VMEM((HD, heads * length), BF16),
            pltpu.VMEM((heads * length, HD), BF16),
            pltpu.VMEM((n_rows, heads * length), BF16),
            pltpu.VMEM((2, n_rows, length), F32),
        ],
        compiler_params=grant(32),
        cost_estimate=cost(7e9, 1e7),
        name="backward",
    )(me_tp, output_weight, part_grad, last_grad, q, v_all, exps, row)

    if dense:
        back = {k: hop(parts[k], "seq", k) for k in far_first}
        returned = [parts[0]] + [back[k] for k in range(1, n_seq)]
        shape = jax.ShapeDtypeStruct(prefix_keys.shape, F32)
        key_grad, value_grad = pl.pallas_call(
            functools.partial(place_kernel, n_seq, cap, here),
            out_shape=[shape] * 2,
            in_specs=[SMEM, SMEM] + [VMEM] * n_seq,
            out_specs=[HBM] * 2,
            scratch_shapes=[
                pltpu.VMEM(prefix_keys.shape, F32),
                pltpu.VMEM(prefix_keys.shape, F32),
                pltpu.SemaphoreType.DMA((cap, 2)),
            ],
            cost_estimate=cost(0, 2 ** 20),
            compiler_params=grant(4),
            name="place",
        )(me_seq, reads, *returned)
    else:
        cache_grads = parts[0].reshape(read_count, flat)
        placer = ((my_owner[None, None, :] == jnp.arange(n_seq, dtype=jnp.int32)[:, None, None])
                  & (my_rank[None, None, :] == slots[None, :, None])).astype(F32)
        leaving = jnp.einsum("ocr,rf->ocf", placer, cache_grads, precision=lax.Precision.HIGHEST)
        back = lax.all_to_all(leaving.astype(BF16), "seq", split_axis=0, concat_axis=0, tiled=True).astype(F32)
        summed = jnp.einsum("dcb,dcf->bf", picker, back, precision=lax.Precision.HIGHEST).reshape(here * PBLK, 2 * HD)
        key_grad, value_grad = summed[:, :HD], summed[:, HD:]
    return layer_output, key_grad, value_grad


def solution(mesh):
    in_specs = (P("seq", "tp"), P("seq", "tp"), P(None, "tp"), P(None, "tp"), P("tp", None),
                P("seq", "tp"), P("seq", "tp"), P(), P("seq", "tp"))
    out_specs = (P("seq", "tp"), P("seq", "tp"), P("seq", "tp"))
    return jax.shard_map(local, mesh=mesh, in_specs=in_specs, out_specs=out_specs, check_vma=False)
```

```python
import functools

import jax
import jax.numpy as jnp
from jax import lax
from jax.experimental import pallas as pl
from jax.experimental.pallas import tpu as pltpu
from jax.sharding import PartitionSpec as P


HD = 128
PBLK = 64
LOG2E = 1.4426950408889634
F32 = jnp.float32
BF16 = jnp.bfloat16
VMEM = pl.BlockSpec(memory_space=pltpu.VMEM)
SMEM = pl.BlockSpec(memory_space=pltpu.SMEM)
HBM = pl.BlockSpec(memory_space=pltpu.HBM)


def dot(a, b, dims):
    return lax.dot_general(a, b, (dims, ((), ())), preferred_element_type=F32)


def hbm(x):
    return pltpu.with_memory_space_constraint(x, pltpu.HBM)


def cost(flops, nbytes, trans=0):
    return pl.CostEstimate(flops=int(flops), bytes_accessed=int(nbytes), transcendentals=int(trans))


def pick_kernel(n, cap, here, me_ref, reads_hbm, keys_hbm, values_hbm, *refs):
    outs, (reads_ref, keys_ref, values_ref, sems) = refs[:n], refs[n:]
    me = me_ref[0]
    copies = [
        pltpu.make_async_copy(src, dst, sems.at[i])
        for i, (src, dst) in enumerate(
            ((reads_hbm, reads_ref), (keys_hbm, keys_ref), (values_hbm, values_ref)))
    ]
    for copy in copies:
        copy.start()
    for copy in copies:
        copy.wait()
    for k in range(n):
        for r in range(cap):
            block = reads_ref[me ^ k, cap * me + r] - here * me
            rows = pl.ds(pl.multiple_of(block * PBLK, PBLK), PBLK)
            outs[k][r * PBLK:(r + 1) * PBLK, :HD] = keys_ref[rows, :]
            outs[k][r * PBLK:(r + 1) * PBLK, HD:] = values_ref[rows, :]


def place_kernel(n, cap, here, me_ref, reads_ref, *refs):
    parts, keys_ref, values_ref = refs[:n], refs[n], refs[n + 1]
    me = me_ref[0]
    keys_ref[...] = jnp.zeros_like(keys_ref)
    values_ref[...] = jnp.zeros_like(values_ref)
    for k in range(n):
        for r in range(cap):
            block = reads_ref[me ^ k, cap * me + r] - here * me
            rows = pl.ds(pl.multiple_of(block * PBLK, PBLK), PBLK)
            piece = parts[k][r * PBLK:(r + 1) * PBLK, :].astype(F32)
            keys_ref[rows, :] += piece[:, :HD]
            values_ref[rows, :] += piece[:, HD:]


def weight_copies(i, me, width, hbms, bufs, slot, sems):
    rows = pl.ds(pl.multiple_of((me ^ i) * width, width), width)
    return [pltpu.make_async_copy(w.at[rows], buf.at[slot], sems.at[j, slot]) for j, (w, buf) in enumerate(zip(hbms, bufs))]


def kv_kernel(order, rest, me_ref, own_hbm, *refs):
    hidden, (wk_hbm, wv_hbm, q_hbm, k_ref, v_ref, q_ref, restk_ref, restv_ref) = refs[:-13], refs[-13:-5]
    own_ref, wk_ref, wv_ref, sems, far_sems = refs[-5:]
    me = me_ref[0]
    width = own_ref.shape[1]

    def fetch(slot, i):
        return weight_copies(i, me, width, (wk_hbm, wv_hbm), (wk_ref, wv_ref), slot, sems)

    for slot, i in enumerate(order):
        for copy in fetch(slot, i):
            copy.start()
    own = pltpu.make_async_copy(own_hbm, own_ref, far_sems.at[0])
    own.start()
    later = [pltpu.make_async_copy(q_hbm, q_ref, far_sems.at[1])]
    for slot, i in enumerate(rest):
        rows = pl.ds(pl.multiple_of((me ^ i) * width, width), width)
        later.append(pltpu.make_async_copy(wk_hbm.at[rows], restk_ref.at[slot], far_sems.at[2 + 2 * slot]))
        later.append(pltpu.make_async_copy(wv_hbm.at[rows], restv_ref.at[slot], far_sems.at[3 + 2 * slot]))
    for copy in later:
        copy.start()
    new_k = jnp.zeros(k_ref.shape, F32)
    new_v = jnp.zeros(k_ref.shape, F32)
    pieces = iter(hidden)
    for slot, i in enumerate(order):
        for copy in fetch(slot, i):
            copy.wait()
        if i == 0:
            own.wait()
        piece = next(pieces)[...] if i else own_ref[...]
        new_k += dot(piece, wk_ref[slot], ((1,), (0,)))
        new_v += dot(piece, wv_ref[slot], ((1,), (0,)))
    k_ref[...] = new_k
    v_ref[...] = new_v
    for copy in later:
        copy.wait()


def forward_kernel(n_rest, n_pre, scaling, wk_ref, wv_ref, *refs):
    hidden, (q_ref, partk_ref, partv_ref), refs = refs[:n_rest], refs[n_rest:n_rest + 3], refs[n_rest + 3:]
    prefix = refs[:n_pre]
    ctx_ref, exps_ref, row_ref, v_all, k_all, vt_all, s_buf, sums = refs[n_pre:]
    length = q_ref.shape[0]
    heads = q_ref.shape[1] // HD
    factor = scaling * LOG2E
    at = 0
    for ref in prefix:
        size = ref.shape[0]
        k_all[at:at + size, :] = ref[:, :HD]
        v_all[at:at + size, :] = ref[:, HD:]
        at += size
    new_k, new_v = partk_ref[...], partv_ref[...]
    for slot, ref in enumerate(hidden):
        new_k += dot(ref[...], wk_ref[slot], ((1,), (0,)))
        new_v += dot(ref[...], wv_ref[slot], ((1,), (0,)))
    k_all[at:, :] = new_k.astype(BF16)
    v_all[at:, :] = new_v.astype(BF16)
    vt_all[...] = v_all[...].astype(F32).T.astype(BF16)
    visible = lax.broadcasted_iota(jnp.int32, (length, length), 0) <= lax.broadcasted_iota(
        jnp.int32, (length, length), 1)

    def scores(h):
        qh = q_ref[:, h * HD:(h + 1) * HD]
        s = dot(k_all[:at, :], qh, ((1,), (1,)))
        s_buf[h % 2, :at, :] = s
        peak = jnp.max(s, axis=0, keepdims=True)
        s = jnp.where(visible, dot(k_all[at:, :], qh, ((1,), (1,))), -jnp.inf)
        s_buf[h % 2, at:, :] = s
        return jnp.maximum(peak, jnp.max(s, axis=0, keepdims=True))

    def finish(h, peak):
        lanes = slice(h * length, (h + 1) * length)
        total = jnp.zeros((1, length), F32)
        step = length // 2
        for start in range(0, at + length, step):
            e = jnp.exp2((s_buf[h % 2, start:start + step, :] - peak) * factor)
            total += jnp.sum(e, axis=0, keepdims=True)
            exps_ref[start:start + step, lanes] = e.astype(BF16)
        inverse = 1.0 / total
        sums[h:h + 1, :] = inverse
        ctx_t = dot(vt_all[...], exps_ref[:, lanes], ((1,), (0,))) * inverse
        ctx_ref[:, h * HD:(h + 1) * HD] = ctx_t.T.astype(BF16)

    peak = scores(0)
    for h in range(heads):
        later = scores(h + 1) if h + 1 < heads else None
        finish(h, peak)
        peak = later
    row_ref[:heads, :] = sums[:heads, :]


def project_kernel(order, me_ref, ctx_ref, w_ref, *outs):
    me = me_ref[0]
    width = outs[0].shape[1]
    ctx = ctx_ref[...]
    for i, out in zip(order, outs):
        cols = pl.ds(pl.multiple_of((me ^ i) * width, 128), width)
        out[...] = dot(ctx, w_ref[:, cols], ((1,), (0,))).astype(BF16)


def grad_kernel(order, me_ref, w_ref, *refs):
    grads, out = refs[:-1], refs[-1]
    me = me_ref[0]
    width = grads[0].shape[1]
    total = jnp.zeros(out.shape, F32)
    for i, grad in zip(order, grads):
        cols = pl.ds(pl.multiple_of((me ^ i) * width, 128), width)
        total += dot(w_ref[:, cols], grad[...], ((1,), (1,)))
    out[...] = total


def backward_kernel(last, n_pre, scaling, me_ref, w_ref, part_ref, grad_ref, q_ref, v_all, exps_ref, row_ref, *refs):
    outs = refs[:n_pre]
    gt_all, q_all, dbuf, slopes = refs[n_pre:]
    me = me_ref[0]
    length, width = grad_ref.shape
    heads = q_ref.shape[1] // HD
    cols = pl.ds(pl.multiple_of((me ^ last) * width, 128), width)
    total = part_ref[...] + dot(w_ref[:, cols], grad_ref[...], ((1,), (1,)))
    for h in range(heads):
        lanes = slice(h * length, (h + 1) * length)
        q_all[lanes, :] = q_ref[:, h * HD:(h + 1) * HD]
        gt_all[:, lanes] = (total[h * HD:(h + 1) * HD, :] * row_ref[h:h + 1, :]).astype(BF16)
    n_rows = dbuf.shape[0]

    def slope(h):
        lanes = slice(h * length, (h + 1) * length)
        s = dot(v_all[...], gt_all[:, lanes], ((1,), (0,)))
        slopes[h % 2] = s[:n_rows]
        delta = jnp.sum(exps_ref[:, lanes].astype(F32) * s, axis=0, keepdims=True)
        return delta * row_ref[h:h + 1, :]

    def finish(h, delta):
        lanes = slice(h * length, (h + 1) * length)
        step = length // 2
        for start in range(0, n_rows, step):
            e = exps_ref[start:start + step, lanes].astype(F32)
            dbuf[start:start + step, lanes] = (e * (slopes[h % 2, start:start + step, :] - delta)).astype(BF16)

    delta = slope(0)
    for h in range(heads):
        later = slope(h + 1) if h + 1 < heads else None
        finish(h, delta)
        delta = later
    value_grad = dot(exps_ref[:n_rows, :], gt_all[...], ((1,), (1,)))
    key_grad = dot(dbuf[...], q_all[...], ((1,), (0,))) * scaling
    at = 0
    for out in outs:
        size = out.shape[0]
        out[:, HD:] = value_grad[at:at + size].astype(out.dtype)
        out[:, :HD] = key_grad[at:at + size].astype(out.dtype)
        at += size


def local(hidden_states, queries, key_weight, value_weight, output_weight, prefix_keys, prefix_values, reads, out_grad):
    length, width = hidden_states.shape
    scaling = HD ** (-0.5)
    heads = queries.shape[1] // HD
    n_tp = lax.axis_size("tp")
    n_seq = lax.axis_size("seq")
    here = prefix_keys.shape[0] // PBLK
    read_count = reads.shape[1]
    cap = max(1, read_count // n_seq)
    dense = cap * n_seq == read_count and n_seq & (n_seq - 1) == 0 and here * n_seq % read_count == 0
    me_tp = lax.axis_index("tp").astype(jnp.int32).reshape(1)
    me_seq = lax.axis_index("seq").astype(jnp.int32).reshape(1)
    n_rows = read_count * PBLK
    keys = n_rows + length

    def hop(x, axis, k):
        n = n_tp if axis == "tp" else n_seq
        return lax.ppermute(x, axis, [(i, i ^ k) for i in range(n)])

    def grant(mib):
        return pltpu.CompilerParams(vmem_limit_bytes=mib * 2 ** 20)

    near_grad = hop(out_grad, "tp", 1)
    far_grad = hop(out_grad, "tp", 2)
    near_hidden = hop(hidden_states, "tp", 1)
    far_hidden = hop(hidden_states, "tp", 2)
    last_hidden = hop(far_hidden, "tp", 1)
    last_grad = hop(far_grad, "tp", 1)
    far_first = sorted(range(1, n_seq), key=lambda k: (-(k // 4), k & 1, -k))

    if dense:
        shape = jax.ShapeDtypeStruct((cap * PBLK, 2 * HD), BF16)
        picked = pl.pallas_call(
            functools.partial(pick_kernel, n_seq, cap, here),
            out_shape=[shape] * n_seq,
            in_specs=[SMEM, HBM, HBM, HBM],
            out_specs=[VMEM] * n_seq,
            scratch_shapes=[
                pltpu.SMEM(reads.shape, jnp.int32),
                pltpu.VMEM(prefix_keys.shape, BF16),
                pltpu.VMEM(prefix_keys.shape, BF16),
                pltpu.SemaphoreType.DMA((3,)),
            ],
            cost_estimate=cost(0, 2 ** 20),
            compiler_params=grant(4),
            name="pick",
        )(me_seq, hbm(reads), hbm(prefix_keys), hbm(prefix_values))
        moved = {k: hop(picked[k], "seq", k) for k in far_first}
        prefix = [picked[0]] + [moved[k] for k in range(1, n_seq)]
    else:
        flat = PBLK * 2 * HD
        local_cache = jnp.concatenate([prefix_keys, prefix_values], axis=1).reshape(here, flat)
        own = me_seq[0]
        owners = reads // here
        slot_here = reads % here
        earlier = jnp.arange(read_count)[None, :] < jnp.arange(read_count)[:, None]
        ranks = jnp.sum((owners[:, :, None] == owners[:, None, :]) & earlier[None], axis=2)
        slots = jnp.arange(cap, dtype=jnp.int32)
        picker = jnp.sum(
            ((owners == own)[:, :, None, None]
             & (ranks[:, :, None, None] == slots[None, None, :, None])
             & (slot_here[:, :, None, None] == jnp.arange(here, dtype=jnp.int32))).astype(F32), axis=1)
        outgoing = jnp.einsum("dcb,bf->dcf", picker.astype(BF16), local_cache, preferred_element_type=F32).astype(BF16)
        incoming = lax.all_to_all(outgoing, "seq", split_axis=0, concat_axis=0, tiled=True)
        my_owner, my_rank = owners[own], ranks[own]
        fetched = jnp.take(incoming.reshape(n_seq * cap, flat), my_owner * cap + my_rank, axis=0)
        prefix = [fetched.reshape(n_rows, 2 * HD)]
    n_pre = len(prefix)

    part = jax.ShapeDtypeStruct((length, HD), F32)
    n_rest = n_tp - 2
    weight = jax.ShapeDtypeStruct((n_rest, width, HD), BF16)
    part_k, part_v, q, rest_k, rest_v = pl.pallas_call(
        functools.partial(kv_kernel, (2, 0), (1, 3)),
        out_shape=[part, part, jax.ShapeDtypeStruct(queries.shape, BF16), weight, weight],
        in_specs=[SMEM, HBM, VMEM] + [HBM] * 3,
        out_specs=[VMEM] * 5,
        scratch_shapes=[
            pltpu.VMEM((length, width), BF16),
            pltpu.VMEM((2, width, HD), BF16),
            pltpu.VMEM((2, width, HD), BF16),
            pltpu.SemaphoreType.DMA((2, 2)),
            pltpu.SemaphoreType.DMA((2 + 2 * n_rest,)),
        ],
        compiler_params=grant(8),
        cost_estimate=cost(4e8, 3e6),
        name="kv",
    )(me_tp, hbm(hidden_states), far_hidden, hbm(key_weight), hbm(value_weight), hbm(queries))

    ctx, exps, row, v_all = pl.pallas_call(
        functools.partial(forward_kernel, n_rest, n_pre, scaling),
        out_shape=[
            jax.ShapeDtypeStruct((length, heads * HD), BF16),
            jax.ShapeDtypeStruct((keys, heads * length), BF16),
            jax.ShapeDtypeStruct((heads + (-heads) % 8, length), F32),
            jax.ShapeDtypeStruct((keys, HD), BF16),
        ],
        in_specs=[VMEM] * (5 + n_rest + n_pre),
        out_specs=[VMEM] * 4,
        scratch_shapes=[
            pltpu.VMEM((keys, HD), BF16),
            pltpu.VMEM((HD, keys), BF16),
            pltpu.VMEM((2, keys, length), F32),
            pltpu.VMEM((heads + (-heads) % 8, length), F32),
        ],
        compiler_params=grant(20),
        cost_estimate=cost(5e9, 1e7, 3e6),
        name="forward",
    )(rest_k, rest_v, near_hidden, last_hidden, q, part_k, part_v, *prefix)

    part_grad = pl.pallas_call(
        functools.partial(grad_kernel, (0, 1, 2)),
        out_shape=jax.ShapeDtypeStruct((heads * HD, length), F32),
        in_specs=[SMEM] + [VMEM] * 4,
        out_specs=VMEM,
        compiler_params=grant(16),
        cost_estimate=cost(1.5e9, 8e6),
        name="grad",
    )(me_tp, output_weight, out_grad, near_grad, far_grad)

    def project(order):
        return pl.pallas_call(
            functools.partial(project_kernel, order),
            out_shape=[jax.ShapeDtypeStruct((length, width), BF16)] * len(order),
            in_specs=[SMEM, VMEM, VMEM],
            out_specs=[VMEM] * len(order),
            compiler_params=grant(16),
            cost_estimate=cost(5e8 * len(order), 2e6 * len(order)),
        )(me_tp, ctx, output_weight)

    share3, share2 = project((3, 2))
    near3 = hop(share3, "tp", 1)
    share1, share0 = project((1, 0))
    near1 = hop(share1, "tp", 1)
    cross = (share2.astype(F32) + near3.astype(F32)).astype(BF16)
    across = hop(cross, "tp", 2)
    layer_output = (share0.astype(F32) + near1.astype(F32) + across.astype(F32)).astype(BF16)

    grad_type = BF16 if dense else F32
    parts = pl.pallas_call(
        functools.partial(backward_kernel, n_tp - 1, n_pre, scaling),
        out_shape=[jax.ShapeDtypeStruct(x.shape, grad_type) for x in prefix],
        in_specs=[SMEM] + [VMEM] * 7,
        out_specs=[VMEM] * n_pre,
        scratch_shapes=[
            pltpu.VMEM((HD, heads * length), BF16),
            pltpu.VMEM((heads * length, HD), BF16),
            pltpu.VMEM((n_rows, heads * length), BF16),
            pltpu.VMEM((2, n_rows, length), F32),
        ],
        compiler_params=grant(32),
        cost_estimate=cost(7e9, 1e7),
        name="backward",
    )(me_tp, output_weight, part_grad, last_grad, q, v_all, exps, row)

    if dense:
        back = {k: hop(parts[k], "seq", k) for k in far_first}
        returned = [parts[0]] + [back[k] for k in range(1, n_seq)]
        shape = jax.ShapeDtypeStruct(prefix_keys.shape, F32)
        key_grad, value_grad = pl.pallas_call(
            functools.partial(place_kernel, n_seq, cap, here),
            out_shape=[shape] * 2,
            in_specs=[SMEM, SMEM] + [VMEM] * n_seq,
            out_specs=[VMEM] * 2,
            cost_estimate=cost(0, 2 ** 20),
            compiler_params=grant(4),
            name="place",
        )(me_seq, reads, *returned)
    else:
        cache_grads = parts[0].reshape(read_count, flat)
        placer = ((my_owner[None, None, :] == jnp.arange(n_seq, dtype=jnp.int32)[:, None, None])
                  & (my_rank[None, None, :] == slots[None, :, None])).astype(F32)
        leaving = jnp.einsum("ocr,rf->ocf", placer, cache_grads, precision=lax.Precision.HIGHEST)
        back = lax.all_to_all(leaving.astype(BF16), "seq", split_axis=0, concat_axis=0, tiled=True).astype(F32)
        summed = jnp.einsum("dcb,dcf->bf", picker, back, precision=lax.Precision.HIGHEST).reshape(here * PBLK, 2 * HD)
        key_grad, value_grad = summed[:, :HD], summed[:, HD:]
    return layer_output, key_grad, value_grad


def solution(mesh):
    in_specs = (P("seq", "tp"), P("seq", "tp"), P(None, "tp"), P(None, "tp"), P("tp", None),
                P("seq", "tp"), P("seq", "tp"), P(), P("seq", "tp"))
    out_specs = (P("seq", "tp"), P("seq", "tp"), P("seq", "tp"))
    return jax.shard_map(local, mesh=mesh, in_specs=in_specs, out_specs=out_specs, check_vma=False)
```
